32 devices in a mesh: groups: 2 (over y), space: 4 (over z), tm: 2 (over x), col: 2 (over core).
Axes of the slice: x: 2, y: 2, z: 4, core: 2. Of those that a mesh axis runs over, the one named last changes fastest.
Arguments:
- activations: bfloat16 [4, 16, 512, 256], P(('groups', 'tm'), ('space', 'col')), parts along dimension 0, may hold values from -6 to 6
- conv_weight: bfloat16 [3, 3, 256, 256], replicated, may hold values from -0.125 to 0.125
- conv_bias: float32 [256], replicated, may hold values from -3 to 3
- head_weight: bfloat16 [256, 32], replicated, may hold values from -0.375 to 0.375
- latent_grad: bfloat16 [4, 8, 256, 16], P(('groups', 'tm'), None, ('space', 'col')), parts along dimension 0, may hold values from -6 to 6
- noise_sample: bfloat16 [4, 8, 256, 16], P(('groups', 'tm'), ('space', 'col')), parts along dimension 0, may hold values from -5 to 5
Outputs:
- x_grad: bfloat16 [4, 16, 512, 256], P(('groups', 'tm'), ('space', 'col')), parts along dimension 0
- conv_weight_grad: float32 [3, 3, 512, 256], P(None, None, ('groups', 'space', 'col')), parts along dimension 2
- head_weight_grad: float32 [512, 32], P(('groups', 'space', 'col')), parts along dimension 0
- conv_bias_grad: float32 [512], P(('groups', 'space', 'col')), parts along dimension 0
The draws below stay inside these ranges and needn't reach their ends.
There are 2 independent parts, one for each index of `groups`. The reference program is written for one: setup_inputs(seed, part) draws one part's arguments, and reference() takes and returns one part's arrays. A program takes and returns all parts, laid end to end along the dimension named above; an argument that names none is the same for every part. Nothing has to cross between parts.
All inputs are finite; a program needn't handle non-finite values.
Results may differ from the reference program's by a relative error of at most 0.007.
Values may be sent and summed in bfloat16 or wider, within the bound.
No kernel may reach another device: no remote copies, remote signals or barrier semaphores. Data moves between devices by JAX's collectives and lax.ppermute only.
A program may use at most 64 MiB of HBM per device.

```python
import math
import jax
import jax.numpy as jnp
from jax import lax

CH = 256
LAT = 16
LAT_W = 256
FRAMES = 2
LAT_H = 8


def levels(rng, extent, pieces, smallest, high):
    factor_of = 1.0
    for axis_at, blocks in pieces:
        draws = jax.random.uniform(jax.random.fold_in(jax.random.fold_in(rng, 6), axis_at), (blocks,), jnp.float32, smallest / len(pieces), high / len(pieces))
        factor_of = factor_of * jnp.repeat(jnp.exp(draws), extent[axis_at] // blocks).reshape((-1,) + (1,) * (len(extent) - 1 - axis_at))
    return factor_of


def gaussian(key, dims, scale, limit, split=(), dtype=jnp.bfloat16):
    result = jax.random.normal(key, dims, jnp.float32) * scale
    if len(split) > 0:
        result = levels(key, dims, split, -0.22, 0.18) * result
    return jnp.clip(result, min=-limit, max=limit).astype(dtype)


def setup_inputs(seed: int = 0, part: int = 0) -> dict:
    keys = jax.random.split(jax.random.key(seed), 7)
    part_splits = jax.random.split(jax.random.fold_in(keys[6], part), 7)
    activations = gaussian(part_splits[0], (FRAMES, 2 * LAT_H, 2 * LAT_W, CH), 1.0, 6.0, ((0, 2), (1, 8)))
    conv_weight = gaussian(keys[1], (3, 3, CH, CH), (9 * CH) ** -0.5, 0.125)
    conv_bias = gaussian(keys[2], (CH,), 0.5, 3.0, (), jnp.float32)
    head_weight = gaussian(keys[3], (CH, 2 * LAT), CH ** -0.5, 0.375)
    latent_grad = gaussian(part_splits[4], (FRAMES, LAT_H, LAT_W, LAT), 1.0, 6.0, ((0, 2), (2, 8)))
    noise_sample = gaussian(part_splits[5], (FRAMES, LAT_H, LAT_W, LAT), 1.0, 5.0, ((0, 2), (1, 8)))
    return {"activations": activations, "conv_weight": conv_weight, "conv_bias": conv_bias, "head_weight": head_weight, "latent_grad": latent_grad, "noise_sample": noise_sample}


kl_weight = 1.0

def frame_backward(frame_items, conv_weight, conv_bias, head_weight):
    x_frame, latent_frame, noise_frame = frame_items
    row_count = x_frame.shape[0] // 2
    col_count = x_frame.shape[1] // 2
    channels = x_frame.shape[2]
    latent_dim = latent_frame.shape[-1]
    padded = jnp.pad(x_frame, ((0, 1), (0, 1), (0, 0))).astype(jnp.float32)
    weights = conv_weight.astype(jnp.float32)
    pre_act = jnp.zeros((row_count, col_count, channels), jnp.float32) + conv_bias
    for row_tap in range(3):
        for col_tap in range(3):
            window = padded[row_tap:row_tap + 2 * row_count:2, col_tap:col_tap + 2 * col_count:2]
            pre_act = pre_act + jnp.einsum('rck,ko->rco', window, weights[row_tap, col_tap], precision=lax.Precision.HIGHEST)
    hidden = jax.nn.silu(pre_act).astype(jnp.bfloat16)
    flattened = hidden.reshape(row_count * col_count, channels)
    moments = jnp.dot(flattened, head_weight, preferred_element_type=jnp.float32)
    mean_part = moments[:, :latent_dim]
    logvar = moments[:, latent_dim:]
    upstream = latent_frame.reshape(-1, latent_dim).astype(jnp.float32)
    sample = noise_frame.reshape(-1, latent_dim).astype(jnp.float32)
    spread = jnp.exp(0.5 * logvar)
    mean_grad = upstream + kl_weight * mean_part
    logvar_grad = 0.5 * upstream * sample * spread + 0.5 * kl_weight * (spread * spread - 1.0)
    moment_grad = jnp.concatenate([mean_grad, logvar_grad], 1).astype(jnp.bfloat16)
    head_term = jnp.dot(flattened.T, moment_grad, preferred_element_type=jnp.float32)
    hidden_grad = jnp.dot(moment_grad, head_weight.T, preferred_element_type=jnp.float32)
    hidden_grad = hidden_grad.reshape(row_count, col_count, channels)
    gating = jax.nn.sigmoid(pre_act)
    pre_grad = (hidden_grad * gating * (1.0 + pre_act * (1.0 - gating))).astype(jnp.bfloat16)
    pre_wide = pre_grad.astype(jnp.float32)
    bias_term = lax.optimization_barrier(jnp.sum(pre_wide, axis=(0, 1)))
    input_grad = jnp.zeros((2 * row_count + 1, 2 * col_count + 1, channels), jnp.float32)
    kernel_terms = []
    for row_tap in range(3):
        for col_tap in range(3):
            window = padded[row_tap:row_tap + 2 * row_count:2, col_tap:col_tap + 2 * col_count:2]
            kernel_terms.append(jnp.einsum('rck,rco->ko', window, pre_wide, precision=lax.Precision.HIGHEST))
            contrib = jnp.einsum('rco,ko->rck', pre_wide, weights[row_tap, col_tap], precision=lax.Precision.HIGHEST)
            input_grad = input_grad.at[row_tap:row_tap + 2 * row_count:2, col_tap:col_tap + 2 * col_count:2].add(contrib)
    kernel_term = jnp.stack(kernel_terms).reshape(3, 3, channels, channels)
    return (input_grad[:2 * row_count, :2 * col_count].astype(jnp.bfloat16), kernel_term, head_term, bias_term)

def reference(activations, conv_weight, conv_bias, head_weight, latent_grad, noise_sample):

    def per_frame(frame_items):
        return frame_backward(frame_items, conv_weight, conv_bias, head_weight)
    x_grad, kernel_terms, head_terms, bias_terms = lax.map(per_frame, (activations, latent_grad, noise_sample))
    grad_scale = 1.0 / math.sqrt(FRAMES * LAT_H * LAT_W)
    return (x_grad, lax.optimization_barrier(jnp.sum(kernel_terms, 0)) * grad_scale, lax.optimization_barrier(jnp.sum(head_terms, 0)) * grad_scale, lax.optimization_barrier(jnp.sum(bias_terms, 0)) * grad_scale)
```

```python
import functools
import math

import jax
import jax.numpy as jnp
from jax import lax
from jax.experimental import pallas as pl
from jax.experimental.pallas import tpu as pltpu
from jax.sharding import PartitionSpec as P

f32 = jnp.float32
bf16 = jnp.bfloat16
kl_weight = 1.0
LANES = 128
TAIL = 8


def dot(a, b, ca, cb):
    return lax.dot_general(a, b, (((ca,), (cb,)), ((), ())), preferred_element_type=f32)


def params():
    return pltpu.CompilerParams(vmem_limit_bytes=24 << 20)


def full_call(kernel, out_shape, scratch, flops, moved, smem=0):
    def call(*args):
        specs = [pl.BlockSpec(memory_space=pltpu.SMEM)] * smem
        specs += [pl.BlockSpec(memory_space=pltpu.VMEM)] * (len(args) - smem)
        return pl.pallas_call(
            kernel,
            out_shape=out_shape,
            in_specs=specs,
            out_specs=jax.tree.map(lambda _: pl.BlockSpec(memory_space=pltpu.VMEM), out_shape),
            scratch_shapes=scratch,
            compiler_params=params(),
            cost_estimate=pl.CostEstimate(flops=flops, bytes_accessed=moved, transcendentals=0),
        )(*args)

    return call


def terms_kernel(
    me_ref, act_ref, next_ref, w_ref, bias_ref, head_ref, up_ref, noise_ref,
    pre_grad_ref, keep_ref, send_ref, stage,
):
    cols = pre_grad_ref.shape[0]
    spaces = keep_ref.shape[0]
    latent = noise_ref.shape[0]
    width = head_ref.shape[1]
    share = width // (2 * spaces) if width % (2 * spaces) == 0 else 0
    first = me_ref[0] == 0
    windows = []
    for row in range(3):
        source = (act_ref[row] if row < 2 else next_ref[...]).astype(f32)
        for lane in range(width // LANES):
            at = row * (width // LANES) + lane
            stage[at, : 2 * cols, :] = source[:, lane * LANES : (lane + 1) * LANES]
            stage[at, 2 * cols :, :] = jnp.zeros((8, LANES), f32)
    for row in range(3):
        for tap in range(3):
            halves = []
            for lane in range(width // LANES):
                at = row * (width // LANES) + lane
                halves.append(stage[at, pl.ds(tap, cols, stride=2), :])
            windows.append(jnp.concatenate(halves, 1).astype(bf16))
    pre_act = jnp.broadcast_to(bias_ref[...], (cols, width))
    for index in range(9):
        pre_act = pre_act + dot(windows[index], w_ref[index], 1, 0)
    gating = jax.nn.sigmoid(pre_act)
    hidden = (pre_act * gating).astype(bf16)
    moments = dot(head_ref[...], hidden, 1, 1)
    mean_part = moments[:latent]
    logvar = moments[latent:]
    tiles = [up_ref[i].astype(f32) for i in range(up_ref.shape[0])]
    upstream = jnp.concatenate(tiles, 1)
    sample = noise_ref[...].astype(f32)
    spread = jnp.exp(0.5 * logvar)
    mean_grad = upstream + kl_weight * mean_part
    logvar_grad = 0.5 * upstream * sample * spread + 0.5 * kl_weight * (spread * spread - 1.0)
    moment_grad = jnp.concatenate([mean_grad, logvar_grad], 0).astype(bf16)
    hidden_grad = dot(moment_grad, head_ref[...], 0, 0)
    pre_grad = (hidden_grad * gating * (1.0 + pre_act * (1.0 - gating))).astype(bf16)
    pre_grad_ref[...] = pre_grad

    def put(s, at, size, even, odd):
        keep_ref[s, at : at + size, :] = jnp.where(first, even, odd)
        send_ref[s, at : at + size, :] = jnp.where(first, odd, even).astype(bf16)

    for index in range(9):
        term = dot(windows[index], pre_grad, 0, 0)
        for s in range(spaces):
            at = 2 * share * s
            put(s, index * share, share, term[at : at + share], term[at + share : at + 2 * share])
    head_term = dot(hidden, moment_grad, 0, 1)
    bias_term = dot(jnp.ones((TAIL, cols), bf16), pre_grad, 1, 0)
    parts = share // TAIL

    def tail(at):
        pieces = [head_term[at + TAIL * i : at + TAIL * (i + 1)] for i in range(parts)]
        pieces.append(bias_term[:, at : at + share])
        used = sum(piece.shape[1] for piece in pieces)
        pieces.append(jnp.zeros((TAIL, width - used), f32))
        return jnp.concatenate(pieces, 1)

    for s in range(spaces):
        at = 2 * share * s
        put(s, 9 * share, TAIL, tail(at), tail(at + share))


def pair_kernel(me_ref, keep_ref, got_ref, *outs):
    me = me_ref[0]
    for k, out in enumerate(outs):
        at = jnp.bitwise_xor(me, k)
        out[...] = (keep_ref[at] + got_ref[at].astype(f32)).astype(out.dtype)


def line_kernel(own_ref, *refs):
    total = own_ref[...]
    for ref in refs[:-1]:
        total = total + ref[...].astype(f32)
    refs[-1][...] = total.astype(bf16)


def final_kernel(scale, a_ref, b_ref, kernel_ref, head_ref, bias_ref):
    share, latents = head_ref.shape
    taps = kernel_ref.shape[0]
    total = (a_ref[...].astype(f32) + b_ref[...].astype(f32)) * scale
    for index in range(taps):
        kernel_ref[index] = total[index * share : (index + 1) * share]
    tail = total[taps * share :]
    for i in range(share // TAIL):
        head_ref[TAIL * i : TAIL * (i + 1), :] = tail[:, latents * i : latents * (i + 1)]
    at = latents * (share // TAIL)
    bias_ref[...] = tail[:1, at : at + share]


def input_kernel(pre_grad_ref, prev_ref, w_ref, out_ref, stage):
    cols, width = pre_grad_ref.shape
    pre_grad = pre_grad_ref[...]
    row_at = lax.broadcasted_iota(jnp.int32, (cols, width), 0)

    def planes(source, row_tap):
        even = dot(source, w_ref[3 * row_tap], 1, 1)
        odd = dot(source, w_ref[3 * row_tap + 1], 1, 1)
        late = pltpu.roll(dot(source, w_ref[3 * row_tap + 2], 1, 1), 1, 0)
        return even + jnp.where(row_at == 0, 0.0, late), odd

    def weave(row, even, odd):
        for lane in range(width // LANES):
            at = row * (width // LANES) + lane
            here = slice(lane * LANES, (lane + 1) * LANES)
            stage[at, pl.ds(0, cols, stride=2), :] = even[:, here]
            stage[at, pl.ds(1, cols, stride=2), :] = odd[:, here]
            out_ref[row, :, here] = stage[at].astype(bf16)

    even, odd = planes(pre_grad, 1)
    weave(1, even, odd)
    even, odd = planes(pre_grad, 0)
    even_rim, odd_rim = planes(prev_ref[...], 2)
    weave(0, even + even_rim, odd + odd_rim)


def body(activations, conv_weight, conv_bias, head_weight, latent_grad, noise_sample):
    frames, double_rows, double_cols, channels = activations.shape
    cols = double_cols // 2
    latent_dim = latent_grad.shape[-1]
    spaces = lax.axis_size("space")
    times = lax.axis_size("tm")
    line = ("space", "col")
    peers = lax.axis_size(line)
    assert frames == 1 and double_rows == 2 and lax.axis_size("col") == 2
    taps = conv_weight.reshape(9, channels, channels)
    col_at = lax.axis_index("col").astype(jnp.int32).reshape(1)
    space_at = lax.axis_index("space").astype(jnp.int32).reshape(1)

    next_row = lax.ppermute(activations[0, 0], line, [(i, i - 1) for i in range(1, peers)])
    tiles = jnp.transpose(latent_grad[0], (0, 2, 1))
    upstream = lax.all_to_all(tiles, line, split_axis=0, concat_axis=0, tiled=True)

    share = channels // peers
    if share % TAIL or spaces & (spaces - 1) or spaces > 4 or times != 2:
        return wide_body(
            activations, taps, conv_bias, head_weight, upstream, noise_sample, next_row
        )
    rows = 9 * share + TAIL
    square = 2 * cols * channels * channels
    pre_grad, keep, send = full_call(
        terms_kernel,
        (
            jax.ShapeDtypeStruct((cols, channels), bf16),
            jax.ShapeDtypeStruct((spaces, rows, channels), f32),
            jax.ShapeDtypeStruct((spaces, rows, channels), bf16),
        ),
        [pltpu.VMEM((3 * (channels // LANES), double_cols + 8, LANES), f32)],
        18 * square,
        6 << 20,
        1,
    )(
        col_at,
        activations[0],
        next_row,
        taps,
        conv_bias.reshape(1, channels),
        head_weight.T,
        upstream,
        jnp.transpose(noise_sample[0, 0]),
    )
    got = lax.ppermute(send, "col", [(0, 1), (1, 0)])
    pieces = full_call(
        pair_kernel,
        tuple(
            jax.ShapeDtypeStruct((rows, channels), f32 if k == 0 else bf16) for k in range(spaces)
        ),
        [],
        spaces * rows * channels,
        3 << 20,
        1,
    )(space_at, keep, got)
    far = [
        lax.ppermute(pieces[k], "space", [(i, i ^ k) for i in range(spaces)])
        for k in range(1, spaces)
    ]
    prev = lax.ppermute(pre_grad, line, [(i, i + 1) for i in range(peers - 1)])
    x_grad = full_call(
        input_kernel,
        jax.ShapeDtypeStruct((2, double_cols, channels), bf16),
        [pltpu.VMEM((2 * (channels // LANES), double_cols, LANES), f32)],
        9 * square,
        4 << 20,
    )(pre_grad, prev, taps)
    frame_term = full_call(
        line_kernel,
        jax.ShapeDtypeStruct((rows, channels), bf16),
        [],
        4 * rows * channels,
        1 << 20,
    )(pieces[0], *far)
    other = lax.ppermute(frame_term, "tm", [(0, 1), (1, 0)])
    positions = frames * times * peers * cols
    kernel_grad, head_grad, bias_grad = full_call(
        functools.partial(final_kernel, 1.0 / math.sqrt(positions)),
        (
            jax.ShapeDtypeStruct((9, share, channels), f32),
            jax.ShapeDtypeStruct((share, 2 * latent_dim), f32),
            jax.ShapeDtypeStruct((1, share), f32),
        ),
        [],
        rows * channels,
        1 << 20,
    )(frame_term, other)
    return (
        x_grad[None],
        kernel_grad.reshape(3, 3, share, channels),
        head_grad,
        bias_grad.reshape(share),
    )


def wide_body(activations, taps, conv_bias, head_weight, upstream, noise_sample, next_row):
    _, _, double_cols, channels = activations.shape
    cols = double_cols // 2
    latent_dim = noise_sample.shape[-1]
    line = ("space", "col")
    peers = lax.axis_size(line)
    padded = jnp.pad(jnp.concatenate([activations[0], next_row[None]], 0), ((0, 0), (0, 1), (0, 0)))
    windows = [
        padded[index // 3, index % 3 : index % 3 + 2 * cols : 2] for index in range(9)
    ]
    pre_act = jnp.zeros((cols, channels), f32) + conv_bias
    for index in range(9):
        pre_act = pre_act + dot(windows[index], taps[index], 1, 0)
    gating = jax.nn.sigmoid(pre_act)
    hidden = (pre_act * gating).astype(bf16)
    moments = dot(hidden, head_weight, 1, 0)
    upstream = jnp.transpose(upstream, (0, 2, 1)).reshape(cols, latent_dim).astype(f32)
    spread = jnp.exp(0.5 * moments[:, latent_dim:])
    mean_grad = upstream + kl_weight * moments[:, :latent_dim]
    logvar_grad = 0.5 * upstream * noise_sample[0, 0].astype(f32) * spread
    logvar_grad = logvar_grad + 0.5 * kl_weight * (spread * spread - 1.0)
    moment_grad = jnp.concatenate([mean_grad, logvar_grad], 1).astype(bf16)
    hidden_grad = dot(moment_grad, head_weight, 1, 1)
    pre_grad = (hidden_grad * gating * (1.0 + pre_act * (1.0 - gating))).astype(bf16)
    prev = lax.ppermute(pre_grad, line, [(i, i + 1) for i in range(peers - 1)])
    x_grad = full_call(
        input_kernel,
        jax.ShapeDtypeStruct((2, double_cols, channels), bf16),
        [pltpu.VMEM((2 * (channels // LANES), double_cols, LANES), f32)],
        18 * cols * channels * channels,
        4 << 20,
    )(pre_grad, prev, taps)
    kernel_term = jnp.stack([dot(window, pre_grad, 0, 0) for window in windows], 1)
    terms = (
        kernel_term.reshape(channels, 9 * channels),
        dot(hidden, moment_grad, 0, 0),
        jnp.sum(pre_grad, axis=0, dtype=f32),
    )
    grad_scale = 1.0 / math.sqrt(lax.axis_size("tm") * peers * cols)
    shares = [
        lax.psum_scatter(lax.psum(term, "tm"), line, scatter_dimension=0, tiled=True) * grad_scale
        for term in terms
    ]
    kernel_grad = jnp.transpose(shares[0].reshape(-1, 3, 3, channels), (1, 2, 0, 3))
    return x_grad[None], kernel_grad, shares[1], shares[2]


def solution(mesh):
    in_specs = (
        P(("groups", "tm"), ("space", "col"), None, None),
        P(),
        P(),
        P(),
        P(("groups", "tm"), None, ("space", "col"), None),
        P(("groups", "tm"), ("space", "col"), None, None),
    )
    out_specs = (
        P(("groups", "tm"), ("space", "col"), None, None),
        P(None, None, ("groups", "space", "col"), None),
        P(("groups", "space", "col"), None),
        P(("groups", "space", "col")),
    )
    return jax.shard_map(body, mesh=mesh, in_specs=in_specs, out_specs=out_specs, check_vma=False)
```

```python
import functools
import math

import jax
import jax.numpy as jnp
from jax import lax
from jax.experimental import pallas as pl
from jax.experimental.pallas import tpu as pltpu
from jax.sharding import PartitionSpec as P

f32 = jnp.float32
bf16 = jnp.bfloat16
kl_weight = 1.0
LANES = 128
HALVED = 6
TAIL = 8


def dot(a, b, ca, cb):
    return lax.dot_general(a, b, (((ca,), (cb,)), ((), ())), preferred_element_type=f32)


def params():
    return pltpu.CompilerParams(vmem_limit_bytes=24 << 20)


SPACES = {"s": pltpu.SMEM, "v": pltpu.VMEM, "h": pltpu.HBM}


def full_call(kernel, out_shape, scratch, flops, moved, places):
    call = pl.pallas_call(
        kernel,
        out_shape=out_shape,
        in_specs=[pl.BlockSpec(memory_space=SPACES[place]) for place in places],
        out_specs=jax.tree.map(lambda _: pl.BlockSpec(memory_space=pltpu.VMEM), out_shape),
        scratch_shapes=scratch,
        compiler_params=params(),
        cost_estimate=pl.CostEstimate(flops=flops, bytes_accessed=moved, transcendentals=0),
    )

    def placed(*args):
        pinned = [
            pltpu.with_memory_space_constraint(arg, pltpu.HBM) if place == "h" else arg
            for arg, place in zip(args, places)
        ]
        return call(*pinned)

    return placed


def start_kernel(core_ref, act_ref, tiles_ref, row_ref, later_ref, own_ref, send_ref, sems):
    core = core_ref[0]
    half = later_ref.shape[0]
    copies = [
        pltpu.make_async_copy(act_ref.at[0, pl.ds(half, half)], later_ref, sems.at[0]),
        pltpu.make_async_copy(act_ref.at[0], row_ref, sems.at[1]),
    ]
    for j in range(own_ref.shape[0]):
        mine = tiles_ref.at[2 * j + core]
        theirs = tiles_ref.at[2 * j + 1 - core]
        copies.append(pltpu.make_async_copy(mine, own_ref.at[j], sems.at[2 + 2 * j]))
        copies.append(pltpu.make_async_copy(theirs, send_ref.at[j], sems.at[3 + 2 * j]))
    for copy in copies:
        copy.start()
    for copy in copies:
        copy.wait()


def tiles_kernel(core_ref, space_ref, row_ref, later_ref, own_ref, got_ref, *outs):
    spaces = own_ref.shape[0]
    height, width = own_ref.shape[1:]
    half = later_ref.shape[0]
    first = core_ref[0] == 0
    down = outs[-1]
    down[:half, :] = jnp.where(first, row_ref[:half, :], later_ref[...])
    for k, out in enumerate(outs):
        at = lax.rem(space_ref[0] + k, spaces)
        mine, other = own_ref[at], got_ref[at]
        top = half if k == spaces - 1 else 0
        lanes = out.shape[1]
        pieces = [jnp.where(first, mine, other), jnp.where(first, other, mine)]
        pieces.append(jnp.zeros((height, lanes - 2 * width), bf16))
        out[top:, :] = jnp.concatenate(pieces, 1)


def split_columns(row, source, stage):
    length, width = source.shape
    lanes = width // LANES
    source = source.astype(f32)
    for lane in range(lanes):
        stage[row * lanes + lane, :length, :] = source[:, lane * LANES : (lane + 1) * LANES]
        stage[row * lanes + lane, length:, :] = jnp.zeros((8, LANES), f32)
    windows = []
    for tap in range(3):
        halves = [
            stage[row * lanes + lane, pl.ds(tap, length // 2, stride=2), :]
            for lane in range(lanes)
        ]
        windows.append(jnp.concatenate(halves, 1).astype(bf16))
    return windows


def early_kernel(
    act_ref, w_in, bias_in, head_in, noise_in,
    windows_ref, pre_act_ref, w_ref, head_ref, noise_ref, act, bias, stage, sems,
):
    pairs = [
        (act_ref.at[0], act.at[0]), (w_in.at[:3], w_ref.at[:3]),
        (act_ref.at[1], act.at[1]), (w_in.at[3:6], w_ref.at[3:6]),
        (bias_in, bias), (w_in.at[6:], w_ref.at[6:]), (head_in, head_ref), (noise_in, noise_ref),
    ]
    copies = [pltpu.make_async_copy(a, b, sems.at[i]) for i, (a, b) in enumerate(pairs)]
    for copy in copies:
        copy.start()
    copies[4].wait()
    pre_act = jnp.broadcast_to(bias[...], pre_act_ref.shape)
    for row in range(2):
        copies[2 * row].wait()
        windows = split_columns(row, act[row], stage)
        copies[2 * row + 1].wait()
        for tap in range(3):
            windows_ref[3 * row + tap] = windows[tap]
            pre_act = pre_act + dot(windows[tap], w_ref[3 * row + tap], 1, 0)
    pre_act_ref[...] = pre_act
    for copy in copies[5:]:
        copy.wait()


def terms_kernel(
    core_ref, space_ref, windows_ref, early_ref, w_ref, head_ref, noise_ref,
    beside_ref, fixed_ref, *rest,
):
    spaces = len(rest) - 7
    tiles = rest[:spaces]
    pre_grad_ref, keep_a, send_a, keep_b, send_b, tiles_at, stage = rest[spaces:]
    cols, width = pre_grad_ref.shape
    latent = noise_ref.shape[0]
    share = width // (2 * spaces)
    first = core_ref[0] == 0
    height, lanes = tiles_at.shape[1:]
    for k in range(spaces):
        top = tiles[k].shape[0] - height
        tiles_at[lax.rem(space_ref[0] + spaces - k, spaces)] = tiles[k][top:, :lanes]
    half = tiles[-1].shape[0] - height
    above = jnp.concatenate([fixed_ref[:half, :], tiles[-1][:half, :]], 0)
    above = jnp.where(space_ref[0] == spaces - 1, jnp.zeros_like(above), above)
    next_row = jnp.where(first, beside_ref[...], above)
    windows = [windows_ref[i] for i in range(6)] + split_columns(0, next_row, stage)
    pre_act = early_ref[...]
    for index in range(6, 9):
        pre_act = pre_act + dot(windows[index], w_ref[index], 1, 0)
    gating = jax.nn.sigmoid(pre_act)
    hidden = (pre_act * gating).astype(bf16)
    moments = dot(head_ref[...], hidden, 1, 1)
    mean_part = moments[:latent]
    logvar = moments[latent:]
    upstream = jnp.concatenate(
        [tiles_at[i][:, : cols // spaces].astype(f32) for i in range(spaces)], 1
    )
    sample = noise_ref[...].astype(f32)
    spread = jnp.exp(0.5 * logvar)
    mean_grad = upstream + kl_weight * mean_part
    logvar_grad = 0.5 * upstream * sample * spread + 0.5 * kl_weight * (spread * spread - 1.0)
    moment_grad = jnp.concatenate([mean_grad, logvar_grad], 0).astype(bf16)
    hidden_grad = dot(moment_grad, head_ref[...], 0, 0)
    pre_grad = (hidden_grad * gating * (1.0 + pre_act * (1.0 - gating))).astype(bf16)
    pre_grad_ref[...] = pre_grad

    def put(keep_ref, send_ref, s, at, even, odd):
        here = slice(at, at + even.shape[0])
        keep_ref[s, here, :] = jnp.where(first, even, odd)
        send_ref[s, here, :] = jnp.where(first, odd, even).astype(bf16)

    for index in range(9):
        term = dot(windows[index], pre_grad, 0, 0)
        refs = (keep_a, send_a) if index < HALVED else (keep_b, send_b)
        at = share * (index if index < HALVED else index - HALVED)
        for s in range(spaces):
            row = 2 * share * s
            put(*refs, s, at, term[row : row + share], term[row + share : row + 2 * share])
    head_term = dot(hidden, moment_grad, 0, 1)
    bias_term = dot(jnp.ones((TAIL, cols), bf16), pre_grad, 1, 0)

    def tail(row):
        pieces = [head_term[row + i : row + i + TAIL] for i in range(0, share, TAIL)]
        pieces.append(bias_term[:, row : row + share])
        used = sum(piece.shape[1] for piece in pieces)
        pieces.append(jnp.zeros((TAIL, width - used), f32))
        return jnp.concatenate(pieces, 1)

    for s in range(spaces):
        row = 2 * share * s
        put(keep_b, send_b, s, (9 - HALVED) * share, tail(row), tail(row + share))


def halve_kernel(time_ref, keep_ref, got_ref, own_ref, send_ref):
    half = own_ref.shape[2]
    first = time_ref[0] == 0
    total = keep_ref[...] + got_ref[...].astype(f32)
    own_ref[...] = jnp.where(first, total[:, :, :half], total[:, :, half:])
    send_ref[...] = jnp.where(first, total[:, :, half:], total[:, :, :half]).astype(bf16)


def pair_kernel(space_ref, keep_ref, got_ref, *outs):
    spaces = len(outs)
    for k, out in enumerate(outs):
        at = lax.rem(space_ref[0] + k, spaces)
        out[...] = (keep_ref[at] + got_ref[at].astype(f32)).astype(out.dtype)


def pair_rim_kernel(core_ref, space_ref, keep_ref, got_ref, mine_ref, beside_ref, *outs):
    spaces = len(outs)
    rows = keep_ref.shape[1]
    for k, out in enumerate(outs):
        at = lax.rem(space_ref[0] + k, spaces)
        out[:rows, :] = (keep_ref[at] + got_ref[at].astype(f32)).astype(out.dtype)
    half = mine_ref.shape[0] // 2
    first = core_ref[0] == 0
    outs[1][rows:, :] = jnp.where(first, beside_ref[half:, :], mine_ref[:half, :])


def line_kernel(own_ref, *refs):
    total = own_ref[...]
    for ref in refs[:-1]:
        total = total + ref[...].astype(f32)
    refs[-1][...] = total.astype(bf16)


def line_rim_kernel(own_ref, *refs):
    rows = own_ref.shape[0]
    total = own_ref[...]
    for ref in refs[:-2]:
        total = total + ref[:rows, :].astype(f32)
    refs[-2][...] = total.astype(bf16)
    refs[-1][...] = refs[0][rows:, :]


def final_kernel(
    scale, time_ref, a_ref, a_far_ref, b_ref, b_far_ref, kernel_ref, head_ref, bias_ref
):
    share, latents = head_ref.shape
    first = time_ref[0] == 0
    mine, far = a_ref[...].astype(f32) * scale, a_far_ref[...].astype(f32) * scale
    low, high = jnp.where(first, mine, far), jnp.where(first, far, mine)
    total = (b_ref[...].astype(f32) + b_far_ref[...].astype(f32)) * scale
    half = mine.shape[1]
    for index in range(HALVED):
        kernel_ref[index, :, :half] = low[index * share : (index + 1) * share]
        kernel_ref[index, :, half:] = high[index * share : (index + 1) * share]
    for index in range(HALVED, 9):
        at = (index - HALVED) * share
        kernel_ref[index] = total[at : at + share]
    tail = total[(9 - HALVED) * share :]
    for i in range(share // TAIL):
        head_ref[TAIL * i : TAIL * (i + 1), :] = tail[:, latents * i : latents * (i + 1)]
    at = latents * (share // TAIL)
    bias_ref[...] = tail[:1, at : at + share]


def input_kernel(pre_grad_ref, prev_ref, w_ref, out_ref, stage):
    input_rows(pre_grad_ref, prev_ref[...], w_ref, out_ref, stage)


def input_chip_kernel(
    core_ref, space_ref, pre_grad_ref, beside_ref, low_ref, high_ref, w_ref, out_ref, stage
):
    below = jnp.concatenate([low_ref[...], high_ref[...]], 0)
    below = jnp.where(space_ref[0] == 0, jnp.zeros_like(below), below)
    prev = jnp.where(core_ref[0] == 0, below, beside_ref[...])
    input_rows(pre_grad_ref, prev, w_ref, out_ref, stage)


def input_rows(pre_grad_ref, prev, w_ref, out_ref, stage):
    cols, width = pre_grad_ref.shape
    pre_grad = pre_grad_ref[...]
    row_at = lax.broadcasted_iota(jnp.int32, (cols, width), 0)

    def planes(source, row_tap):
        even = dot(source, w_ref[3 * row_tap], 1, 1)
        odd = dot(source, w_ref[3 * row_tap + 1], 1, 1)
        late = pltpu.roll(dot(source, w_ref[3 * row_tap + 2], 1, 1), 1, 0)
        return even + jnp.where(row_at == 0, 0.0, late), odd

    def weave(row, even, odd):
        for lane in range(width // LANES):
            at = row * (width // LANES) + lane
            here = slice(lane * LANES, (lane + 1) * LANES)
            stage[at, pl.ds(0, cols, stride=2), :] = even[:, here]
            stage[at, pl.ds(1, cols, stride=2), :] = odd[:, here]
            out_ref[row, :, here] = stage[at].astype(bf16)

    even, odd = planes(pre_grad, 1)
    weave(1, even, odd)
    even, odd = planes(pre_grad, 0)
    even_rim, odd_rim = planes(prev, 2)
    weave(0, even + even_rim, odd + odd_rim)


def body(activations, conv_weight, conv_bias, head_weight, latent_grad, noise_sample):
    frames, double_rows, double_cols, channels = activations.shape
    cols = double_cols // 2
    latent_dim = latent_grad.shape[-1]
    spaces = lax.axis_size("space")
    times = lax.axis_size("tm")
    line = ("space", "col")
    peers = lax.axis_size(line)
    assert frames == 1 and double_rows == 2 and lax.axis_size("col") == 2
    share = channels // peers
    taps = conv_weight.reshape(9, channels, channels)
    tiles = jnp.transpose(latent_grad[0], (0, 2, 1))
    if share % TAIL or not 2 <= spaces <= 4 or times != 2:
        return wide_body(activations, taps, conv_bias, head_weight, tiles, noise_sample)
    core_at = lax.axis_index("col").astype(jnp.int32).reshape(1)
    space_at = lax.axis_index("space").astype(jnp.int32).reshape(1)
    time_at = lax.axis_index("tm").astype(jnp.int32).reshape(1)
    swap = [(0, 1), (1, 0)]
    hops = list(range(spaces - 1, 0, -1))
    down = spaces - 1
    array = jax.ShapeDtypeStruct

    def over_space(pieces):
        sent = {
            k: lax.ppermute(pieces[k], "space", [(i, (i + k) % spaces) for i in range(spaces)])
            for k in hops
        }
        return [sent[k] for k in range(1, spaces)]

    tile = tiles.shape[1:]
    row, later, own_tiles, send_tiles = full_call(
        start_kernel,
        (
            array((double_cols, channels), bf16),
            array((cols, channels), bf16),
            array((spaces, *tile), bf16),
            array((spaces, *tile), bf16),
        ),
        [pltpu.SemaphoreType.DMA((2 + 2 * spaces,))],
        0,
        1 << 19,
        "shh",
    )(core_at, activations[0], tiles)
    got_tiles = lax.ppermute(send_tiles, "col", swap)
    got_later = lax.ppermute(later, "col", swap)
    tile_sets = full_call(
        tiles_kernel,
        tuple(
            array((cols + tile[0], channels) if k == down else (tile[0], LANES), bf16)
            for k in range(spaces)
        ),
        [],
        0,
        1 << 15,
        "ssvvvv",
    )(core_at, space_at, row, got_later, own_tiles, got_tiles)
    far_tiles = over_space(tile_sets)
    beside = lax.ppermute(row, "col", swap)
    square = 2 * cols * channels * channels
    windows, early, w_here, head_here, noise_here = full_call(
        early_kernel,
        (
            array((6, cols, channels), bf16),
            array((cols, channels), f32),
            array(taps.shape, bf16),
            array((2 * latent_dim, channels), bf16),
            array((latent_dim, cols), bf16),
        ),
        [
            pltpu.VMEM((2, double_cols, channels), bf16),
            pltpu.VMEM((1, channels), f32),
            pltpu.VMEM((2 * (channels // LANES), double_cols + 8, LANES), f32),
            pltpu.SemaphoreType.DMA((8,)),
        ],
        6 * square,
        5 << 20,
        "hhhhh",
    )(
        activations[0],
        taps,
        conv_bias.reshape(1, channels),
        head_weight.T,
        jnp.transpose(noise_sample[0, 0]),
    )
    early, *far_tiles = lax.optimization_barrier((early, *far_tiles))
    fixed = lax.ppermute(far_tiles[-1], "col", swap)
    rows_a = HALVED * share
    rows_b = (9 - HALVED) * share + TAIL
    half = channels // 2
    pre_grad, keep_a, send_a, keep_b, send_b = full_call(
        terms_kernel,
        (
            array((cols, channels), bf16),
            array((spaces, rows_a, channels), f32),
            array((spaces, rows_a, channels), bf16),
            array((spaces, rows_b, channels), f32),
            array((spaces, rows_b, channels), bf16),
        ),
        [
            pltpu.VMEM((spaces, tile[0], LANES), bf16),
            pltpu.VMEM((channels // LANES, double_cols + 8, LANES), f32),
        ],
        12 * square,
        5 << 20,
        "ss" + "v" * (7 + spaces),
    )(
        core_at, space_at, windows, early, w_here, head_here, noise_here, beside, fixed,
        tile_sets[0], *far_tiles,
    )
    beside_grad = lax.ppermute(pre_grad, "col", swap)
    got_a = lax.ppermute(send_a, "col", swap)
    got_b = lax.ppermute(send_b, "col", swap)
    own_a, cross_a = full_call(
        halve_kernel,
        (array((spaces, rows_a, half), f32), array((spaces, rows_a, half), bf16)),
        [],
        spaces * rows_a * channels,
        2 << 20,
        "svv",
    )(time_at, keep_a, got_a)
    crossed_a = lax.ppermute(cross_a, "tm", swap)

    half_grad = cols // 2
    pieces_b = full_call(
        pair_rim_kernel,
        tuple(
            array((rows_b + (half_grad if k == 1 else 0), channels), f32 if k == 0 else bf16)
            for k in range(spaces)
        ),
        [],
        spaces * rows_b * channels,
        1 << 20,
        "ssvvvv",
    )(core_at, space_at, keep_b, got_b, pre_grad, beside_grad)
    far_b = over_space(pieces_b)
    pieces_a = full_call(
        pair_kernel,
        tuple(array((rows_a, half), f32 if k == 0 else bf16) for k in range(spaces)),
        [],
        spaces * rows_a * half,
        1 << 20,
        "svv",
    )(space_at, own_a, crossed_a)
    far_a = over_space(pieces_a)
    sum_b, high = full_call(
        line_rim_kernel,
        (array((rows_b, channels), bf16), array((half_grad, channels), bf16)),
        [],
        4 * rows_b * channels,
        1 << 19,
        "v" * spaces,
    )(pieces_b[0], *far_b)
    other_b = lax.ppermute(sum_b, "tm", swap)
    low = lax.ppermute(high, "col", swap)
    sum_a = full_call(
        line_kernel, array((rows_a, half), bf16), [], 4 * rows_a * half, 1 << 19, "v" * spaces
    )(pieces_a[0], *far_a)
    other_a = lax.ppermute(sum_a, "tm", swap)
    x_grad = full_call(
        input_chip_kernel,
        array((2, double_cols, channels), bf16),
        [pltpu.VMEM((2 * (channels // LANES), double_cols, LANES), f32)],
        9 * square,
        4 << 20,
        "ssvvvvv",
    )(core_at, space_at, pre_grad, beside_grad, low, high, w_here)
    positions = frames * times * peers * cols
    kernel_grad, head_grad, bias_grad = full_call(
        functools.partial(final_kernel, 1.0 / math.sqrt(positions)),
        (
            array((9, share, channels), f32),
            array((share, 2 * latent_dim), f32),
            array((1, share), f32),
        ),
        [],
        rows_a * half + rows_b * channels,
        1 << 20,
        "svvvv",
    )(time_at, sum_a, other_a, sum_b, other_b)
    return (
        x_grad[None],
        kernel_grad.reshape(3, 3, share, channels),
        head_grad,
        bias_grad.reshape(share),
    )


def input_gradient(pre_grad, prev, taps):
    cols, channels = pre_grad.shape
    return full_call(
        input_kernel,
        jax.ShapeDtypeStruct((2, 2 * cols, channels), bf16),
        [pltpu.VMEM((2 * (channels // LANES), 2 * cols, LANES), f32)],
        18 * cols * channels * channels,
        4 << 20,
        "vvv",
    )(pre_grad, prev, taps)


def wide_body(activations, taps, conv_bias, head_weight, tiles, noise_sample):
    _, _, double_cols, channels = activations.shape
    cols = double_cols // 2
    latent_dim = noise_sample.shape[-1]
    line = ("space", "col")
    peers = lax.axis_size(line)
    next_row = lax.ppermute(activations[0, 0], line, [(i, i - 1) for i in range(1, peers)])
    upstream = lax.all_to_all(tiles, line, split_axis=0, concat_axis=0, tiled=True)
    padded = jnp.pad(jnp.concatenate([activations[0], next_row[None]], 0), ((0, 0), (0, 1), (0, 0)))
    windows = [
        padded[index // 3, index % 3 : index % 3 + 2 * cols : 2] for index in range(9)
    ]
    pre_act = jnp.zeros((cols, channels), f32) + conv_bias
    for index in range(9):
        pre_act = pre_act + dot(windows[index], taps[index], 1, 0)
    gating = jax.nn.sigmoid(pre_act)
    hidden = (pre_act * gating).astype(bf16)
    moments = dot(hidden, head_weight, 1, 0)
    upstream = jnp.transpose(upstream, (0, 2, 1)).reshape(cols, latent_dim).astype(f32)
    spread = jnp.exp(0.5 * moments[:, latent_dim:])
    mean_grad = upstream + kl_weight * moments[:, :latent_dim]
    logvar_grad = 0.5 * upstream * noise_sample[0, 0].astype(f32) * spread
    logvar_grad = logvar_grad + 0.5 * kl_weight * (spread * spread - 1.0)
    moment_grad = jnp.concatenate([mean_grad, logvar_grad], 1).astype(bf16)
    hidden_grad = dot(moment_grad, head_weight, 1, 1)
    pre_grad = (hidden_grad * gating * (1.0 + pre_act * (1.0 - gating))).astype(bf16)
    prev = lax.ppermute(pre_grad, line, [(i, i + 1) for i in range(peers - 1)])
    x_grad = input_gradient(pre_grad, prev, taps)
    kernel_term = jnp.stack([dot(window, pre_grad, 0, 0) for window in windows], 1)
    terms = (
        kernel_term.reshape(channels, 9 * channels),
        dot(hidden, moment_grad, 0, 0),
        jnp.sum(pre_grad, axis=0, dtype=f32),
    )
    grad_scale = 1.0 / math.sqrt(lax.axis_size("tm") * peers * cols)
    shares = [
        lax.psum_scatter(lax.psum(term, "tm"), line, scatter_dimension=0, tiled=True) * grad_scale
        for term in terms
    ]
    kernel_grad = jnp.transpose(shares[0].reshape(-1, 3, 3, channels), (1, 2, 0, 3))
    return x_grad[None], kernel_grad, shares[1], shares[2]


def solution(mesh):
    in_specs = (
        P(("groups", "tm"), ("space", "col"), None, None),
        P(),
        P(),
        P(),
        P(("groups", "tm"), None, ("space", "col"), None),
        P(("groups", "tm"), ("space", "col"), None, None),
    )
    out_specs = (
        P(("groups", "tm"), ("space", "col"), None, None),
        P(None, None, ("groups", "space", "col"), None),
        P(("groups", "space", "col"), None),
        P(("groups", "space", "col")),
    )
    return jax.shard_map(body, mesh=mesh, in_specs=in_specs, out_specs=out_specs, check_vma=False)
```

```python
import functools
import math

import jax
import jax.numpy as jnp
from jax import lax
from jax.experimental import pallas as pl
from jax.experimental.pallas import tpu as pltpu
from jax.sharding import PartitionSpec as P

f32 = jnp.float32
bf16 = jnp.bfloat16
kl_weight = 1.0
LANES = 128
HALVED = 6
TAIL = 8


def dot(a, b, ca, cb):
    return lax.dot_general(a, b, (((ca,), (cb,)), ((), ())), preferred_element_type=f32)


def params():
    return pltpu.CompilerParams(vmem_limit_bytes=12 << 20)


SPACES = {"s": pltpu.SMEM, "v": pltpu.VMEM, "h": pltpu.HBM}


def full_call(kernel, out_shape, scratch, flops, moved, places):
    call = pl.pallas_call(
        kernel,
        out_shape=out_shape,
        in_specs=[pl.BlockSpec(memory_space=SPACES[place]) for place in places],
        out_specs=jax.tree.map(lambda _: pl.BlockSpec(memory_space=pltpu.VMEM), out_shape),
        scratch_shapes=scratch,
        compiler_params=params(),
        cost_estimate=pl.CostEstimate(flops=flops, bytes_accessed=moved, transcendentals=0),
    )

    def placed(*args):
        pinned = [
            pltpu.with_memory_space_constraint(arg, pltpu.HBM) if place == "h" else arg
            for arg, place in zip(args, places)
        ]
        return call(*pinned)

    return placed


def start_kernel(act_ref, tiles_in, row_ref, tiles_ref, sems):
    copies = [
        pltpu.make_async_copy(tiles_in, tiles_ref, sems.at[0]),
        pltpu.make_async_copy(act_ref.at[0], row_ref, sems.at[1]),
    ]
    for copy in copies:
        copy.start()
    for copy in copies:
        copy.wait()


def tiles_kernel(core_ref, space_ref, row_ref, own_ref, got_ref, here_ref, far_ref, down_ref):
    spaces = own_ref.shape[0] // 2
    height, width = own_ref.shape[1:]
    cols = row_ref.shape[0]
    core, chip = core_ref[0], space_ref[0]
    first = core == 0

    def side_by_side(at):
        mine, other = own_ref[at], got_ref[at]
        return [jnp.where(first, mine, other), jnp.where(first, other, mine)]

    def put(ref, top, pieces):
        used = width * len(pieces)
        if used < ref.shape[1]:
            pieces = [*pieces, jnp.zeros((height, ref.shape[1] - used), bf16)]
        ref[top:, :] = jnp.concatenate(pieces, 1)

    put(here_ref, 0, side_by_side(2 * chip + core))
    there = 2 * lax.rem(chip + 1 + core, spaces)
    put(far_ref, 0, side_by_side(there) + side_by_side(there + 1))
    down_ref[:cols, :] = row_ref[...]
    there = 2 * lax.rem(chip + spaces - 1, spaces)
    put(down_ref, cols, side_by_side(there) + side_by_side(there + 1))


def split_columns(row, source, stage):
    length, width = source.shape
    lanes = width // LANES
    source = source.astype(f32)
    for lane in range(lanes):
        stage[row * lanes + lane, :length, :] = source[:, lane * LANES : (lane + 1) * LANES]
        stage[row * lanes + lane, length:, :] = jnp.zeros((8, LANES), f32)
    windows = []
    for tap in range(3):
        halves = [
            stage[row * lanes + lane, pl.ds(tap, length // 2, stride=2), :]
            for lane in range(lanes)
        ]
        windows.append(jnp.concatenate(halves, 1).astype(bf16))
    return windows


def early_kernel(
    act_ref, w_in, bias_in, head_in, noise_in, here_ref,
    windows_ref, pre_act_ref, w_ref, act, bias, head, noise, stage, sems,
):
    pairs = [
        (act_ref.at[0], act.at[0]), (w_in.at[:3], w_ref.at[:3]),
        (act_ref.at[1], act.at[1]), (w_in.at[3:6], w_ref.at[3:6]),
        (bias_in, bias), (w_in.at[6:], w_ref.at[6:]), (head_in, head), (noise_in, noise),
    ]
    copies = [pltpu.make_async_copy(a, b, sems.at[i]) for i, (a, b) in enumerate(pairs)]
    for copy in copies:
        copy.start()
    copies[4].wait()
    cols = noise.shape[1]
    width = head.shape[1]
    pre_act = jnp.broadcast_to(bias[...], (cols, width))
    for row in range(2):
        copies[2 * row].wait()
        windows = split_columns(row, act[row], stage)
        copies[2 * row + 1].wait()
        for tap in range(3):
            windows_ref[3 * row + tap] = windows[tap]
            pre_act = pre_act + dot(windows[tap], w_ref[3 * row + tap], 1, 0)
    pre_act_ref[:cols, :] = pre_act
    for copy in copies[5:]:
        copy.wait()
    at = cols
    for ref in (head, noise, here_ref):
        pre_act_ref[at : at + ref.shape[0], : ref.shape[1]] = ref[...].astype(f32)
        at += ref.shape[0]


def conv_kernel(
    chips, core_ref, space_ref, early_ref, w_ref, far_ref, above_ref,
    pre_act_ref, windows_ref, hidden_ref, tiles_ref, stage,
):
    cols = hidden_ref.shape[0]
    height = far_ref.shape[0]
    lanes = far_ref.shape[1]
    last = (core_ref[0] == 1) & (space_ref[0] == chips - 1)
    row = above_ref[: 2 * cols, :]
    windows = split_columns(0, jnp.where(last, jnp.zeros_like(row), row), stage)
    tiles_ref[:height, :] = far_ref[...]
    tiles_ref[height:, :] = above_ref[2 * cols :, :lanes]
    pre_act = early_ref[:cols, :]
    for tap in range(3):
        windows_ref[tap] = windows[tap]
        pre_act = pre_act + dot(windows[tap], w_ref[6 + tap], 1, 0)
    pre_act_ref[...] = pre_act
    hidden_ref[...] = jax.nn.silu(pre_act).astype(bf16)


def grad_kernel(
    core_ref, space_ref, early_ref, pre_act_ref, hidden_ref, tiles_ref, other_tiles_ref,
    pre_grad_ref, moment_grad_ref, tiles_at,
):
    cols, width = pre_grad_ref.shape
    spaces, latent, lanes = tiles_at.shape
    head = early_ref[cols : cols + 2 * latent, :].astype(bf16)
    at = cols + 2 * latent
    sample = early_ref[at : at + latent, :cols]
    chip = space_ref[0]
    first = core_ref[0] == 0
    tiles_at[chip] = early_ref[at + latent : at + 2 * latent, :lanes].astype(bf16)
    mine, other = tiles_ref[...], other_tiles_ref[...]
    for there, both in (
        (spaces - 1, jnp.where(first, mine[:latent], other[:latent])),
        (spaces - 2, jnp.where(first, other[:latent], mine[:latent])),
        (1, jnp.where(first, other[latent:], mine[latent:])),
    ):
        band = jnp.where(first, both[:, :lanes], both[:, lanes:])
        tiles_at[lax.rem(chip + there, spaces)] = band
    pre_act = pre_act_ref[...]
    gating = jax.nn.sigmoid(pre_act)
    moments = dot(head, hidden_ref[...], 1, 1)
    mean_part = moments[:latent]
    logvar = moments[latent:]
    upstream = jnp.concatenate([tiles_at[i].astype(f32) for i in range(spaces)], 1)
    spread = jnp.exp(0.5 * logvar)
    mean_grad = upstream + kl_weight * mean_part
    logvar_grad = 0.5 * upstream * sample * spread + 0.5 * kl_weight * (spread * spread - 1.0)
    moment_grad = jnp.concatenate([mean_grad, logvar_grad], 0).astype(bf16)
    hidden_grad = dot(moment_grad, head, 0, 0)
    pre_grad = (hidden_grad * gating * (1.0 + pre_act * (1.0 - gating))).astype(bf16)
    pre_grad_ref[...] = pre_grad
    moment_grad_ref[...] = moment_grad


def put_shares(first, keep_ref, send_ref, at, term):
    spaces = keep_ref.shape[0]
    share = term.shape[0] // (2 * spaces)
    for s in range(spaces):
        row = 2 * share * s
        even, odd = term[row : row + share], term[row + share : row + 2 * share]
        keep_ref[s, at : at + share, :] = jnp.where(first, even, odd)
        send_ref[s, at : at + share, :] = jnp.where(first, odd, even).astype(bf16)


def frame_terms_kernel(
    core_ref, windows_ref, pre_grad_ref, hidden_ref, moment_grad_ref, keep_ref, send_ref
):
    cols, width = pre_grad_ref.shape
    spaces = keep_ref.shape[0]
    share = width // (2 * spaces)
    first = core_ref[0] == 0
    pre_grad = pre_grad_ref[...]
    taps = windows_ref.shape[0]
    for tap in range(taps):
        put_shares(first, keep_ref, send_ref, tap * share, dot(windows_ref[tap], pre_grad, 0, 0))
    head_term = dot(hidden_ref[...], moment_grad_ref[...], 0, 1)
    bias_term = dot(jnp.ones((TAIL, cols), bf16), pre_grad, 1, 0)

    def tail(row):
        pieces = [head_term[row + i : row + i + TAIL] for i in range(0, share, TAIL)]
        pieces.append(bias_term[:, row : row + share])
        used = sum(piece.shape[1] for piece in pieces)
        pieces.append(jnp.zeros((TAIL, width - used), f32))
        return jnp.concatenate(pieces, 1)

    tails = []
    for s in range(2 * spaces):
        tails.append(tail(share * s))
    put_shares(first, keep_ref, send_ref, taps * share, jnp.concatenate(tails, 0))
    rows, part = keep_ref.shape[1], cols // spaces
    for s in range(spaces):
        send_ref[s, rows:, :] = pre_grad[part * s : part * (s + 1)]


def early_terms_kernel(core_ref, windows_ref, pre_grad_ref, keep_ref, send_ref):
    first = core_ref[0] == 0
    pre_grad = pre_grad_ref[...]
    share = pre_grad.shape[1] // (2 * keep_ref.shape[0])
    for index in range(HALVED):
        term = dot(windows_ref[index], pre_grad, 0, 0)
        put_shares(first, keep_ref, send_ref, index * share, term)


def halve_kernel(time_ref, keep_ref, got_ref, own_ref, send_ref):
    half = own_ref.shape[2]
    first = time_ref[0] == 0
    total = keep_ref[...] + got_ref[...].astype(f32)
    own_ref[...] = jnp.where(first, total[:, :, :half], total[:, :, half:])
    send_ref[...] = jnp.where(first, total[:, :, half:], total[:, :, :half]).astype(bf16)


def pair_kernel(space_ref, keep_ref, got_ref, *outs):
    spaces = len(outs)
    for k, out in enumerate(outs):
        at = lax.rem(space_ref[0] + k, spaces)
        out[...] = (keep_ref[at] + got_ref[at].astype(f32)).astype(out.dtype)


def pair_rim_kernel(core_ref, space_ref, keep_ref, got_ref, mine_ref, *outs):
    *outs, beside_ref = outs
    spaces = len(outs)
    rows = keep_ref.shape[1]
    for k, out in enumerate(outs):
        at = lax.rem(space_ref[0] + k, spaces)
        out[:rows, :] = (keep_ref[at] + got_ref[at, :rows, :].astype(f32)).astype(out.dtype)
    half = mine_ref.shape[0] // 2
    first = core_ref[0] == 0
    beside = jnp.concatenate([got_ref[s, rows:, :] for s in range(spaces)], 0)
    beside_ref[...] = beside
    outs[1][rows:, :] = jnp.where(first, beside[half:], mine_ref[:half, :])


def line_kernel(own_ref, *refs):
    total = own_ref[...]
    for ref in refs[:-1]:
        total = total + ref[...].astype(f32)
    refs[-1][...] = total.astype(bf16)


def line_rim_kernel(own_ref, *refs):
    rows = own_ref.shape[0]
    total = own_ref[...]
    for ref in refs[:-2]:
        total = total + ref[:rows, :].astype(f32)
    refs[-2][...] = total.astype(bf16)
    refs[-1][...] = refs[0][rows:, :]


def final_kernel(
    scale, time_ref, a_ref, a_far_ref, b_ref, b_far_ref, kernel_ref, head_ref, bias_ref
):
    share, latents = head_ref.shape
    first = time_ref[0] == 0
    mine, far = a_ref[...].astype(f32) * scale, a_far_ref[...].astype(f32) * scale
    low, high = jnp.where(first, mine, far), jnp.where(first, far, mine)
    total = (b_ref[...].astype(f32) + b_far_ref[...].astype(f32)) * scale
    half = mine.shape[1]
    for index in range(HALVED):
        kernel_ref[index, :, :half] = low[index * share : (index + 1) * share]
        kernel_ref[index, :, half:] = high[index * share : (index + 1) * share]
    for index in range(HALVED, 9):
        at = (index - HALVED) * share
        kernel_ref[index] = total[at : at + share]
    tail = total[(9 - HALVED) * share :]
    for i in range(share // TAIL):
        head_ref[TAIL * i : TAIL * (i + 1), :] = tail[:, latents * i : latents * (i + 1)]
    at = latents * (share // TAIL)
    bias_ref[...] = tail[:1, at : at + share]


def input_kernel(pre_grad_ref, prev_ref, w_ref, out_ref, stage):
    input_rows(pre_grad_ref, prev_ref[...], w_ref, out_ref, stage)


def input_chip_kernel(
    core_ref, space_ref, pre_grad_ref, beside_ref, low_ref, high_ref, w_ref, out_ref, stage
):
    below = jnp.concatenate([low_ref[...], high_ref[...]], 0)
    below = jnp.where(space_ref[0] == 0, jnp.zeros_like(below), below)
    prev = jnp.where(core_ref[0] == 0, below, beside_ref[...])
    input_rows(pre_grad_ref, prev, w_ref, out_ref, stage)


def input_rows(pre_grad_ref, prev, w_ref, out_ref, stage):
    cols, width = pre_grad_ref.shape
    pre_grad = pre_grad_ref[...]
    row_at = lax.broadcasted_iota(jnp.int32, (cols, width), 0)

    def planes(source, row_tap):
        even = dot(source, w_ref[3 * row_tap], 1, 1)
        odd = dot(source, w_ref[3 * row_tap + 1], 1, 1)
        late = pltpu.roll(dot(source, w_ref[3 * row_tap + 2], 1, 1), 1, 0)
        return even + jnp.where(row_at == 0, 0.0, late), odd

    def weave(row, even, odd):
        for lane in range(width // LANES):
            at = row * (width // LANES) + lane
            here = slice(lane * LANES, (lane + 1) * LANES)
            stage[at, pl.ds(0, cols, stride=2), :] = even[:, here]
            stage[at, pl.ds(1, cols, stride=2), :] = odd[:, here]
            out_ref[row, :, here] = stage[at].astype(bf16)

    even, odd = planes(pre_grad, 1)
    weave(1, even, odd)
    even, odd = planes(pre_grad, 0)
    even_rim, odd_rim = planes(prev, 2)
    weave(0, even + even_rim, odd + odd_rim)


def body(activations, conv_weight, conv_bias, head_weight, latent_grad, noise_sample):
    frames, double_rows, double_cols, channels = activations.shape
    cols = double_cols // 2
    latent_dim = latent_grad.shape[-1]
    spaces = lax.axis_size("space")
    times = lax.axis_size("tm")
    line = ("space", "col")
    peers = lax.axis_size(line)
    assert frames == 1 and double_rows == 2 and lax.axis_size("col") == 2
    share = channels // peers
    taps = conv_weight.reshape(9, channels, channels)
    tiles = jnp.transpose(latent_grad[0], (0, 2, 1))
    if share % TAIL or spaces != 4 or times != 2:
        return wide_body(activations, taps, conv_bias, head_weight, tiles, noise_sample)
    core_at = lax.axis_index("col").astype(jnp.int32).reshape(1)
    space_at = lax.axis_index("space").astype(jnp.int32).reshape(1)
    time_at = lax.axis_index("tm").astype(jnp.int32).reshape(1)
    swap = [(0, 1), (1, 0)]
    array = jax.ShapeDtypeStruct

    def over_space(pieces):
        return [
            lax.ppermute(pieces[k], "space", [(i, (i + k) % spaces) for i in range(spaces)])
            for k in range(1, spaces)
        ]

    tile = tiles.shape[1:]
    got_tiles = lax.ppermute(tiles, "col", swap)
    row, own_tiles = full_call(
        start_kernel,
        (array((double_cols, channels), bf16), array(tiles.shape, bf16)),
        [pltpu.SemaphoreType.DMA((2,))],
        0,
        1 << 19,
        "hh",
    )(activations[0], tiles)
    here, far, lower = full_call(
        tiles_kernel,
        (
            array((tile[0], LANES), bf16),
            array((tile[0], LANES), bf16),
            array((double_cols + tile[0], channels), bf16),
        ),
        [],
        0,
        1 << 18,
        "ssvvv",
    )(core_at, space_at, row, own_tiles, got_tiles)
    above = lax.ppermute(lower, line, [(i, (i - 1) % peers) for i in range(peers)])
    hops = [(2 * i + c, 2 * ((i + 1 + c) % spaces) + c) for i in range(spaces) for c in range(2)]
    far = lax.ppermute(far, line, hops)
    square = 2 * cols * channels * channels
    windows, early, w_here = full_call(
        early_kernel,
        (
            array((6, cols, channels), bf16),
            array((cols + 4 * latent_dim, channels), f32),
            array(taps.shape, bf16),
        ),
        [
            pltpu.VMEM((2, double_cols, channels), bf16),
            pltpu.VMEM((1, channels), f32),
            pltpu.VMEM((2 * latent_dim, channels), bf16),
            pltpu.VMEM((latent_dim, cols), bf16),
            pltpu.VMEM((2 * (channels // LANES), double_cols + 8, LANES), f32),
            pltpu.SemaphoreType.DMA((8,)),
        ],
        6 * square,
        5 << 20,
        "hhhhhv",
    )(
        activations[0],
        taps,
        conv_bias.reshape(1, channels),
        head_weight.T,
        jnp.transpose(noise_sample[0, 0]),
        here,
    )
    early, far, above = lax.optimization_barrier((early, far, above))
    rows_a = HALVED * share
    rows_b = (9 - HALVED) * share + TAIL
    half = channels // 2
    pre_act, last_windows, hidden, came = full_call(
        functools.partial(conv_kernel, spaces),
        (
            array((cols, channels), f32),
            array((3, cols, channels), bf16),
            array((cols, channels), bf16),
            array((2 * tile[0], LANES), bf16),
        ),
        [pltpu.VMEM((channels // LANES, double_cols + 8, LANES), f32)],
        3 * square,
        2 << 20,
        "ssvvvv",
    )(core_at, space_at, early, w_here, far, above)
    other_came = lax.ppermute(came, "col", swap)
    pre_grad, moment_grad = full_call(
        grad_kernel,
        (array((cols, channels), bf16), array((2 * latent_dim, cols), bf16)),
        [pltpu.VMEM((spaces, tile[0], 2 * tile[1]), bf16)],
        square,
        1 << 20,
        "ssvvvvv",
    )(core_at, space_at, early, pre_act, hidden, came, other_came)
    keep_a, send_a = full_call(
        early_terms_kernel,
        (
            array((spaces, rows_a, channels), f32),
            array((spaces, rows_a, channels), bf16),
        ),
        [],
        6 * square,
        2 << 20,
        "svv",
    )(core_at, windows, pre_grad)
    got_a = lax.ppermute(send_a, "col", swap)
    keep_b, send_b = full_call(
        frame_terms_kernel,
        (
            array((spaces, rows_b, channels), f32),
            array((spaces, rows_b + cols // spaces, channels), bf16),
        ),
        [],
        cols,
        cols,
        "svvvv",
    )(core_at, last_windows, pre_grad, hidden, moment_grad)
    got_b = lax.ppermute(send_b, "col", swap)
    own_a, cross_a = full_call(
        halve_kernel,
        (array((spaces, rows_a, half), f32), array((spaces, rows_a, half), bf16)),
        [],
        spaces * rows_a * channels,
        2 << 20,
        "svv",
    )(time_at, keep_a, got_a)
    crossed_a = lax.ppermute(cross_a, "tm", swap)
    half_grad = cols // 2
    *pieces_b, beside_grad = full_call(
        pair_rim_kernel,
        (
            *(
                array((rows_b + (half_grad if k == 1 else 0), channels), f32 if k == 0 else bf16)
                for k in range(spaces)
            ),
            array((cols, channels), bf16),
        ),
        [],
        spaces * rows_b * channels,
        1 << 20,
        "ssvvv",
    )(core_at, space_at, keep_b, got_b, pre_grad)
    far_b = over_space(pieces_b)
    pieces_a = full_call(
        pair_kernel,
        tuple(array((rows_a, half), f32 if k == 0 else bf16) for k in range(spaces)),
        [],
        spaces * rows_a * half,
        1 << 20,
        "svv",
    )(space_at, own_a, crossed_a)
    far_a = over_space(pieces_a)
    sum_b, high = full_call(
        line_rim_kernel,
        (array((rows_b, channels), bf16), array((half_grad, channels), bf16)),
        [],
        4 * rows_b * channels,
        1 << 19,
        "v" * spaces,
    )(pieces_b[0], *far_b)
    other_b = lax.ppermute(sum_b, "tm", swap)
    low = lax.ppermute(high, "col", swap)
    sum_a = full_call(
        line_kernel, array((rows_a, half), bf16), [], 4 * rows_a * half, 1 << 19, "v" * spaces
    )(pieces_a[0], *far_a)
    other_a = lax.ppermute(sum_a, "tm", swap)
    x_grad = full_call(
        input_chip_kernel,
        array((2, double_cols, channels), bf16),
        [pltpu.VMEM((2 * (channels // LANES), double_cols, LANES), f32)],
        9 * square,
        4 << 20,
        "ssvvvvv",
    )(core_at, space_at, pre_grad, beside_grad, low, high, taps)
    other_a, x_grad = lax.optimization_barrier((other_a, x_grad))
    positions = frames * times * peers * cols
    kernel_grad, head_grad, bias_grad = full_call(
        functools.partial(final_kernel, 1.0 / math.sqrt(positions)),
        (
            array((9, share, channels), f32),
            array((share, 2 * latent_dim), f32),
            array((1, share), f32),
        ),
        [],
        rows_a * half + rows_b * channels,
        1 << 20,
        "svvvv",
    )(time_at, sum_a, other_a, sum_b, other_b)
    return (
        x_grad[None],
        kernel_grad.reshape(3, 3, share, channels),
        head_grad,
        bias_grad.reshape(share),
    )


def input_gradient(pre_grad, prev, taps):
    cols, channels = pre_grad.shape
    return full_call(
        input_kernel,
        jax.ShapeDtypeStruct((2, 2 * cols, channels), bf16),
        [pltpu.VMEM((2 * (channels // LANES), 2 * cols, LANES), f32)],
        18 * cols * channels * channels,
        4 << 20,
        "vvv",
    )(pre_grad, prev, taps)


def wide_body(activations, taps, conv_bias, head_weight, tiles, noise_sample):
    _, _, double_cols, channels = activations.shape
    cols = double_cols // 2
    latent_dim = noise_sample.shape[-1]
    line = ("space", "col")
    peers = lax.axis_size(line)
    next_row = lax.ppermute(activations[0, 0], line, [(i, i - 1) for i in range(1, peers)])
    upstream = lax.all_to_all(tiles, line, split_axis=0, concat_axis=0, tiled=True)
    padded = jnp.pad(jnp.concatenate([activations[0], next_row[None]], 0), ((0, 0), (0, 1), (0, 0)))
    windows = [
        padded[index // 3, index % 3 : index % 3 + 2 * cols : 2] for index in range(9)
    ]
    pre_act = jnp.zeros((cols, channels), f32) + conv_bias
    for index in range(9):
        pre_act = pre_act + dot(windows[index], taps[index], 1, 0)
    gating = jax.nn.sigmoid(pre_act)
    hidden = (pre_act * gating).astype(bf16)
    moments = dot(hidden, head_weight, 1, 0)
    upstream = jnp.transpose(upstream, (0, 2, 1)).reshape(cols, latent_dim).astype(f32)
    spread = jnp.exp(0.5 * moments[:, latent_dim:])
    mean_grad = upstream + kl_weight * moments[:, :latent_dim]
    logvar_grad = 0.5 * upstream * noise_sample[0, 0].astype(f32) * spread
    logvar_grad = logvar_grad + 0.5 * kl_weight * (spread * spread - 1.0)
    moment_grad = jnp.concatenate([mean_grad, logvar_grad], 1).astype(bf16)
    hidden_grad = dot(moment_grad, head_weight, 1, 1)
    pre_grad = (hidden_grad * gating * (1.0 + pre_act * (1.0 - gating))).astype(bf16)
    prev = lax.ppermute(pre_grad, line, [(i, i + 1) for i in range(peers - 1)])
    x_grad = input_gradient(pre_grad, prev, taps)
    kernel_term = jnp.stack([dot(window, pre_grad, 0, 0) for window in windows], 1)
    terms = (
        kernel_term.reshape(channels, 9 * channels),
        dot(hidden, moment_grad, 0, 0),
        jnp.sum(pre_grad, axis=0, dtype=f32),
    )
    grad_scale = 1.0 / math.sqrt(lax.axis_size("tm") * peers * cols)
    shares = [
        lax.psum_scatter(lax.psum(term, "tm"), line, scatter_dimension=0, tiled=True) * grad_scale
        for term in terms
    ]
    kernel_grad = jnp.transpose(shares[0].reshape(-1, 3, 3, channels), (1, 2, 0, 3))
    return x_grad[None], kernel_grad, shares[1], shares[2]


def solution(mesh):
    in_specs = (
        P(("groups", "tm"), ("space", "col"), None, None),
        P(),
        P(),
        P(),
        P(("groups", "tm"), None, ("space", "col"), None),
        P(("groups", "tm"), ("space", "col"), None, None),
    )
    out_specs = (
        P(("groups", "tm"), ("space", "col"), None, None),
        P(None, None, ("groups", "space", "col"), None),
        P(("groups", "space", "col"), None),
        P(("groups", "space", "col")),
    )
    return jax.shard_map(body, mesh=mesh, in_specs=in_specs, out_specs=out_specs, check_vma=False)
```

```python
import functools
import math

import jax
import jax.numpy as jnp
from jax import lax
from jax.experimental import pallas as pl
from jax.experimental.pallas import tpu as pltpu
from jax.sharding import PartitionSpec as P

f32 = jnp.float32
bf16 = jnp.bfloat16
kl_weight = 1.0
LANES = 128
HALVED = 6
TAIL = 8


def dot(a, b, ca, cb):
    return lax.dot_general(a, b, (((ca,), (cb,)), ((), ())), preferred_element_type=f32)


def params():
    return pltpu.CompilerParams(vmem_limit_bytes=12 << 20)


SPACES = {"s": pltpu.SMEM, "v": pltpu.VMEM, "h": pltpu.HBM}


def full_call(kernel, out_shape, scratch, flops, moved, places):
    call = pl.pallas_call(
        kernel,
        out_shape=out_shape,
        in_specs=[pl.BlockSpec(memory_space=SPACES[place]) for place in places],
        out_specs=jax.tree.map(lambda _: pl.BlockSpec(memory_space=pltpu.VMEM), out_shape),
        scratch_shapes=scratch,
        compiler_params=params(),
        cost_estimate=pl.CostEstimate(flops=flops, bytes_accessed=moved, transcendentals=0),
    )

    def placed(*args):
        pinned = [
            pltpu.with_memory_space_constraint(arg, pltpu.HBM) if place == "h" else arg
            for arg, place in zip(args, places)
        ]
        return call(*pinned)

    return placed


def start_kernel(act_ref, tiles_in, row_ref, tiles_ref, sems):
    copies = [
        pltpu.make_async_copy(tiles_in, tiles_ref, sems.at[0]),
        pltpu.make_async_copy(act_ref.at[0], row_ref, sems.at[1]),
    ]
    for copy in copies:
        copy.start()
    for copy in copies:
        copy.wait()


def tiles_kernel(core_ref, space_ref, row_ref, own_ref, got_ref, here_ref, far_ref, down_ref):
    spaces = own_ref.shape[0] // 2
    height, width = own_ref.shape[1:]
    cols = row_ref.shape[0]
    core, chip = core_ref[0], space_ref[0]
    first = core == 0

    def side_by_side(at):
        mine, other = own_ref[at], got_ref[at]
        return [jnp.where(first, mine, other), jnp.where(first, other, mine)]

    def put(ref, top, pieces):
        used = width * len(pieces)
        if used < ref.shape[1]:
            pieces = [*pieces, jnp.zeros((height, ref.shape[1] - used), bf16)]
        ref[top:, :] = jnp.concatenate(pieces, 1)

    put(here_ref, 0, side_by_side(2 * chip + core))
    there = 2 * lax.rem(chip + 1 + core, spaces)
    put(far_ref, 0, side_by_side(there) + side_by_side(there + 1))
    down_ref[:cols, :] = row_ref[...]
    there = 2 * lax.rem(chip + spaces - 1, spaces)
    put(down_ref, cols, side_by_side(there) + side_by_side(there + 1))


def split_columns(row, source, stage):
    length, width = source.shape
    lanes = width // LANES
    source = source.astype(f32)
    for lane in range(lanes):
        stage[row * lanes + lane, :length, :] = source[:, lane * LANES : (lane + 1) * LANES]
        stage[row * lanes + lane, length:, :] = jnp.zeros((8, LANES), f32)
    windows = []
    for tap in range(3):
        halves = [
            stage[row * lanes + lane, pl.ds(tap, length // 2, stride=2), :]
            for lane in range(lanes)
        ]
        windows.append(jnp.concatenate(halves, 1).astype(bf16))
    return windows


def early_kernel(
    act_ref, w_in, bias_in, head_in, noise_in, here_ref,
    pre_act_ref, w_ref, act, bias, head, noise, stage, sems,
):
    pairs = [
        (act_ref.at[0], act.at[0]), (w_in.at[:3], w_ref.at[:3]),
        (act_ref.at[1], act.at[1]), (w_in.at[3:6], w_ref.at[3:6]),
        (bias_in, bias), (w_in.at[6:], w_ref.at[6:]), (head_in, head), (noise_in, noise),
    ]
    copies = [pltpu.make_async_copy(a, b, sems.at[i]) for i, (a, b) in enumerate(pairs)]
    for copy in copies:
        copy.start()
    copies[4].wait()
    cols = noise.shape[1]
    width = head.shape[1]
    pre_act = jnp.broadcast_to(bias[...], (cols, width))
    for row in range(2):
        copies[2 * row].wait()
        windows = split_columns(row, act[row], stage)
        copies[2 * row + 1].wait()
        for tap in range(3):
            pre_act = pre_act + dot(windows[tap], w_ref[3 * row + tap], 1, 0)
    pre_act_ref[:cols, :] = pre_act
    for copy in copies[5:]:
        copy.wait()
    at = cols
    for ref in (head, noise, here_ref):
        pre_act_ref[at : at + ref.shape[0], : ref.shape[1]] = ref[...].astype(f32)
        at += ref.shape[0]


def select_kernel(chips, core_ref, act_in, beside_ref, windows_ref, act, stage, sem):
    copy = pltpu.make_async_copy(act_in, act, sem)
    copy.start()
    rows, length, width = beside_ref.shape
    kept = windows_ref.shape[2]
    share = kept // chips
    source = lax.broadcasted_iota(jnp.int32, (width, kept), 0)
    target = lax.broadcasted_iota(jnp.int32, (width, kept), 1)
    wanted = 2 * share * (target // share) + share * core_ref[0] + target % share
    select = jnp.where(source == wanted, 1.0, 0.0).astype(bf16)
    copy.wait()
    cols = length // 2
    for row in range(rows):
        for at, ref in enumerate((act, beside_ref)):
            picked = dot(ref[row], select, 1, 0)
            windows = split_columns(rows * at + row, picked, stage)
            for tap in range(3):
                windows_ref[3 * row + tap, cols * at : cols * (at + 1), :] = windows[tap]


def conv_kernel(
    chips, core_ref, space_ref, early_ref, w_ref, far_ref, above_ref,
    pre_act_ref, windows_ref, hidden_ref, tiles_ref, stage,
):
    cols = hidden_ref.shape[0]
    height = far_ref.shape[0]
    lanes = far_ref.shape[1]
    last = (core_ref[0] == 1) & (space_ref[0] == chips - 1)
    row = above_ref[: 2 * cols, :]
    windows = split_columns(0, jnp.where(last, jnp.zeros_like(row), row), stage)
    tiles_ref[:height, :] = far_ref[...]
    tiles_ref[height:, :] = above_ref[2 * cols :, :lanes]
    pre_act = early_ref[:cols, :]
    for tap in range(3):
        windows_ref[tap] = windows[tap]
        pre_act = pre_act + dot(windows[tap], w_ref[6 + tap], 1, 0)
    pre_act_ref[...] = pre_act
    hidden_ref[...] = jax.nn.silu(pre_act).astype(bf16)


def grad_kernel(
    core_ref, space_ref, early_ref, pre_act_ref, hidden_ref, tiles_ref, other_tiles_ref,
    pre_grad_ref, moment_grad_ref, tiles_at,
):
    cols, width = pre_grad_ref.shape
    spaces, latent, lanes = tiles_at.shape
    head = early_ref[cols : cols + 2 * latent, :].astype(bf16)
    at = cols + 2 * latent
    sample = early_ref[at : at + latent, :cols]
    chip = space_ref[0]
    first = core_ref[0] == 0
    tiles_at[chip] = early_ref[at + latent : at + 2 * latent, :lanes].astype(bf16)
    mine, other = tiles_ref[...], other_tiles_ref[...]
    for there, both in (
        (spaces - 1, jnp.where(first, mine[:latent], other[:latent])),
        (spaces - 2, jnp.where(first, other[:latent], mine[:latent])),
        (1, jnp.where(first, other[latent:], mine[latent:])),
    ):
        band = jnp.where(first, both[:, :lanes], both[:, lanes:])
        tiles_at[lax.rem(chip + there, spaces)] = band
    pre_act = pre_act_ref[...]
    gating = jax.nn.sigmoid(pre_act)
    moments = dot(head, hidden_ref[...], 1, 1)
    mean_part = moments[:latent]
    logvar = moments[latent:]
    upstream = jnp.concatenate([tiles_at[i].astype(f32) for i in range(spaces)], 1)
    spread = jnp.exp(0.5 * logvar)
    mean_grad = upstream + kl_weight * mean_part
    logvar_grad = 0.5 * upstream * sample * spread + 0.5 * kl_weight * (spread * spread - 1.0)
    moment_grad = jnp.concatenate([mean_grad, logvar_grad], 0).astype(bf16)
    hidden_grad = dot(moment_grad, head, 0, 0)
    pre_grad = (hidden_grad * gating * (1.0 + pre_act * (1.0 - gating))).astype(bf16)
    pre_grad_ref[...] = pre_grad
    moment_grad_ref[...] = moment_grad


def put_shares(first, keep_ref, send_ref, at, term):
    spaces = keep_ref.shape[0]
    share = term.shape[0] // (2 * spaces)
    for s in range(spaces):
        row = 2 * share * s
        even, odd = term[row : row + share], term[row + share : row + 2 * share]
        keep_ref[s, at : at + share, :] = jnp.where(first, even, odd)
        send_ref[s, at : at + share, :] = jnp.where(first, odd, even).astype(bf16)


def frame_terms_kernel(
    core_ref, windows_ref, pre_grad_ref, hidden_ref, moment_grad_ref, keep_ref, send_ref
):
    cols, width = pre_grad_ref.shape
    spaces = keep_ref.shape[0]
    share = width // (2 * spaces)
    first = core_ref[0] == 0
    pre_grad = pre_grad_ref[...]
    taps = windows_ref.shape[0]
    for tap in range(taps):
        put_shares(first, keep_ref, send_ref, tap * share, dot(windows_ref[tap], pre_grad, 0, 0))
    head_term = dot(hidden_ref[...], moment_grad_ref[...], 0, 1)
    bias_term = dot(jnp.ones((TAIL, cols), bf16), pre_grad, 1, 0)

    def tail(row):
        pieces = [head_term[row + i : row + i + TAIL] for i in range(0, share, TAIL)]
        pieces.append(bias_term[:, row : row + share])
        used = sum(piece.shape[1] for piece in pieces)
        pieces.append(jnp.zeros((TAIL, width - used), f32))
        return jnp.concatenate(pieces, 1)

    tails = []
    for s in range(2 * spaces):
        tails.append(tail(share * s))
    put_shares(first, keep_ref, send_ref, taps * share, jnp.concatenate(tails, 0))


def chip_terms_kernel(
    time_ref, windows_ref, pre_grad_ref, beside_ref, own_ref, send_ref
):
    first = time_ref[0] == 0
    pre_grad = jnp.concatenate([pre_grad_ref[...], beside_ref[...]], 0)
    spaces, _, half = own_ref.shape
    share = windows_ref.shape[2] // spaces
    for index in range(HALVED):
        term = dot(windows_ref[index], pre_grad, 0, 0)
        low, high = term[:, :half], term[:, half:]
        mine = jnp.where(first, low, high)
        other = jnp.where(first, high, low).astype(bf16)
        here = slice(index * share, (index + 1) * share)
        for s in range(spaces):
            own_ref[s, here, :] = mine[s * share : (s + 1) * share]
            send_ref[s, here, :] = other[s * share : (s + 1) * share]


def pair_kernel(space_ref, keep_ref, got_ref, *outs):
    spaces = len(outs)
    for k, out in enumerate(outs):
        at = lax.rem(space_ref[0] + k, spaces)
        out[...] = (keep_ref[at] + got_ref[at].astype(f32)).astype(out.dtype)


def pair_rim_kernel(core_ref, space_ref, keep_ref, got_ref, mine_ref, beside_ref, *outs):
    spaces = len(outs)
    rows = keep_ref.shape[1]
    for k, out in enumerate(outs):
        at = lax.rem(space_ref[0] + k, spaces)
        out[:rows, :] = (keep_ref[at] + got_ref[at].astype(f32)).astype(out.dtype)
    half = mine_ref.shape[0] // 2
    first = core_ref[0] == 0
    outs[1][rows:, :] = jnp.where(first, beside_ref[half:, :], mine_ref[:half, :])


def line_kernel(own_ref, *refs):
    total = own_ref[...]
    for ref in refs[:-1]:
        total = total + ref[...].astype(f32)
    refs[-1][...] = total.astype(bf16)


def line_rim_kernel(own_ref, *refs):
    rows = own_ref.shape[0]
    total = own_ref[...]
    for ref in refs[:-2]:
        total = total + ref[:rows, :].astype(f32)
    refs[-2][...] = total.astype(bf16)
    refs[-1][...] = refs[0][rows:, :]


def final_kernel(
    scale, time_ref, a_ref, a_far_ref, b_ref, b_far_ref, kernel_ref, head_ref, bias_ref
):
    share, latents = head_ref.shape
    first = time_ref[0] == 0
    mine, far = a_ref[...].astype(f32) * scale, a_far_ref[...].astype(f32) * scale
    low, high = jnp.where(first, mine, far), jnp.where(first, far, mine)
    total = (b_ref[...].astype(f32) + b_far_ref[...].astype(f32)) * scale
    half = mine.shape[1]
    for index in range(HALVED):
        kernel_ref[index, :, :half] = low[index * share : (index + 1) * share]
        kernel_ref[index, :, half:] = high[index * share : (index + 1) * share]
    for index in range(HALVED, 9):
        at = (index - HALVED) * share
        kernel_ref[index] = total[at : at + share]
    tail = total[(9 - HALVED) * share :]
    for i in range(share // TAIL):
        head_ref[TAIL * i : TAIL * (i + 1), :] = tail[:, latents * i : latents * (i + 1)]
    at = latents * (share // TAIL)
    bias_ref[...] = tail[:1, at : at + share]


def input_kernel(pre_grad_ref, prev_ref, w_ref, out_ref, stage):
    input_rows(pre_grad_ref, prev_ref[...], w_ref, out_ref, stage)


def input_chip_kernel(
    core_ref, space_ref, pre_grad_ref, beside_ref, low_ref, high_ref, w_ref, out_ref, stage
):
    below = jnp.concatenate([low_ref[...], high_ref[...]], 0)
    below = jnp.where(space_ref[0] == 0, jnp.zeros_like(below), below)
    prev = jnp.where(core_ref[0] == 0, below, beside_ref[...])
    input_rows(pre_grad_ref, prev, w_ref, out_ref, stage)


def input_rows(pre_grad_ref, prev, w_ref, out_ref, stage):
    cols, width = pre_grad_ref.shape
    pre_grad = pre_grad_ref[...]
    row_at = lax.broadcasted_iota(jnp.int32, (cols, width), 0)

    def planes(source, row_tap):
        even = dot(source, w_ref[3 * row_tap], 1, 1)
        odd = dot(source, w_ref[3 * row_tap + 1], 1, 1)
        late = pltpu.roll(dot(source, w_ref[3 * row_tap + 2], 1, 1), 1, 0)
        return even + jnp.where(row_at == 0, 0.0, late), odd

    def weave(row, even, odd):
        for lane in range(width // LANES):
            at = row * (width // LANES) + lane
            here = slice(lane * LANES, (lane + 1) * LANES)
            stage[at, pl.ds(0, cols, stride=2), :] = even[:, here]
            stage[at, pl.ds(1, cols, stride=2), :] = odd[:, here]
            out_ref[row, :, here] = stage[at].astype(bf16)

    even, odd = planes(pre_grad, 1)
    weave(1, even, odd)
    even, odd = planes(pre_grad, 0)
    even_rim, odd_rim = planes(prev, 2)
    weave(0, even + even_rim, odd + odd_rim)


def body(activations, conv_weight, conv_bias, head_weight, latent_grad, noise_sample):
    frames, double_rows, double_cols, channels = activations.shape
    cols = double_cols // 2
    latent_dim = latent_grad.shape[-1]
    spaces = lax.axis_size("space")
    times = lax.axis_size("tm")
    line = ("space", "col")
    peers = lax.axis_size(line)
    assert frames == 1 and double_rows == 2 and lax.axis_size("col") == 2
    share = channels // peers
    taps = conv_weight.reshape(9, channels, channels)
    tiles = jnp.transpose(latent_grad[0], (0, 2, 1))
    if share % TAIL or spaces != 4 or times != 2:
        return wide_body(activations, taps, conv_bias, head_weight, tiles, noise_sample)
    core_at = lax.axis_index("col").astype(jnp.int32).reshape(1)
    space_at = lax.axis_index("space").astype(jnp.int32).reshape(1)
    time_at = lax.axis_index("tm").astype(jnp.int32).reshape(1)
    swap = [(0, 1), (1, 0)]
    array = jax.ShapeDtypeStruct

    def over_space(pieces):
        return [
            lax.ppermute(pieces[k], "space", [(i, (i + k) % spaces) for i in range(spaces)])
            for k in range(1, spaces)
        ]

    tile = tiles.shape[1:]
    got_tiles = lax.ppermute(tiles, "col", swap)
    row, own_tiles = full_call(
        start_kernel,
        (array((double_cols, channels), bf16), array(tiles.shape, bf16)),
        [pltpu.SemaphoreType.DMA((2,))],
        0,
        1 << 19,
        "hh",
    )(activations[0], tiles)
    here, far, lower = full_call(
        tiles_kernel,
        (
            array((tile[0], LANES), bf16),
            array((tile[0], LANES), bf16),
            array((double_cols + tile[0], channels), bf16),
        ),
        [],
        0,
        1 << 18,
        "ssvvv",
    )(core_at, space_at, row, own_tiles, got_tiles)
    late_rows, lower = lax.optimization_barrier((activations[0], lower))
    above = lax.ppermute(lower, line, [(i, (i - 1) % peers) for i in range(peers)])
    hops = [(2 * i + c, 2 * ((i + 1 + c) % spaces) + c) for i in range(spaces) for c in range(2)]
    far = lax.ppermute(far, line, hops)
    square = 2 * cols * channels * channels
    early, w_here = full_call(
        early_kernel,
        (
            array((cols + 4 * latent_dim, channels), f32),
            array(taps.shape, bf16),
        ),
        [
            pltpu.VMEM((2, double_cols, channels), bf16),
            pltpu.VMEM((1, channels), f32),
            pltpu.VMEM((2 * latent_dim, channels), bf16),
            pltpu.VMEM((latent_dim, cols), bf16),
            pltpu.VMEM((2 * (channels // LANES), double_cols + 8, LANES), f32),
            pltpu.SemaphoreType.DMA((8,)),
        ],
        120 * square,
        5 << 20,
        "hhhhhv",
    )(
        activations[0],
        taps,
        conv_bias.reshape(1, channels),
        head_weight.T,
        jnp.transpose(noise_sample[0, 0]),
        here,
    )
    beside = lax.ppermute(late_rows, "col", swap)
    chip_windows = full_call(
        functools.partial(select_kernel, spaces),
        array((6, 2 * cols, channels // 2), bf16),
        [
            pltpu.VMEM((2, double_cols, channels), bf16),
            pltpu.VMEM((4 * (channels // 2 // LANES), double_cols + 8, LANES), f32),
            pltpu.SemaphoreType.DMA,
        ],
        4 * square,
        2 << 20,
        "shv",
    )(core_at, activations[0], beside)
    early, chip_windows, far, above = lax.optimization_barrier((early, chip_windows, far, above))
    rows_a = HALVED * share
    rows_b = (9 - HALVED) * share + TAIL
    half = channels // 2
    pre_act, last_windows, hidden, came = full_call(
        functools.partial(conv_kernel, spaces),
        (
            array((cols, channels), f32),
            array((3, cols, channels), bf16),
            array((cols, channels), bf16),
            array((2 * tile[0], LANES), bf16),
        ),
        [pltpu.VMEM((channels // LANES, double_cols + 8, LANES), f32)],
        3 * square,
        2 << 20,
        "ssvvvv",
    )(core_at, space_at, early, w_here, far, above)
    other_came = lax.ppermute(came, "col", swap)
    pre_grad, moment_grad = full_call(
        grad_kernel,
        (array((cols, channels), bf16), array((2 * latent_dim, cols), bf16)),
        [pltpu.VMEM((spaces, tile[0], 2 * tile[1]), bf16)],
        square,
        1 << 20,
        "ssvvvvv",
    )(core_at, space_at, early, pre_act, hidden, came, other_came)
    beside_grad = lax.ppermute(pre_grad, "col", swap)
    keep_b, send_b = full_call(
        frame_terms_kernel,
        (
            array((spaces, rows_b, channels), f32),
            array((spaces, rows_b, channels), bf16),
        ),
        [],
        cols,
        cols,
        "svvvv",
    )(core_at, last_windows, pre_grad, hidden, moment_grad)
    got_b = lax.ppermute(send_b, "col", swap)
    own_a, cross_a = full_call(
        chip_terms_kernel,
        (array((spaces, rows_a, half), f32), array((spaces, rows_a, half), bf16)),
        [],
        6 * square,
        2 << 20,
        "svvv",
    )(time_at, chip_windows, pre_grad, beside_grad)
    crossed_a = lax.ppermute(cross_a, "tm", swap)
    half_grad = cols // 2
    pieces_b = full_call(
        pair_rim_kernel,
        tuple(
            array((rows_b + (half_grad if k == 1 else 0), channels), f32 if k == 0 else bf16)
            for k in range(spaces)
        ),
        [],
        spaces * rows_b * channels,
        1 << 20,
        "ssvvvv",
    )(core_at, space_at, keep_b, got_b, pre_grad, beside_grad)
    far_b = over_space(pieces_b)
    pieces_a = full_call(
        pair_kernel,
        tuple(array((rows_a, half), f32 if k == 0 else bf16) for k in range(spaces)),
        [],
        spaces * rows_a * half,
        1 << 20,
        "svv",
    )(space_at, own_a, crossed_a)
    far_a = over_space(pieces_a)
    sum_b, high = full_call(
        line_rim_kernel,
        (array((rows_b, channels), bf16), array((half_grad, channels), bf16)),
        [],
        4 * rows_b * channels,
        1 << 19,
        "v" * spaces,
    )(pieces_b[0], *far_b)
    other_b = lax.ppermute(sum_b, "tm", swap)
    low = lax.ppermute(high, "col", swap)
    sum_a = full_call(
        line_kernel, array((rows_a, half), bf16), [], 4 * rows_a * half, 1 << 19, "v" * spaces
    )(pieces_a[0], *far_a)
    other_a = lax.ppermute(sum_a, "tm", swap)
    x_grad = full_call(
        input_chip_kernel,
        array((2, double_cols, channels), bf16),
        [pltpu.VMEM((2 * (channels // LANES), double_cols, LANES), f32)],
        9 * square,
        4 << 20,
        "ssvvvvv",
    )(core_at, space_at, pre_grad, beside_grad, low, high, taps)
    other_a, x_grad = lax.optimization_barrier((other_a, x_grad))
    positions = frames * times * peers * cols
    kernel_grad, head_grad, bias_grad = full_call(
        functools.partial(final_kernel, 1.0 / math.sqrt(positions)),
        (
            array((9, share, channels), f32),
            array((share, 2 * latent_dim), f32),
            array((1, share), f32),
        ),
        [],
        rows_a * half + rows_b * channels,
        1 << 20,
        "svvvv",
    )(time_at, sum_a, other_a, sum_b, other_b)
    return (
        x_grad[None],
        kernel_grad.reshape(3, 3, share, channels),
        head_grad,
        bias_grad.reshape(share),
    )


def input_gradient(pre_grad, prev, taps):
    cols, channels = pre_grad.shape
    return full_call(
        input_kernel,
        jax.ShapeDtypeStruct((2, 2 * cols, channels), bf16),
        [pltpu.VMEM((2 * (channels // LANES), 2 * cols, LANES), f32)],
        18 * cols * channels * channels,
        4 << 20,
        "vvv",
    )(pre_grad, prev, taps)


def wide_body(activations, taps, conv_bias, head_weight, tiles, noise_sample):
    _, _, double_cols, channels = activations.shape
    cols = double_cols // 2
    latent_dim = noise_sample.shape[-1]
    line = ("space", "col")
    peers = lax.axis_size(line)
    next_row = lax.ppermute(activations[0, 0], line, [(i, i - 1) for i in range(1, peers)])
    upstream = lax.all_to_all(tiles, line, split_axis=0, concat_axis=0, tiled=True)
    padded = jnp.pad(jnp.concatenate([activations[0], next_row[None]], 0), ((0, 0), (0, 1), (0, 0)))
    windows = [
        padded[index // 3, index % 3 : index % 3 + 2 * cols : 2] for index in range(9)
    ]
    pre_act = jnp.zeros((cols, channels), f32) + conv_bias
    for index in range(9):
        pre_act = pre_act + dot(windows[index], taps[index], 1, 0)
    gating = jax.nn.sigmoid(pre_act)
    hidden = (pre_act * gating).astype(bf16)
    moments = dot(hidden, head_weight, 1, 0)
    upstream = jnp.transpose(upstream, (0, 2, 1)).reshape(cols, latent_dim).astype(f32)
    spread = jnp.exp(0.5 * moments[:, latent_dim:])
    mean_grad = upstream + kl_weight * moments[:, :latent_dim]
    logvar_grad = 0.5 * upstream * noise_sample[0, 0].astype(f32) * spread
    logvar_grad = logvar_grad + 0.5 * kl_weight * (spread * spread - 1.0)
    moment_grad = jnp.concatenate([mean_grad, logvar_grad], 1).astype(bf16)
    hidden_grad = dot(moment_grad, head_weight, 1, 1)
    pre_grad = (hidden_grad * gating * (1.0 + pre_act * (1.0 - gating))).astype(bf16)
    prev = lax.ppermute(pre_grad, line, [(i, i + 1) for i in range(peers - 1)])
    x_grad = input_gradient(pre_grad, prev, taps)
    kernel_term = jnp.stack([dot(window, pre_grad, 0, 0) for window in windows], 1)
    terms = (
        kernel_term.reshape(channels, 9 * channels),
        dot(hidden, moment_grad, 0, 0),
        jnp.sum(pre_grad, axis=0, dtype=f32),
    )
    grad_scale = 1.0 / math.sqrt(lax.axis_size("tm") * peers * cols)
    shares = [
        lax.psum_scatter(lax.psum(term, "tm"), line, scatter_dimension=0, tiled=True) * grad_scale
        for term in terms
    ]
    kernel_grad = jnp.transpose(shares[0].reshape(-1, 3, 3, channels), (1, 2, 0, 3))
    return x_grad[None], kernel_grad, shares[1], shares[2]


def solution(mesh):
    in_specs = (
        P(("groups", "tm"), ("space", "col"), None, None),
        P(),
        P(),
        P(),
        P(("groups", "tm"), None, ("space", "col"), None),
        P(("groups", "tm"), ("space", "col"), None, None),
    )
    out_specs = (
        P(("groups", "tm"), ("space", "col"), None, None),
        P(None, None, ("groups", "space", "col"), None),
        P(("groups", "space", "col"), None),
        P(("groups", "space", "col")),
    )
    return jax.shard_map(body, mesh=mesh, in_specs=in_specs, out_specs=out_specs, check_vma=False)
```

```python
import functools
import math

import jax
import jax.numpy as jnp
from jax import lax
from jax.experimental import pallas as pl
from jax.experimental.pallas import tpu as pltpu
from jax.sharding import PartitionSpec as P

f32 = jnp.float32
bf16 = jnp.bfloat16
kl_weight = 1.0
LANES = 128
HALVED = 6
TAIL = 8


def dot(a, b, ca, cb):
    return lax.dot_general(a, b, (((ca,), (cb,)), ((), ())), preferred_element_type=f32)


def params():
    return pltpu.CompilerParams(vmem_limit_bytes=12 << 20)


SPACES = {"s": pltpu.SMEM, "v": pltpu.VMEM, "h": pltpu.HBM}


def full_call(kernel, out_shape, scratch, flops, moved, places):
    call = pl.pallas_call(
        kernel,
        out_shape=out_shape,
        in_specs=[pl.BlockSpec(memory_space=SPACES[place]) for place in places],
        out_specs=jax.tree.map(lambda _: pl.BlockSpec(memory_space=pltpu.VMEM), out_shape),
        scratch_shapes=scratch,
        compiler_params=params(),
        cost_estimate=pl.CostEstimate(flops=flops, bytes_accessed=moved, transcendentals=0),
    )

    def placed(*args):
        pinned = [
            pltpu.with_memory_space_constraint(arg, pltpu.HBM) if place == "h" else arg
            for arg, place in zip(args, places)
        ]
        return call(*pinned)

    return placed


def start_kernel(act_ref, tiles_in, row_ref, tiles_ref, sems):
    copies = [pltpu.make_async_copy(tiles_in, tiles_ref, sems.at[0])]
    pieces = sems.shape[0] - 1
    length = row_ref.shape[0] // pieces
    for i in range(pieces):
        here = pl.ds(i * length, length)
        copies.append(
            pltpu.make_async_copy(act_ref.at[0, here], row_ref.at[here], sems.at[1 + i])
        )
    for copy in copies:
        copy.start()
    for copy in copies:
        copy.wait()


def tiles_kernel(core_ref, space_ref, own_ref, got_ref, here_ref, far_ref, before_ref):
    spaces = own_ref.shape[0] // 2
    height, width = own_ref.shape[1:]
    core, chip = core_ref[0], space_ref[0]
    first = core == 0

    def side_by_side(at):
        mine, other = own_ref[at], got_ref[at]
        return [jnp.where(first, mine, other), jnp.where(first, other, mine)]

    rest = [jnp.zeros((height, here_ref.shape[1] - 2 * width), bf16)]
    here_ref[...] = jnp.concatenate(side_by_side(2 * chip + core) + rest, 1)
    there = 2 * lax.rem(chip + 1 + core, spaces)
    far_ref[...] = jnp.concatenate(side_by_side(there) + side_by_side(there + 1), 1)
    there = 2 * lax.rem(chip + spaces - 1, spaces)
    before_ref[...] = jnp.concatenate(side_by_side(there) + side_by_side(there + 1), 1)


def join_kernel(far_ref, next_ref, out_ref):
    height = far_ref.shape[0]
    out_ref[:height, :] = far_ref[...]
    out_ref[height:, :] = next_ref[...]


def split_columns(row, source, stage):
    length, width = source.shape
    lanes = width // LANES
    source = source.astype(f32)
    for lane in range(lanes):
        stage[row * lanes + lane, :length, :] = source[:, lane * LANES : (lane + 1) * LANES]
        stage[row * lanes + lane, length:, :] = jnp.zeros((8, LANES), f32)
    windows = []
    for tap in range(3):
        halves = [
            stage[row * lanes + lane, pl.ds(tap, length // 2, stride=2), :]
            for lane in range(lanes)
        ]
        windows.append(jnp.concatenate(halves, 1).astype(bf16))
    return windows


def early_kernel(
    act_ref, w_in, bias_in, head_in, noise_in, here_ref, before_ref,
    pre_act_ref, w_ref, later_ref, act, bias, head, noise, stage, sems,
):
    pairs = [
        (act_ref.at[0], act.at[0]), (w_in.at[:3], w_ref.at[:3]),
        (act_ref.at[1], act.at[1]), (w_in.at[3:6], w_ref.at[3:6]),
        (bias_in, bias), (w_in.at[6:], w_ref.at[6:]), (head_in, head), (noise_in, noise),
    ]
    copies = [pltpu.make_async_copy(a, b, sems.at[i]) for i, (a, b) in enumerate(pairs)]
    for copy in copies:
        copy.start()
    later_ref[...] = before_ref[...]
    copies[4].wait()
    cols = noise.shape[1]
    width = head.shape[1]
    pre_act = jnp.broadcast_to(bias[...], (cols, width))
    for row in range(2):
        copies[2 * row].wait()
        windows = split_columns(row, act[row], stage)
        copies[2 * row + 1].wait()
        for tap in range(3):
            pre_act = pre_act + dot(windows[tap], w_ref[3 * row + tap], 1, 0)
    pre_act_ref[:cols, :] = pre_act
    for copy in copies[5:]:
        copy.wait()
    at = cols
    for ref in (head, noise, here_ref):
        pre_act_ref[at : at + ref.shape[0], : ref.shape[1]] = ref[...].astype(f32)
        at += ref.shape[0]


def select_kernel(chips, core_ref, act_in, beside_ref, windows_ref, act, stage, sem):
    copy = pltpu.make_async_copy(act_in, act, sem)
    copy.start()
    rows, length, width = beside_ref.shape
    kept = windows_ref.shape[2]
    share = kept // chips
    source = lax.broadcasted_iota(jnp.int32, (width, kept), 0)
    target = lax.broadcasted_iota(jnp.int32, (width, kept), 1)
    wanted = 2 * share * (target // share) + share * core_ref[0] + target % share
    select = jnp.where(source == wanted, 1.0, 0.0).astype(bf16)
    copy.wait()
    cols = length // 2
    for row in range(rows):
        for at, ref in enumerate((act, beside_ref)):
            picked = dot(ref[row], select, 1, 0)
            windows = split_columns(rows * at + row, picked, stage)
            for tap in range(3):
                windows_ref[3 * row + tap, cols * at : cols * (at + 1), :] = windows[tap]


def conv_kernel(
    chips, core_ref, space_ref, early_ref, w_ref, above_ref,
    pre_act_ref, windows_ref, hidden_ref, stage,
):
    cols = hidden_ref.shape[0]
    last = (core_ref[0] == 1) & (space_ref[0] == chips - 1)
    row = above_ref[...]
    windows = split_columns(0, jnp.where(last, jnp.zeros_like(row), row), stage)
    pre_act = early_ref[:cols, :]
    for tap in range(3):
        windows_ref[tap] = windows[tap]
        pre_act = pre_act + dot(windows[tap], w_ref[6 + tap], 1, 0)
    pre_act_ref[...] = pre_act
    hidden_ref[...] = jax.nn.silu(pre_act).astype(bf16)


def grad_kernel(
    core_ref, space_ref, early_ref, pre_act_ref, hidden_ref, tiles_ref, other_tiles_ref,
    pre_grad_ref, moment_grad_ref, tiles_at,
):
    cols, width = pre_grad_ref.shape
    spaces, latent, lanes = tiles_at.shape
    head = early_ref[cols : cols + 2 * latent, :].astype(bf16)
    at = cols + 2 * latent
    sample = early_ref[at : at + latent, :cols]
    chip = space_ref[0]
    first = core_ref[0] == 0
    tiles_at[chip] = early_ref[at + latent : at + 2 * latent, :lanes].astype(bf16)
    mine, other = tiles_ref[...], other_tiles_ref[...]
    for there, both in (
        (spaces - 1, jnp.where(first, mine[:latent], other[:latent])),
        (spaces - 2, jnp.where(first, other[:latent], mine[:latent])),
        (1, jnp.where(first, mine[latent:], other[latent:])),
    ):
        band = jnp.where(first, both[:, :lanes], both[:, lanes:])
        tiles_at[lax.rem(chip + there, spaces)] = band
    pre_act = pre_act_ref[...]
    gating = jax.nn.sigmoid(pre_act)
    moments = dot(head, hidden_ref[...], 1, 1)
    mean_part = moments[:latent]
    logvar = moments[latent:]
    upstream = jnp.concatenate([tiles_at[i].astype(f32) for i in range(spaces)], 1)
    spread = jnp.exp(0.5 * logvar)
    mean_grad = upstream + kl_weight * mean_part
    logvar_grad = 0.5 * upstream * sample * spread + 0.5 * kl_weight * (spread * spread - 1.0)
    moment_grad = jnp.concatenate([mean_grad, logvar_grad], 0).astype(bf16)
    hidden_grad = dot(moment_grad, head, 0, 0)
    pre_grad = (hidden_grad * gating * (1.0 + pre_act * (1.0 - gating))).astype(bf16)
    pre_grad_ref[...] = pre_grad
    moment_grad_ref[...] = moment_grad


def put_shares(first, keep_ref, send_ref, at, term):
    spaces = keep_ref.shape[0]
    share = term.shape[0] // (2 * spaces)
    for s in range(spaces):
        row = 2 * share * s
        even, odd = term[row : row + share], term[row + share : row + 2 * share]
        keep_ref[s, at : at + share, :] = jnp.where(first, even, odd)
        send_ref[s, at : at + share, :] = jnp.where(first, odd, even).astype(bf16)


def frame_terms_kernel(
    core_ref, windows_ref, pre_grad_ref, hidden_ref, moment_grad_ref, keep_ref, send_ref
):
    cols, width = pre_grad_ref.shape
    spaces = keep_ref.shape[0]
    share = width // (2 * spaces)
    first = core_ref[0] == 0
    pre_grad = pre_grad_ref[...]
    taps = windows_ref.shape[0]
    for tap in range(taps):
        put_shares(first, keep_ref, send_ref, tap * share, dot(windows_ref[tap], pre_grad, 0, 0))
    head_term = dot(hidden_ref[...], moment_grad_ref[...], 0, 1)
    bias_term = dot(jnp.ones((TAIL, cols), bf16), pre_grad, 1, 0)

    def tail(row):
        pieces = [head_term[row + i : row + i + TAIL] for i in range(0, share, TAIL)]
        pieces.append(bias_term[:, row : row + share])
        used = sum(piece.shape[1] for piece in pieces)
        pieces.append(jnp.zeros((TAIL, width - used), f32))
        return jnp.concatenate(pieces, 1)

    tails = []
    for s in range(2 * spaces):
        tails.append(tail(share * s))
    put_shares(first, keep_ref, send_ref, taps * share, jnp.concatenate(tails, 0))


def chip_terms_kernel(
    time_ref, windows_ref, pre_grad_ref, beside_ref, own_ref, send_ref
):
    first = time_ref[0] == 0
    pre_grad = jnp.concatenate([pre_grad_ref[...], beside_ref[...]], 0)
    spaces, _, half = own_ref.shape
    share = windows_ref.shape[2] // spaces
    for index in range(HALVED):
        term = dot(windows_ref[index], pre_grad, 0, 0)
        low, high = term[:, :half], term[:, half:]
        mine = jnp.where(first, low, high)
        other = jnp.where(first, high, low).astype(bf16)
        here = slice(index * share, (index + 1) * share)
        for s in range(spaces):
            own_ref[s, here, :] = mine[s * share : (s + 1) * share]
            send_ref[s, here, :] = other[s * share : (s + 1) * share]


def pair_kernel(space_ref, keep_ref, got_ref, *outs):
    spaces = len(outs)
    for k, out in enumerate(outs):
        at = lax.rem(space_ref[0] + k, spaces)
        out[...] = (keep_ref[at] + got_ref[at].astype(f32)).astype(out.dtype)


def pair_rim_kernel(core_ref, space_ref, keep_ref, got_ref, mine_ref, beside_ref, *outs):
    spaces = len(outs)
    rows = keep_ref.shape[1]
    for k, out in enumerate(outs):
        at = lax.rem(space_ref[0] + k, spaces)
        out[:rows, :] = (keep_ref[at] + got_ref[at].astype(f32)).astype(out.dtype)
    half = mine_ref.shape[0] // 2
    first = core_ref[0] == 0
    outs[1][rows:, :] = jnp.where(first, beside_ref[half:, :], mine_ref[:half, :])


def line_kernel(own_ref, *refs):
    total = own_ref[...]
    for ref in refs[:-1]:
        total = total + ref[...].astype(f32)
    refs[-1][...] = total.astype(bf16)


def line_rim_kernel(own_ref, *refs):
    rows = own_ref.shape[0]
    total = own_ref[...]
    for ref in refs[:-2]:
        total = total + ref[:rows, :].astype(f32)
    refs[-2][...] = total.astype(bf16)
    refs[-1][...] = refs[0][rows:, :]


def final_kernel(
    scale, time_ref, a_ref, a_far_ref, b_ref, b_far_ref, kernel_ref, head_ref, bias_ref
):
    share, latents = head_ref.shape
    first = time_ref[0] == 0
    mine, far = a_ref[...].astype(f32) * scale, a_far_ref[...].astype(f32) * scale
    low, high = jnp.where(first, mine, far), jnp.where(first, far, mine)
    total = (b_ref[...].astype(f32) + b_far_ref[...].astype(f32)) * scale
    half = mine.shape[1]
    for index in range(HALVED):
        kernel_ref[index, :, :half] = low[index * share : (index + 1) * share]
        kernel_ref[index, :, half:] = high[index * share : (index + 1) * share]
    for index in range(HALVED, 9):
        at = (index - HALVED) * share
        kernel_ref[index] = total[at : at + share]
    tail = total[(9 - HALVED) * share :]
    for i in range(share // TAIL):
        head_ref[TAIL * i : TAIL * (i + 1), :] = tail[:, latents * i : latents * (i + 1)]
    at = latents * (share // TAIL)
    bias_ref[...] = tail[:1, at : at + share]


def input_kernel(pre_grad_ref, prev_ref, w_ref, out_ref, stage):
    input_rows(pre_grad_ref, prev_ref[...], w_ref, out_ref, stage)


def input_chip_kernel(
    core_ref, space_ref, pre_grad_ref, beside_ref, low_ref, high_ref, w_ref, out_ref, stage
):
    below = jnp.concatenate([low_ref[...], high_ref[...]], 0)
    below = jnp.where(space_ref[0] == 0, jnp.zeros_like(below), below)
    prev = jnp.where(core_ref[0] == 0, below, beside_ref[...])
    input_rows(pre_grad_ref, prev, w_ref, out_ref, stage)


def input_rows(pre_grad_ref, prev, w_ref, out_ref, stage):
    cols, width = pre_grad_ref.shape
    pre_grad = pre_grad_ref[...]
    row_at = lax.broadcasted_iota(jnp.int32, (cols, width), 0)

    def planes(source, row_tap):
        even = dot(source, w_ref[3 * row_tap], 1, 1)
        odd = dot(source, w_ref[3 * row_tap + 1], 1, 1)
        late = pltpu.roll(dot(source, w_ref[3 * row_tap + 2], 1, 1), 1, 0)
        return even + jnp.where(row_at == 0, 0.0, late), odd

    def weave(row, even, odd):
        for lane in range(width // LANES):
            at = row * (width // LANES) + lane
            here = slice(lane * LANES, (lane + 1) * LANES)
            stage[at, pl.ds(0, cols, stride=2), :] = even[:, here]
            stage[at, pl.ds(1, cols, stride=2), :] = odd[:, here]
            out_ref[row, :, here] = stage[at].astype(bf16)

    even, odd = planes(pre_grad, 1)
    weave(1, even, odd)
    even, odd = planes(pre_grad, 0)
    even_rim, odd_rim = planes(prev, 2)
    weave(0, even + even_rim, odd + odd_rim)


def body(activations, conv_weight, conv_bias, head_weight, latent_grad, noise_sample):
    frames, double_rows, double_cols, channels = activations.shape
    cols = double_cols // 2
    latent_dim = latent_grad.shape[-1]
    spaces = lax.axis_size("space")
    times = lax.axis_size("tm")
    line = ("space", "col")
    peers = lax.axis_size(line)
    assert frames == 1 and double_rows == 2 and lax.axis_size("col") == 2
    share = channels // peers
    taps = conv_weight.reshape(9, channels, channels)
    tiles = jnp.transpose(latent_grad[0], (0, 2, 1))
    if share % TAIL or spaces != 4 or times != 2:
        return wide_body(activations, taps, conv_bias, head_weight, tiles, noise_sample)
    core_at = lax.axis_index("col").astype(jnp.int32).reshape(1)
    space_at = lax.axis_index("space").astype(jnp.int32).reshape(1)
    time_at = lax.axis_index("tm").astype(jnp.int32).reshape(1)
    swap = [(0, 1), (1, 0)]
    array = jax.ShapeDtypeStruct

    def over_space(pieces):
        return [
            lax.ppermute(pieces[k], "space", [(i, (i + k) % spaces) for i in range(spaces)])
            for k in range(1, spaces)
        ]

    tile = tiles.shape[1:]
    got_tiles = lax.ppermute(tiles, "col", swap)
    row, own_tiles = full_call(
        start_kernel,
        (array((double_cols, channels), bf16), array(tiles.shape, bf16)),
        [pltpu.SemaphoreType.DMA((9,))],
        0,
        1 << 19,
        "hh",
    )(activations[0], tiles)
    here, far, before = full_call(
        tiles_kernel, (array((tile[0], LANES), bf16),) * 3, [], 0, 1 << 16, "ssvv"
    )(core_at, space_at, own_tiles, got_tiles)
    late_rows, row, far = lax.optimization_barrier((activations[0], row, far))
    above = lax.ppermute(row, line, [(i, (i - 1) % peers) for i in range(peers)])
    hops = [(2 * i + c, 2 * ((i + 1 + c) % spaces) + c) for i in range(spaces) for c in range(2)]
    far = lax.ppermute(far, line, hops)
    square = 2 * cols * channels * channels
    early, w_here, before = full_call(
        early_kernel,
        (
            array((cols + 4 * latent_dim, channels), f32),
            array(taps.shape, bf16),
            array((tile[0], LANES), bf16),
        ),
        [
            pltpu.VMEM((2, double_cols, channels), bf16),
            pltpu.VMEM((1, channels), f32),
            pltpu.VMEM((2 * latent_dim, channels), bf16),
            pltpu.VMEM((latent_dim, cols), bf16),
            pltpu.VMEM((2 * (channels // LANES), double_cols + 8, LANES), f32),
            pltpu.SemaphoreType.DMA((8,)),
        ],
        120 * square,
        5 << 20,
        "hhhhhvv",
    )(
        activations[0],
        taps,
        conv_bias.reshape(1, channels),
        head_weight.T,
        jnp.transpose(noise_sample[0, 0]),
        here,
        before,
    )
    back = [(2 * i + 1, 2 * ((i - 1) % spaces)) for i in range(spaces)]
    after = lax.ppermute(before, line, back + [(2 * i, 2 * i + 1) for i in range(spaces)])
    beside = lax.ppermute(late_rows, "col", swap)
    chip_windows = full_call(
        functools.partial(select_kernel, spaces),
        array((6, 2 * cols, channels // 2), bf16),
        [
            pltpu.VMEM((2, double_cols, channels), bf16),
            pltpu.VMEM((4 * (channels // 2 // LANES), double_cols + 8, LANES), f32),
            pltpu.SemaphoreType.DMA,
        ],
        4 * square,
        2 << 20,
        "shv",
    )(core_at, activations[0], beside)
    early, chip_windows, far, after = lax.optimization_barrier((early, chip_windows, far, after))
    came = full_call(
        join_kernel, array((2 * tile[0], LANES), bf16), [], 0, 1 << 14, "vv"
    )(far, after)
    other_came = lax.ppermute(came, "col", swap)
    above, came = lax.optimization_barrier((above, came))
    rows_a = HALVED * share
    rows_b = (9 - HALVED) * share + TAIL
    half = channels // 2
    pre_act, last_windows, hidden = full_call(
        functools.partial(conv_kernel, spaces),
        (
            array((cols, channels), f32),
            array((3, cols, channels), bf16),
            array((cols, channels), bf16),
        ),
        [pltpu.VMEM((channels // LANES, double_cols + 8, LANES), f32)],
        3 * square,
        2 << 20,
        "ssvvv",
    )(core_at, space_at, early, w_here, above)
    pre_grad, moment_grad = full_call(
        grad_kernel,
        (array((cols, channels), bf16), array((2 * latent_dim, cols), bf16)),
        [pltpu.VMEM((spaces, tile[0], 2 * tile[1]), bf16)],
        square,
        1 << 20,
        "ssvvvvv",
    )(core_at, space_at, early, pre_act, hidden, came, other_came)
    beside_grad = lax.ppermute(pre_grad, "col", swap)
    keep_b, send_b = full_call(
        frame_terms_kernel,
        (
            array((spaces, rows_b, channels), f32),
            array((spaces, rows_b, channels), bf16),
        ),
        [],
        cols,
        cols,
        "svvvv",
    )(core_at, last_windows, pre_grad, hidden, moment_grad)
    got_b = lax.ppermute(send_b, "col", swap)
    own_a, cross_a = full_call(
        chip_terms_kernel,
        (array((spaces, rows_a, half), f32), array((spaces, rows_a, half), bf16)),
        [],
        6 * square,
        2 << 20,
        "svvv",
    )(time_at, chip_windows, pre_grad, beside_grad)
    crossed_a = lax.ppermute(cross_a, "tm", swap)
    half_grad = cols // 2
    pieces_b = full_call(
        pair_rim_kernel,
        tuple(
            array((rows_b + (half_grad if k == 1 else 0), channels), f32 if k == 0 else bf16)
            for k in range(spaces)
        ),
        [],
        spaces * rows_b * channels,
        1 << 20,
        "ssvvvv",
    )(core_at, space_at, keep_b, got_b, pre_grad, beside_grad)
    far_b = over_space(pieces_b)
    pieces_a = full_call(
        pair_kernel,
        tuple(array((rows_a, half), f32 if k == 0 else bf16) for k in range(spaces)),
        [],
        spaces * rows_a * half,
        1 << 20,
        "svv",
    )(space_at, own_a, crossed_a)
    far_a = over_space(pieces_a)
    sum_b, high = full_call(
        line_rim_kernel,
        (array((rows_b, channels), bf16), array((half_grad, channels), bf16)),
        [],
        4 * rows_b * channels,
        1 << 19,
        "v" * spaces,
    )(pieces_b[0], *far_b)
    other_b = lax.ppermute(sum_b, "tm", swap)
    low = lax.ppermute(high, "col", swap)
    sum_a = full_call(
        line_kernel, array((rows_a, half), bf16), [], 4 * rows_a * half, 1 << 19, "v" * spaces
    )(pieces_a[0], *far_a)
    other_a = lax.ppermute(sum_a, "tm", swap)
    x_grad = full_call(
        input_chip_kernel,
        array((2, double_cols, channels), bf16),
        [pltpu.VMEM((2 * (channels // LANES), double_cols, LANES), f32)],
        9 * square,
        4 << 20,
        "ssvvvvv",
    )(core_at, space_at, pre_grad, beside_grad, low, high, taps)
    other_a, x_grad = lax.optimization_barrier((other_a, x_grad))
    positions = frames * times * peers * cols
    kernel_grad, head_grad, bias_grad = full_call(
        functools.partial(final_kernel, 1.0 / math.sqrt(positions)),
        (
            array((9, share, channels), f32),
            array((share, 2 * latent_dim), f32),
            array((1, share), f32),
        ),
        [],
        rows_a * half + rows_b * channels,
        1 << 20,
        "svvvv",
    )(time_at, sum_a, other_a, sum_b, other_b)
    return (
        x_grad[None],
        kernel_grad.reshape(3, 3, share, channels),
        head_grad,
        bias_grad.reshape(share),
    )


def input_gradient(pre_grad, prev, taps):
    cols, channels = pre_grad.shape
    return full_call(
        input_kernel,
        jax.ShapeDtypeStruct((2, 2 * cols, channels), bf16),
        [pltpu.VMEM((2 * (channels // LANES), 2 * cols, LANES), f32)],
        18 * cols * channels * channels,
        4 << 20,
        "vvv",
    )(pre_grad, prev, taps)


def wide_body(activations, taps, conv_bias, head_weight, tiles, noise_sample):
    _, _, double_cols, channels = activations.shape
    cols = double_cols // 2
    latent_dim = noise_sample.shape[-1]
    line = ("space", "col")
    peers = lax.axis_size(line)
    next_row = lax.ppermute(activations[0, 0], line, [(i, i - 1) for i in range(1, peers)])
    upstream = lax.all_to_all(tiles, line, split_axis=0, concat_axis=0, tiled=True)
    padded = jnp.pad(jnp.concatenate([activations[0], next_row[None]], 0), ((0, 0), (0, 1), (0, 0)))
    windows = [
        padded[index // 3, index % 3 : index % 3 + 2 * cols : 2] for index in range(9)
    ]
    pre_act = jnp.zeros((cols, channels), f32) + conv_bias
    for index in range(9):
        pre_act = pre_act + dot(windows[index], taps[index], 1, 0)
    gating = jax.nn.sigmoid(pre_act)
    hidden = (pre_act * gating).astype(bf16)
    moments = dot(hidden, head_weight, 1, 0)
    upstream = jnp.transpose(upstream, (0, 2, 1)).reshape(cols, latent_dim).astype(f32)
    spread = jnp.exp(0.5 * moments[:, latent_dim:])
    mean_grad = upstream + kl_weight * moments[:, :latent_dim]
    logvar_grad = 0.5 * upstream * noise_sample[0, 0].astype(f32) * spread
    logvar_grad = logvar_grad + 0.5 * kl_weight * (spread * spread - 1.0)
    moment_grad = jnp.concatenate([mean_grad, logvar_grad], 1).astype(bf16)
    hidden_grad = dot(moment_grad, head_weight, 1, 1)
    pre_grad = (hidden_grad * gating * (1.0 + pre_act * (1.0 - gating))).astype(bf16)
    prev = lax.ppermute(pre_grad, line, [(i, i + 1) for i in range(peers - 1)])
    x_grad = input_gradient(pre_grad, prev, taps)
    kernel_term = jnp.stack([dot(window, pre_grad, 0, 0) for window in windows], 1)
    terms = (
        kernel_term.reshape(channels, 9 * channels),
        dot(hidden, moment_grad, 0, 0),
        jnp.sum(pre_grad, axis=0, dtype=f32),
    )
    grad_scale = 1.0 / math.sqrt(lax.axis_size("tm") * peers * cols)
    shares = [
        lax.psum_scatter(lax.psum(term, "tm"), line, scatter_dimension=0, tiled=True) * grad_scale
        for term in terms
    ]
    kernel_grad = jnp.transpose(shares[0].reshape(-1, 3, 3, channels), (1, 2, 0, 3))
    return x_grad[None], kernel_grad, shares[1], shares[2]


def solution(mesh):
    in_specs = (
        P(("groups", "tm"), ("space", "col"), None, None),
        P(),
        P(),
        P(),
        P(("groups", "tm"), None, ("space", "col"), None),
        P(("groups", "tm"), ("space", "col"), None, None),
    )
    out_specs = (
        P(("groups", "tm"), ("space", "col"), None, None),
        P(None, None, ("groups", "space", "col"), None),
        P(("groups", "space", "col"), None),
        P(("groups", "space", "col")),
    )
    return jax.shard_map(body, mesh=mesh, in_specs=in_specs, out_specs=out_specs, check_vma=False)
```

```python
import functools
import math

import jax
import jax.numpy as jnp
from jax import lax
from jax.experimental import pallas as pl
from jax.experimental.pallas import tpu as pltpu
from jax.sharding import PartitionSpec as P

f32 = jnp.float32
bf16 = jnp.bfloat16
kl_weight = 1.0
LANES = 128
HALVED = 6
TAIL = 8


def dot(a, b, ca, cb):
    return lax.dot_general(a, b, (((ca,), (cb,)), ((), ())), preferred_element_type=f32)


def params():
    return pltpu.CompilerParams(vmem_limit_bytes=12 << 20)


SPACES = {"s": pltpu.SMEM, "v": pltpu.VMEM, "h": pltpu.HBM}


def full_call(kernel, out_shape, scratch, flops, moved, places):
    call = pl.pallas_call(
        kernel,
        out_shape=out_shape,
        in_specs=[pl.BlockSpec(memory_space=SPACES[place]) for place in places],
        out_specs=jax.tree.map(lambda _: pl.BlockSpec(memory_space=pltpu.VMEM), out_shape),
        scratch_shapes=scratch,
        compiler_params=params(),
        cost_estimate=pl.CostEstimate(flops=flops, bytes_accessed=moved, transcendentals=0),
    )

    def placed(*args):
        pinned = [
            pltpu.with_memory_space_constraint(arg, pltpu.HBM) if place == "h" else arg
            for arg, place in zip(args, places)
        ]
        return call(*pinned)

    return placed


def start_kernel(act_ref, tiles_in, row_ref, tiles_ref, sems):
    copies = [pltpu.make_async_copy(tiles_in, tiles_ref, sems.at[0])]
    pieces = sems.shape[0] - 1
    length = row_ref.shape[0] // pieces
    for i in range(pieces):
        here = pl.ds(i * length, length)
        copies.append(
            pltpu.make_async_copy(act_ref.at[0, here], row_ref.at[here], sems.at[1 + i])
        )
    for copy in copies:
        copy.start()
    for copy in copies:
        copy.wait()


def tiles_kernel(core_ref, space_ref, own_ref, got_ref, here_ref, far_ref, before_ref):
    spaces = own_ref.shape[0] // 2
    height, width = own_ref.shape[1:]
    core, chip = core_ref[0], space_ref[0]
    first = core == 0

    def side_by_side(at):
        mine, other = own_ref[at], got_ref[at]
        return [jnp.where(first, mine, other), jnp.where(first, other, mine)]

    rest = [jnp.zeros((height, here_ref.shape[1] - 2 * width), bf16)]
    here_ref[...] = jnp.concatenate(side_by_side(2 * chip + core) + rest, 1)
    there = 2 * lax.rem(chip + 1 + core, spaces)
    far_ref[...] = jnp.concatenate(side_by_side(there) + side_by_side(there + 1), 1)
    there = 2 * lax.rem(chip + spaces - 1, spaces)
    before_ref[...] = jnp.concatenate(side_by_side(there) + side_by_side(there + 1), 1)


def join_kernel(far_ref, next_ref, out_ref):
    height = far_ref.shape[0]
    out_ref[:height, :] = far_ref[...]
    out_ref[height:, :] = next_ref[...]


def split_columns(row, source, stage):
    length, width = source.shape
    lanes = width // LANES
    source = source.astype(f32)
    for lane in range(lanes):
        stage[row * lanes + lane, :length, :] = source[:, lane * LANES : (lane + 1) * LANES]
        stage[row * lanes + lane, length:, :] = jnp.zeros((8, LANES), f32)
    windows = []
    for tap in range(3):
        halves = [
            stage[row * lanes + lane, pl.ds(tap, length // 2, stride=2), :]
            for lane in range(lanes)
        ]
        windows.append(jnp.concatenate(halves, 1).astype(bf16))
    return windows


def load_kernel(act_in, before_ref, act_ref, later_ref, sems):
    rows = act_in.shape[0]
    copies = [
        pltpu.make_async_copy(act_in.at[i], act_ref.at[i], sems.at[i]) for i in range(rows)
    ]
    for copy in copies:
        copy.start()
    later_ref[...] = before_ref[...]
    for copy in copies:
        copy.wait()


def early_kernel(
    bias_in, head_in, noise_in, w_in, act_ref, here_ref,
    pre_act_ref, w_ref, bias, head, noise, stage, sems,
):
    pairs = [(w_in.at[i : i + 3], w_ref.at[i : i + 3]) for i in (0, 3, 6)]
    pairs += [(bias_in, bias), (head_in, head), (noise_in, noise)]
    copies = [pltpu.make_async_copy(a, b, sems.at[i]) for i, (a, b) in enumerate(pairs)]
    for copy in copies:
        copy.start()
    cols = noise.shape[1]
    pre_act = None
    for row in range(2):
        windows = split_columns(row, act_ref[row], stage)
        copies[row].wait()
        for tap in range(3):
            term = dot(windows[tap], w_ref[3 * row + tap], 1, 0)
            pre_act = term if pre_act is None else pre_act + term
    for copy in copies[2:]:
        copy.wait()
    pre_act_ref[:cols, :] = pre_act + bias[...]
    at = cols
    for ref in (head, noise, here_ref):
        pre_act_ref[at : at + ref.shape[0], : ref.shape[1]] = ref[...].astype(f32)
        at += ref.shape[0]


def select_kernel(chips, core_ref, act_ref, beside_ref, windows_ref, stage):
    rows, length, width = beside_ref.shape
    kept = windows_ref.shape[2]
    share = kept // chips
    source = lax.broadcasted_iota(jnp.int32, (width, kept), 0)
    target = lax.broadcasted_iota(jnp.int32, (width, kept), 1)
    wanted = 2 * share * (target // share) + share * core_ref[0] + target % share
    select = jnp.where(source == wanted, 1.0, 0.0).astype(bf16)
    cols = length // 2
    for row in range(rows):
        for at, ref in enumerate((act_ref, beside_ref)):
            picked = dot(ref[row], select, 1, 0)
            windows = split_columns(rows * at + row, picked, stage)
            for tap in range(3):
                windows_ref[3 * row + tap, cols * at : cols * (at + 1), :] = windows[tap]


def conv_kernel(
    chips, core_ref, space_ref, early_ref, w_ref, above_ref,
    pre_act_ref, windows_ref, hidden_ref, stage,
):
    cols = hidden_ref.shape[0]
    last = (core_ref[0] == 1) & (space_ref[0] == chips - 1)
    row = above_ref[...]
    windows = split_columns(0, jnp.where(last, jnp.zeros_like(row), row), stage)
    pre_act = early_ref[:cols, :]
    for tap in range(3):
        windows_ref[tap] = windows[tap]
        pre_act = pre_act + dot(windows[tap], w_ref[6 + tap], 1, 0)
    pre_act_ref[...] = pre_act
    hidden_ref[...] = jax.nn.silu(pre_act).astype(bf16)


def grad_kernel(
    core_ref, space_ref, early_ref, pre_act_ref, hidden_ref, tiles_ref, other_tiles_ref,
    pre_grad_ref, moment_grad_ref, tiles_at,
):
    cols, width = pre_grad_ref.shape
    spaces, latent, lanes = tiles_at.shape
    head = early_ref[cols : cols + 2 * latent, :].astype(bf16)
    at = cols + 2 * latent
    sample = early_ref[at : at + latent, :cols]
    chip = space_ref[0]
    first = core_ref[0] == 0
    tiles_at[chip] = early_ref[at + latent : at + 2 * latent, :lanes].astype(bf16)
    mine, other = tiles_ref[...], other_tiles_ref[...]
    for there, both in (
        (spaces - 1, jnp.where(first, mine[:latent], other[:latent])),
        (spaces - 2, jnp.where(first, other[:latent], mine[:latent])),
        (1, jnp.where(first, mine[latent:], other[latent:])),
    ):
        band = jnp.where(first, both[:, :lanes], both[:, lanes:])
        tiles_at[lax.rem(chip + there, spaces)] = band
    pre_act = pre_act_ref[...]
    gating = jax.nn.sigmoid(pre_act)
    moments = dot(head, hidden_ref[...], 1, 1)
    mean_part = moments[:latent]
    logvar = moments[latent:]
    upstream = jnp.concatenate([tiles_at[i].astype(f32) for i in range(spaces)], 1)
    spread = jnp.exp(0.5 * logvar)
    mean_grad = upstream + kl_weight * mean_part
    logvar_grad = 0.5 * upstream * sample * spread + 0.5 * kl_weight * (spread * spread - 1.0)
    moment_grad = jnp.concatenate([mean_grad, logvar_grad], 0).astype(bf16)
    hidden_grad = dot(moment_grad, head, 0, 0)
    pre_grad = (hidden_grad * gating * (1.0 + pre_act * (1.0 - gating))).astype(bf16)
    pre_grad_ref[...] = pre_grad
    moment_grad_ref[...] = moment_grad


def put_shares(first, keep_ref, send_ref, at, term):
    spaces = keep_ref.shape[0]
    share = term.shape[0] // (2 * spaces)
    for s in range(spaces):
        row = 2 * share * s
        even, odd = term[row : row + share], term[row + share : row + 2 * share]
        keep_ref[s, at : at + share, :] = jnp.where(first, even, odd)
        send_ref[s, at : at + share, :] = jnp.where(first, odd, even).astype(bf16)


def frame_terms_kernel(
    core_ref, windows_ref, pre_grad_ref, hidden_ref, moment_grad_ref, keep_ref, send_ref
):
    cols, width = pre_grad_ref.shape
    spaces = keep_ref.shape[0]
    share = width // (2 * spaces)
    first = core_ref[0] == 0
    pre_grad = pre_grad_ref[...]
    taps = windows_ref.shape[0]
    for tap in range(taps):
        put_shares(first, keep_ref, send_ref, tap * share, dot(windows_ref[tap], pre_grad, 0, 0))
    head_term = dot(hidden_ref[...], moment_grad_ref[...], 0, 1)
    bias_term = dot(jnp.ones((TAIL, cols), bf16), pre_grad, 1, 0)

    def tail(row):
        pieces = [head_term[row + i : row + i + TAIL] for i in range(0, share, TAIL)]
        pieces.append(bias_term[:, row : row + share])
        used = sum(piece.shape[1] for piece in pieces)
        pieces.append(jnp.zeros((TAIL, width - used), f32))
        return jnp.concatenate(pieces, 1)

    tails = []
    for s in range(2 * spaces):
        tails.append(tail(share * s))
    put_shares(first, keep_ref, send_ref, taps * share, jnp.concatenate(tails, 0))


def chip_terms_kernel(
    time_ref, windows_ref, pre_grad_ref, beside_ref, own_ref, send_ref
):
    first = time_ref[0] == 0
    pre_grad = jnp.concatenate([pre_grad_ref[...], beside_ref[...]], 0)
    spaces, _, half = own_ref.shape
    share = windows_ref.shape[2] // spaces
    for index in range(HALVED):
        term = dot(windows_ref[index], pre_grad, 0, 0)
        low, high = term[:, :half], term[:, half:]
        mine = jnp.where(first, low, high)
        other = jnp.where(first, high, low).astype(bf16)
        here = slice(index * share, (index + 1) * share)
        for s in range(spaces):
            own_ref[s, here, :] = mine[s * share : (s + 1) * share]
            send_ref[s, here, :] = other[s * share : (s + 1) * share]


def pair_kernel(space_ref, keep_ref, got_ref, *outs):
    spaces = len(outs)
    for k, out in enumerate(outs):
        at = lax.rem(space_ref[0] + k, spaces)
        out[...] = (keep_ref[at] + got_ref[at].astype(f32)).astype(out.dtype)


def pair_rim_kernel(core_ref, space_ref, keep_ref, got_ref, mine_ref, beside_ref, *outs):
    spaces = len(outs)
    rows = keep_ref.shape[1]
    for k, out in enumerate(outs):
        at = lax.rem(space_ref[0] + k, spaces)
        out[:rows, :] = (keep_ref[at] + got_ref[at].astype(f32)).astype(out.dtype)
    half = mine_ref.shape[0] // 2
    first = core_ref[0] == 0
    outs[1][rows:, :] = jnp.where(first, beside_ref[half:, :], mine_ref[:half, :])


def line_kernel(own_ref, *refs):
    total = own_ref[...]
    for ref in refs[:-1]:
        total = total + ref[...].astype(f32)
    refs[-1][...] = total.astype(bf16)


def line_rim_kernel(own_ref, *refs):
    rows = own_ref.shape[0]
    total = own_ref[...]
    for ref in refs[:-2]:
        total = total + ref[:rows, :].astype(f32)
    refs[-2][...] = total.astype(bf16)
    refs[-1][...] = refs[0][rows:, :]


def final_kernel(
    scale, time_ref, a_ref, a_far_ref, b_ref, b_far_ref, kernel_ref, head_ref, bias_ref
):
    share, latents = head_ref.shape
    first = time_ref[0] == 0
    mine, far = a_ref[...].astype(f32) * scale, a_far_ref[...].astype(f32) * scale
    low, high = jnp.where(first, mine, far), jnp.where(first, far, mine)
    total = (b_ref[...].astype(f32) + b_far_ref[...].astype(f32)) * scale
    half = mine.shape[1]
    for index in range(HALVED):
        kernel_ref[index, :, :half] = low[index * share : (index + 1) * share]
        kernel_ref[index, :, half:] = high[index * share : (index + 1) * share]
    for index in range(HALVED, 9):
        at = (index - HALVED) * share
        kernel_ref[index] = total[at : at + share]
    tail = total[(9 - HALVED) * share :]
    for i in range(share // TAIL):
        head_ref[TAIL * i : TAIL * (i + 1), :] = tail[:, latents * i : latents * (i + 1)]
    at = latents * (share // TAIL)
    bias_ref[...] = tail[:1, at : at + share]


def input_kernel(pre_grad_ref, prev_ref, w_ref, out_ref, stage):
    input_rows(pre_grad_ref, prev_ref[...], w_ref, out_ref, stage)


def input_chip_kernel(
    core_ref, space_ref, pre_grad_ref, beside_ref, low_ref, high_ref, w_ref, out_ref, stage
):
    below = jnp.concatenate([low_ref[...], high_ref[...]], 0)
    below = jnp.where(space_ref[0] == 0, jnp.zeros_like(below), below)
    prev = jnp.where(core_ref[0] == 0, below, beside_ref[...])
    input_rows(pre_grad_ref, prev, w_ref, out_ref, stage)


def input_rows(pre_grad_ref, prev, w_ref, out_ref, stage):
    cols, width = pre_grad_ref.shape
    pre_grad = pre_grad_ref[...]
    row_at = lax.broadcasted_iota(jnp.int32, (cols, width), 0)

    def planes(source, row_tap):
        even = dot(source, w_ref[3 * row_tap], 1, 1)
        odd = dot(source, w_ref[3 * row_tap + 1], 1, 1)
        late = pltpu.roll(dot(source, w_ref[3 * row_tap + 2], 1, 1), 1, 0)
        return even + jnp.where(row_at == 0, 0.0, late), odd

    def weave(row, even, odd):
        for lane in range(width // LANES):
            at = row * (width // LANES) + lane
            here = slice(lane * LANES, (lane + 1) * LANES)
            stage[at, pl.ds(0, cols, stride=2), :] = even[:, here]
            stage[at, pl.ds(1, cols, stride=2), :] = odd[:, here]
            out_ref[row, :, here] = stage[at].astype(bf16)

    even, odd = planes(pre_grad, 1)
    weave(1, even, odd)
    even, odd = planes(pre_grad, 0)
    even_rim, odd_rim = planes(prev, 2)
    weave(0, even + even_rim, odd + odd_rim)


def body(activations, conv_weight, conv_bias, head_weight, latent_grad, noise_sample):
    frames, double_rows, double_cols, channels = activations.shape
    cols = double_cols // 2
    latent_dim = latent_grad.shape[-1]
    spaces = lax.axis_size("space")
    times = lax.axis_size("tm")
    line = ("space", "col")
    peers = lax.axis_size(line)
    assert frames == 1 and double_rows == 2 and lax.axis_size("col") == 2
    share = channels // peers
    taps = conv_weight.reshape(9, channels, channels)
    tiles = jnp.transpose(latent_grad[0], (0, 2, 1))
    if share % TAIL or spaces != 4 or times != 2:
        return wide_body(activations, taps, conv_bias, head_weight, tiles, noise_sample)
    core_at = lax.axis_index("col").astype(jnp.int32).reshape(1)
    space_at = lax.axis_index("space").astype(jnp.int32).reshape(1)
    time_at = lax.axis_index("tm").astype(jnp.int32).reshape(1)
    swap = [(0, 1), (1, 0)]
    array = jax.ShapeDtypeStruct

    def over_space(pieces):
        return [
            lax.ppermute(pieces[k], "space", [(i, (i + k) % spaces) for i in range(spaces)])
            for k in range(1, spaces)
        ]

    tile = tiles.shape[1:]
    got_tiles = lax.ppermute(tiles, "col", swap)
    row, own_tiles = full_call(
        start_kernel,
        (array((double_cols, channels), bf16), array(tiles.shape, bf16)),
        [pltpu.SemaphoreType.DMA((9,))],
        0,
        1 << 19,
        "hh",
    )(activations[0], tiles)
    here, far, before = full_call(
        tiles_kernel, (array((tile[0], LANES), bf16),) * 3, [], 0, 1 << 16, "ssvv"
    )(core_at, space_at, own_tiles, got_tiles)
    late_rows, row, far = lax.optimization_barrier((activations[0], row, far))
    above = lax.ppermute(row, line, [(i, (i - 1) % peers) for i in range(peers)])
    hops = [(2 * i + c, 2 * ((i + 1 + c) % spaces) + c) for i in range(spaces) for c in range(2)]
    far = lax.ppermute(far, line, hops)
    square = 2 * cols * channels * channels
    act_here, before = full_call(
        load_kernel,
        (
            array((double_rows, double_cols, channels), bf16),
            array((tile[0], LANES), bf16),
        ),
        [pltpu.SemaphoreType.DMA((double_rows,))],
        60 * square,
        2 << 20,
        "hv",
    )(activations[0], before)
    early, w_here = full_call(
        early_kernel,
        (array((cols + 4 * latent_dim, channels), f32), array(taps.shape, bf16)),
        [
            pltpu.VMEM((1, channels), f32),
            pltpu.VMEM((2 * latent_dim, channels), bf16),
            pltpu.VMEM((latent_dim, cols), bf16),
            pltpu.VMEM((2 * (channels // LANES), double_cols + 8, LANES), f32),
            pltpu.SemaphoreType.DMA((6,)),
        ],
        60 * square,
        3 << 20,
        "hhhhvv",
    )(
        conv_bias.reshape(1, channels),
        head_weight.T,
        jnp.transpose(noise_sample[0, 0]),
        taps,
        act_here,
        here,
    )
    back = [(2 * i + 1, 2 * ((i - 1) % spaces)) for i in range(spaces)]
    after = lax.ppermute(before, line, back + [(2 * i, 2 * i + 1) for i in range(spaces)])
    beside = lax.ppermute(late_rows, "col", swap)
    chip_windows = full_call(
        functools.partial(select_kernel, spaces),
        array((6, 2 * cols, channels // 2), bf16),
        [pltpu.VMEM((4 * (channels // 2 // LANES), double_cols + 8, LANES), f32)],
        4 * square,
        2 << 20,
        "svv",
    )(core_at, act_here, beside)
    early, chip_windows, far, after = lax.optimization_barrier((early, chip_windows, far, after))
    came = full_call(
        join_kernel, array((2 * tile[0], LANES), bf16), [], 0, 1 << 14, "vv"
    )(far, after)
    other_came = lax.ppermute(came, "col", swap)
    above, came = lax.optimization_barrier((above, came))
    rows_a = HALVED * share
    rows_b = (9 - HALVED) * share + TAIL
    half = channels // 2
    pre_act, last_windows, hidden = full_call(
        functools.partial(conv_kernel, spaces),
        (
            array((cols, channels), f32),
            array((3, cols, channels), bf16),
            array((cols, channels), bf16),
        ),
        [pltpu.VMEM((channels // LANES, double_cols + 8, LANES), f32)],
        3 * square,
        2 << 20,
        "ssvvv",
    )(core_at, space_at, early, w_here, above)
    pre_grad, moment_grad = full_call(
        grad_kernel,
        (array((cols, channels), bf16), array((2 * latent_dim, cols), bf16)),
        [pltpu.VMEM((spaces, tile[0], 2 * tile[1]), bf16)],
        square,
        1 << 20,
        "ssvvvvv",
    )(core_at, space_at, early, pre_act, hidden, came, other_came)
    beside_grad = lax.ppermute(pre_grad, "col", swap)
    keep_b, send_b = full_call(
        frame_terms_kernel,
        (
            array((spaces, rows_b, channels), f32),
            array((spaces, rows_b, channels), bf16),
        ),
        [],
        cols,
        cols,
        "svvvv",
    )(core_at, last_windows, pre_grad, hidden, moment_grad)
    got_b = lax.ppermute(send_b, "col", swap)
    own_a, cross_a = full_call(
        chip_terms_kernel,
        (array((spaces, rows_a, half), f32), array((spaces, rows_a, half), bf16)),
        [],
        6 * square,
        2 << 20,
        "svvv",
    )(time_at, chip_windows, pre_grad, beside_grad)
    crossed_a = lax.ppermute(cross_a, "tm", swap)
    half_grad = cols // 2
    pieces_b = full_call(
        pair_rim_kernel,
        tuple(
            array((rows_b + (half_grad if k == 1 else 0), channels), f32 if k == 0 else bf16)
            for k in range(spaces)
        ),
        [],
        spaces * rows_b * channels,
        1 << 20,
        "ssvvvv",
    )(core_at, space_at, keep_b, got_b, pre_grad, beside_grad)
    far_b = over_space(pieces_b)
    pieces_a = full_call(
        pair_kernel,
        tuple(array((rows_a, half), f32 if k == 0 else bf16) for k in range(spaces)),
        [],
        spaces * rows_a * half,
        1 << 20,
        "svv",
    )(space_at, own_a, crossed_a)
    far_a = over_space(pieces_a)
    sum_b, high = full_call(
        line_rim_kernel,
        (array((rows_b, channels), bf16), array((half_grad, channels), bf16)),
        [],
        4 * rows_b * channels,
        1 << 19,
        "v" * spaces,
    )(pieces_b[0], *far_b)
    other_b = lax.ppermute(sum_b, "tm", swap)
    low = lax.ppermute(high, "col", swap)
    sum_a = full_call(
        line_kernel, array((rows_a, half), bf16), [], 4 * rows_a * half, 1 << 19, "v" * spaces
    )(pieces_a[0], *far_a)
    other_a = lax.ppermute(sum_a, "tm", swap)
    x_grad = full_call(
        input_chip_kernel,
        array((2, double_cols, channels), bf16),
        [pltpu.VMEM((2 * (channels // LANES), double_cols, LANES), f32)],
        9 * square,
        4 << 20,
        "ssvvvvv",
    )(core_at, space_at, pre_grad, beside_grad, low, high, taps)
    other_a, x_grad = lax.optimization_barrier((other_a, x_grad))
    positions = frames * times * peers * cols
    kernel_grad, head_grad, bias_grad = full_call(
        functools.partial(final_kernel, 1.0 / math.sqrt(positions)),
        (
            array((9, share, channels), f32),
            array((share, 2 * latent_dim), f32),
            array((1, share), f32),
        ),
        [],
        rows_a * half + rows_b * channels,
        1 << 20,
        "svvvv",
    )(time_at, sum_a, other_a, sum_b, other_b)
    return (
        x_grad[None],
        kernel_grad.reshape(3, 3, share, channels),
        head_grad,
        bias_grad.reshape(share),
    )


def input_gradient(pre_grad, prev, taps):
    cols, channels = pre_grad.shape
    return full_call(
        input_kernel,
        jax.ShapeDtypeStruct((2, 2 * cols, channels), bf16),
        [pltpu.VMEM((2 * (channels // LANES), 2 * cols, LANES), f32)],
        18 * cols * channels * channels,
        4 << 20,
        "vvv",
    )(pre_grad, prev, taps)


def wide_body(activations, taps, conv_bias, head_weight, tiles, noise_sample):
    _, _, double_cols, channels = activations.shape
    cols = double_cols // 2
    latent_dim = noise_sample.shape[-1]
    line = ("space", "col")
    peers = lax.axis_size(line)
    next_row = lax.ppermute(activations[0, 0], line, [(i, i - 1) for i in range(1, peers)])
    upstream = lax.all_to_all(tiles, line, split_axis=0, concat_axis=0, tiled=True)
    padded = jnp.pad(jnp.concatenate([activations[0], next_row[None]], 0), ((0, 0), (0, 1), (0, 0)))
    windows = [
        padded[index // 3, index % 3 : index % 3 + 2 * cols : 2] for index in range(9)
    ]
    pre_act = jnp.zeros((cols, channels), f32) + conv_bias
    for index in range(9):
        pre_act = pre_act + dot(windows[index], taps[index], 1, 0)
    gating = jax.nn.sigmoid(pre_act)
    hidden = (pre_act * gating).astype(bf16)
    moments = dot(hidden, head_weight, 1, 0)
    upstream = jnp.transpose(upstream, (0, 2, 1)).reshape(cols, latent_dim).astype(f32)
    spread = jnp.exp(0.5 * moments[:, latent_dim:])
    mean_grad = upstream + kl_weight * moments[:, :latent_dim]
    logvar_grad = 0.5 * upstream * noise_sample[0, 0].astype(f32) * spread
    logvar_grad = logvar_grad + 0.5 * kl_weight * (spread * spread - 1.0)
    moment_grad = jnp.concatenate([mean_grad, logvar_grad], 1).astype(bf16)
    hidden_grad = dot(moment_grad, head_weight, 1, 1)
    pre_grad = (hidden_grad * gating * (1.0 + pre_act * (1.0 - gating))).astype(bf16)
    prev = lax.ppermute(pre_grad, line, [(i, i + 1) for i in range(peers - 1)])
    x_grad = input_gradient(pre_grad, prev, taps)
    kernel_term = jnp.stack([dot(window, pre_grad, 0, 0) for window in windows], 1)
    terms = (
        kernel_term.reshape(channels, 9 * channels),
        dot(hidden, moment_grad, 0, 0),
        jnp.sum(pre_grad, axis=0, dtype=f32),
    )
    grad_scale = 1.0 / math.sqrt(lax.axis_size("tm") * peers * cols)
    shares = [
        lax.psum_scatter(lax.psum(term, "tm"), line, scatter_dimension=0, tiled=True) * grad_scale
        for term in terms
    ]
    kernel_grad = jnp.transpose(shares[0].reshape(-1, 3, 3, channels), (1, 2, 0, 3))
    return x_grad[None], kernel_grad, shares[1], shares[2]


def solution(mesh):
    in_specs = (
        P(("groups", "tm"), ("space", "col"), None, None),
        P(),
        P(),
        P(),
        P(("groups", "tm"), None, ("space", "col"), None),
        P(("groups", "tm"), ("space", "col"), None, None),
    )
    out_specs = (
        P(("groups", "tm"), ("space", "col"), None, None),
        P(None, None, ("groups", "space", "col"), None),
        P(("groups", "space", "col"), None),
        P(("groups", "space", "col")),
    )
    return jax.shard_map(body, mesh=mesh, in_specs=in_specs, out_specs=out_specs, check_vma=False)
```

```python
import functools
import math

import jax
import jax.numpy as jnp
from jax import lax
from jax.experimental import pallas as pl
from jax.experimental.pallas import tpu as pltpu
from jax.sharding import PartitionSpec as P

f32 = jnp.float32
bf16 = jnp.bfloat16
kl_weight = 1.0
LANES = 128
HALVED = 6
TAIL = 8


def dot(a, b, ca, cb):
    return lax.dot_general(a, b, (((ca,), (cb,)), ((), ())), preferred_element_type=f32)


def params():
    return pltpu.CompilerParams(vmem_limit_bytes=12 << 20)


SPACES = {"s": pltpu.SMEM, "v": pltpu.VMEM, "h": pltpu.HBM}


def full_call(kernel, out_shape, scratch, flops, moved, places):
    call = pl.pallas_call(
        kernel,
        out_shape=out_shape,
        in_specs=[pl.BlockSpec(memory_space=SPACES[place]) for place in places],
        out_specs=jax.tree.map(lambda _: pl.BlockSpec(memory_space=pltpu.VMEM), out_shape),
        scratch_shapes=scratch,
        compiler_params=params(),
        cost_estimate=pl.CostEstimate(flops=flops, bytes_accessed=moved, transcendentals=0),
    )

    def placed(*args):
        pinned = [
            pltpu.with_memory_space_constraint(arg, pltpu.HBM) if place == "h" else arg
            for arg, place in zip(args, places)
        ]
        return call(*pinned)

    return placed


def start_kernel(act_ref, tiles_in, row_ref, tiles_ref, sems):
    copies = [pltpu.make_async_copy(tiles_in, tiles_ref, sems.at[0])]
    pieces = sems.shape[0] - 1
    length = row_ref.shape[0] // pieces
    for i in range(pieces):
        here = pl.ds(i * length, length)
        copies.append(
            pltpu.make_async_copy(act_ref.at[0, here], row_ref.at[here], sems.at[1 + i])
        )
    for copy in copies:
        copy.start()
    for copy in copies:
        copy.wait()


def tiles_kernel(core_ref, space_ref, own_ref, got_ref, here_ref, far_ref, before_ref):
    spaces = own_ref.shape[0] // 2
    height, width = own_ref.shape[1:]
    core, chip = core_ref[0], space_ref[0]
    first = core == 0

    def side_by_side(at):
        mine, other = own_ref[at], got_ref[at]
        return [jnp.where(first, mine, other), jnp.where(first, other, mine)]

    rest = [jnp.zeros((height, here_ref.shape[1] - 2 * width), bf16)]
    here_ref[...] = jnp.concatenate(side_by_side(2 * chip + core) + rest, 1)
    there = 2 * lax.rem(chip + 1 + core, spaces)
    far_ref[...] = jnp.concatenate(side_by_side(there) + side_by_side(there + 1), 1)
    there = 2 * lax.rem(chip + spaces - 1, spaces)
    before_ref[...] = jnp.concatenate(side_by_side(there) + side_by_side(there + 1), 1)


def join_kernel(far_ref, next_ref, out_ref):
    height = far_ref.shape[0]
    out_ref[:height, :] = far_ref[...]
    out_ref[height:, :] = next_ref[...]


def split_columns(row, source, stage):
    length, width = source.shape
    lanes = width // LANES
    source = source.astype(f32)
    for lane in range(lanes):
        stage[row * lanes + lane, :length, :] = source[:, lane * LANES : (lane + 1) * LANES]
        stage[row * lanes + lane, length:, :] = jnp.zeros((8, LANES), f32)
    windows = []
    for tap in range(3):
        halves = [
            stage[row * lanes + lane, pl.ds(tap, length // 2, stride=2), :]
            for lane in range(lanes)
        ]
        windows.append(jnp.concatenate(halves, 1).astype(bf16))
    return windows


def load_kernel(act_in, before_ref, act_ref, later_ref, sems):
    rows = act_in.shape[0]
    copies = [
        pltpu.make_async_copy(act_in.at[i], act_ref.at[i], sems.at[i]) for i in range(rows)
    ]
    for copy in copies:
        copy.start()
    later_ref[...] = before_ref[...]
    for copy in copies:
        copy.wait()


def early_kernel(
    bias_in, head_in, noise_in, w_in, act_ref, here_ref,
    pre_act_ref, w_ref, bias, head, noise, stage, sems,
):
    pairs = [(w_in.at[i : i + 3], w_ref.at[i : i + 3]) for i in (0, 3, 6)]
    pairs += [(bias_in, bias), (head_in, head), (noise_in, noise)]
    copies = [pltpu.make_async_copy(a, b, sems.at[i]) for i, (a, b) in enumerate(pairs)]
    for copy in copies:
        copy.start()
    cols = noise.shape[1]
    pre_act = None
    for row in range(2):
        windows = split_columns(row, act_ref[row], stage)
        copies[row].wait()
        for tap in range(3):
            term = dot(windows[tap], w_ref[3 * row + tap], 1, 0)
            pre_act = term if pre_act is None else pre_act + term
    for copy in copies[2:]:
        copy.wait()
    pre_act_ref[:cols, :] = pre_act + bias[...]
    at = cols
    for ref in (head, noise, here_ref):
        pre_act_ref[at : at + ref.shape[0], : ref.shape[1]] = ref[...].astype(f32)
        at += ref.shape[0]


def select_kernel(chips, core_ref, act_ref, beside_ref, windows_ref, stage):
    rows, length, width = beside_ref.shape
    kept = windows_ref.shape[2]
    share = kept // chips
    source = lax.broadcasted_iota(jnp.int32, (width, kept), 0)
    target = lax.broadcasted_iota(jnp.int32, (width, kept), 1)
    wanted = 2 * share * (target // share) + share * core_ref[0] + target % share
    select = jnp.where(source == wanted, 1.0, 0.0).astype(bf16)
    cols = length // 2
    for row in range(rows):
        for at, ref in enumerate((act_ref, beside_ref)):
            picked = dot(ref[row], select, 1, 0)
            windows = split_columns(rows * at + row, picked, stage)
            for tap in range(3):
                windows_ref[3 * row + tap, cols * at : cols * (at + 1), :] = windows[tap]


def conv_kernel(
    chips, core_ref, space_ref, early_ref, w_ref, above_ref,
    pre_act_ref, windows_ref, hidden_ref, stage,
):
    cols = hidden_ref.shape[0]
    last = (core_ref[0] == 1) & (space_ref[0] == chips - 1)
    row = above_ref[...]
    windows = split_columns(0, jnp.where(last, jnp.zeros_like(row), row), stage)
    pre_act = early_ref[:cols, :]
    for tap in range(3):
        windows_ref[tap] = windows[tap]
        pre_act = pre_act + dot(windows[tap], w_ref[6 + tap], 1, 0)
    pre_act_ref[...] = pre_act
    hidden_ref[...] = jax.nn.silu(pre_act).astype(bf16)


def grad_kernel(
    core_ref, space_ref, early_ref, pre_act_ref, hidden_ref, tiles_ref, other_tiles_ref,
    pre_grad_ref, moment_grad_ref, tiles_at,
):
    cols, width = pre_grad_ref.shape
    spaces, latent, lanes = tiles_at.shape
    head = early_ref[cols : cols + 2 * latent, :].astype(bf16)
    at = cols + 2 * latent
    sample = early_ref[at : at + latent, :cols]
    chip = space_ref[0]
    first = core_ref[0] == 0
    tiles_at[chip] = early_ref[at + latent : at + 2 * latent, :lanes].astype(bf16)
    mine, other = tiles_ref[...], other_tiles_ref[...]
    for there, both in (
        (spaces - 1, jnp.where(first, mine[:latent], other[:latent])),
        (spaces - 2, jnp.where(first, other[:latent], mine[:latent])),
        (1, jnp.where(first, mine[latent:], other[latent:])),
    ):
        band = jnp.where(first, both[:, :lanes], both[:, lanes:])
        tiles_at[lax.rem(chip + there, spaces)] = band
    pre_act = pre_act_ref[...]
    gating = jax.nn.sigmoid(pre_act)
    moments = dot(head, hidden_ref[...], 1, 1)
    mean_part = moments[:latent]
    logvar = moments[latent:]
    upstream = jnp.concatenate([tiles_at[i].astype(f32) for i in range(spaces)], 1)
    spread = jnp.exp(0.5 * logvar)
    mean_grad = upstream + kl_weight * mean_part
    logvar_grad = 0.5 * upstream * sample * spread + 0.5 * kl_weight * (spread * spread - 1.0)
    moment_grad = jnp.concatenate([mean_grad, logvar_grad], 0).astype(bf16)
    hidden_grad = dot(moment_grad, head, 0, 0)
    pre_grad = (hidden_grad * gating * (1.0 + pre_act * (1.0 - gating))).astype(bf16)
    pre_grad_ref[...] = pre_grad
    moment_grad_ref[...] = moment_grad


def put_shares(first, keep_ref, send_ref, at, term):
    spaces = keep_ref.shape[0]
    share = term.shape[0] // (2 * spaces)
    for s in range(spaces):
        row = 2 * share * s
        even, odd = term[row : row + share], term[row + share : row + 2 * share]
        keep_ref[s, at : at + share, :] = jnp.where(first, even, odd)
        send_ref[s, at : at + share, :] = jnp.where(first, odd, even).astype(bf16)


def frame_terms_kernel(
    core_ref, windows_ref, pre_grad_ref, hidden_ref, moment_grad_ref, keep_ref, send_ref
):
    cols, width = pre_grad_ref.shape
    spaces = keep_ref.shape[0]
    share = width // (2 * spaces)
    first = core_ref[0] == 0
    pre_grad = pre_grad_ref[...]
    taps = windows_ref.shape[0]
    for tap in range(taps):
        put_shares(first, keep_ref, send_ref, tap * share, dot(windows_ref[tap], pre_grad, 0, 0))
    head_term = dot(hidden_ref[...], moment_grad_ref[...], 0, 1)
    bias_term = dot(jnp.ones((TAIL, cols), bf16), pre_grad, 1, 0)

    def tail(row):
        pieces = [head_term[row + i : row + i + TAIL] for i in range(0, share, TAIL)]
        pieces.append(bias_term[:, row : row + share])
        used = sum(piece.shape[1] for piece in pieces)
        pieces.append(jnp.zeros((TAIL, width - used), f32))
        return jnp.concatenate(pieces, 1)

    tails = []
    for s in range(2 * spaces):
        tails.append(tail(share * s))
    put_shares(first, keep_ref, send_ref, taps * share, jnp.concatenate(tails, 0))


def chip_terms_kernel(
    time_ref, windows_ref, pre_grad_ref, beside_ref, own_ref, send_ref
):
    first = time_ref[0] == 0
    pre_grad = jnp.concatenate([pre_grad_ref[...], beside_ref[...]], 0)
    spaces, _, half = own_ref.shape
    share = windows_ref.shape[2] // spaces
    for index in range(HALVED):
        term = dot(windows_ref[index], pre_grad, 0, 0)
        low, high = term[:, :half], term[:, half:]
        mine = jnp.where(first, low, high)
        other = jnp.where(first, high, low).astype(bf16)
        here = slice(index * share, (index + 1) * share)
        for s in range(spaces):
            own_ref[s, here, :] = mine[s * share : (s + 1) * share]
            send_ref[s, here, :] = other[s * share : (s + 1) * share]


def pair_kernel(space_ref, keep_ref, got_ref, *outs):
    spaces = len(outs)
    for k, out in enumerate(outs):
        at = lax.rem(space_ref[0] + k, spaces)
        out[...] = (keep_ref[at] + got_ref[at].astype(f32)).astype(out.dtype)


def pair_rim_kernel(core_ref, space_ref, keep_ref, got_ref, mine_ref, beside_ref, *outs):
    spaces = len(outs)
    rows = keep_ref.shape[1]
    for k, out in enumerate(outs):
        at = lax.rem(space_ref[0] + k, spaces)
        out[:rows, :] = (keep_ref[at] + got_ref[at].astype(f32)).astype(out.dtype)
    half = mine_ref.shape[0] // 2
    first = core_ref[0] == 0
    outs[1][rows:, :] = jnp.where(first, beside_ref[half:, :], mine_ref[:half, :])


def line_kernel(own_ref, *refs):
    total = own_ref[...]
    for ref in refs[:-1]:
        total = total + ref[...].astype(f32)
    refs[-1][...] = total.astype(bf16)


def line_rim_kernel(own_ref, *refs):
    rows = own_ref.shape[0]
    total = own_ref[...]
    for ref in refs[:-2]:
        total = total + ref[:rows, :].astype(f32)
    refs[-2][...] = total.astype(bf16)
    refs[-1][...] = refs[0][rows:, :]


def final_kernel(
    scale, time_ref, a_ref, a_far_ref, b_ref, b_far_ref, kernel_ref, head_ref, bias_ref
):
    share, latents = head_ref.shape
    first = time_ref[0] == 0
    mine, far = a_ref[...].astype(f32) * scale, a_far_ref[...].astype(f32) * scale
    low, high = jnp.where(first, mine, far), jnp.where(first, far, mine)
    total = (b_ref[...].astype(f32) + b_far_ref[...].astype(f32)) * scale
    half = mine.shape[1]
    for index in range(HALVED):
        kernel_ref[index, :, :half] = low[index * share : (index + 1) * share]
        kernel_ref[index, :, half:] = high[index * share : (index + 1) * share]
    for index in range(HALVED, 9):
        at = (index - HALVED) * share
        kernel_ref[index] = total[at : at + share]
    tail = total[(9 - HALVED) * share :]
    for i in range(share // TAIL):
        head_ref[TAIL * i : TAIL * (i + 1), :] = tail[:, latents * i : latents * (i + 1)]
    at = latents * (share // TAIL)
    bias_ref[...] = tail[:1, at : at + share]


def input_kernel(pre_grad_ref, prev_ref, w_ref, out_ref, stage):
    input_rows(pre_grad_ref, prev_ref[...], w_ref, out_ref, stage)


def input_chip_kernel(
    core_ref, space_ref, pre_grad_ref, beside_ref, low_ref, high_ref, w_ref, out_ref, stage
):
    below = jnp.concatenate([low_ref[...], high_ref[...]], 0)
    below = jnp.where(space_ref[0] == 0, jnp.zeros_like(below), below)
    prev = jnp.where(core_ref[0] == 0, below, beside_ref[...])
    input_rows(pre_grad_ref, prev, w_ref, out_ref, stage)


def input_rows(pre_grad_ref, prev, w_ref, out_ref, stage):
    cols, width = pre_grad_ref.shape
    pre_grad = pre_grad_ref[...]
    row_at = lax.broadcasted_iota(jnp.int32, (cols, width), 0)

    def planes(source, row_tap):
        even = dot(source, w_ref[3 * row_tap], 1, 1)
        odd = dot(source, w_ref[3 * row_tap + 1], 1, 1)
        late = pltpu.roll(dot(source, w_ref[3 * row_tap + 2], 1, 1), 1, 0)
        return even + jnp.where(row_at == 0, 0.0, late), odd

    def weave(row, even, odd):
        for lane in range(width // LANES):
            at = row * (width // LANES) + lane
            here = slice(lane * LANES, (lane + 1) * LANES)
            stage[at, pl.ds(0, cols, stride=2), :] = even[:, here]
            stage[at, pl.ds(1, cols, stride=2), :] = odd[:, here]
            out_ref[row, :, here] = stage[at].astype(bf16)

    even, odd = planes(pre_grad, 1)
    weave(1, even, odd)
    even, odd = planes(pre_grad, 0)
    even_rim, odd_rim = planes(prev, 2)
    weave(0, even + even_rim, odd + odd_rim)


def body(activations, conv_weight, conv_bias, head_weight, latent_grad, noise_sample):
    frames, double_rows, double_cols, channels = activations.shape
    cols = double_cols // 2
    latent_dim = latent_grad.shape[-1]
    spaces = lax.axis_size("space")
    times = lax.axis_size("tm")
    line = ("space", "col")
    peers = lax.axis_size(line)
    assert frames == 1 and double_rows == 2 and lax.axis_size("col") == 2
    share = channels // peers
    taps = conv_weight.reshape(9, channels, channels)
    tiles = jnp.transpose(latent_grad[0], (0, 2, 1))
    if share % TAIL or spaces != 4 or times != 2:
        return wide_body(activations, taps, conv_bias, head_weight, tiles, noise_sample)
    core_at = lax.axis_index("col").astype(jnp.int32).reshape(1)
    space_at = lax.axis_index("space").astype(jnp.int32).reshape(1)
    time_at = lax.axis_index("tm").astype(jnp.int32).reshape(1)
    swap = [(0, 1), (1, 0)]
    array = jax.ShapeDtypeStruct

    def over_space(pieces):
        return [
            lax.ppermute(pieces[k], "space", [(i, (i + k) % spaces) for i in range(spaces)])
            for k in range(1, spaces)
        ]

    tile = tiles.shape[1:]
    got_tiles = lax.ppermute(tiles, "col", swap)
    row, own_tiles = full_call(
        start_kernel,
        (array((double_cols, channels), bf16), array(tiles.shape, bf16)),
        [pltpu.SemaphoreType.DMA((9,))],
        0,
        1 << 19,
        "hh",
    )(activations[0], tiles)
    here, far, before = full_call(
        tiles_kernel, (array((tile[0], LANES), bf16),) * 3, [], 0, 1 << 16, "ssvv"
    )(core_at, space_at, own_tiles, got_tiles)
    row, far = lax.optimization_barrier((row, far))
    above = lax.ppermute(row, line, [(i, (i - 1) % peers) for i in range(peers)])
    hops = [(2 * i + c, 2 * ((i + 1 + c) % spaces) + c) for i in range(spaces) for c in range(2)]
    far = lax.ppermute(far, line, hops)
    square = 2 * cols * channels * channels
    act_here, before = full_call(
        load_kernel,
        (
            array((double_rows, double_cols, channels), bf16),
            array((tile[0], LANES), bf16),
        ),
        [pltpu.SemaphoreType.DMA((double_rows,))],
        60 * square,
        2 << 20,
        "hv",
    )(activations[0], before)
    early, w_here = full_call(
        early_kernel,
        (array((cols + 4 * latent_dim, channels), f32), array(taps.shape, bf16)),
        [
            pltpu.VMEM((1, channels), f32),
            pltpu.VMEM((2 * latent_dim, channels), bf16),
            pltpu.VMEM((latent_dim, cols), bf16),
            pltpu.VMEM((2 * (channels // LANES), double_cols + 8, LANES), f32),
            pltpu.SemaphoreType.DMA((6,)),
        ],
        300 * square,
        3 << 20,
        "hhhhvv",
    )(
        conv_bias.reshape(1, channels),
        head_weight.T,
        jnp.transpose(noise_sample[0, 0]),
        taps,
        act_here,
        here,
    )
    back = [(2 * i + 1, 2 * ((i - 1) % spaces)) for i in range(spaces)]
    after = lax.ppermute(before, line, back + [(2 * i, 2 * i + 1) for i in range(spaces)])
    beside = lax.ppermute(act_here, "col", swap)
    chip_windows = full_call(
        functools.partial(select_kernel, spaces),
        array((6, 2 * cols, channels // 2), bf16),
        [pltpu.VMEM((4 * (channels // 2 // LANES), double_cols + 8, LANES), f32)],
        4 * square,
        2 << 20,
        "svv",
    )(core_at, act_here, beside)
    early, chip_windows, far, after = lax.optimization_barrier((early, chip_windows, far, after))
    came = full_call(
        join_kernel, array((2 * tile[0], LANES), bf16), [], 0, 1 << 14, "vv"
    )(far, after)
    other_came = lax.ppermute(came, "col", swap)
    above, came = lax.optimization_barrier((above, came))
    rows_a = HALVED * share
    rows_b = (9 - HALVED) * share + TAIL
    half = channels // 2
    pre_act, last_windows, hidden = full_call(
        functools.partial(conv_kernel, spaces),
        (
            array((cols, channels), f32),
            array((3, cols, channels), bf16),
            array((cols, channels), bf16),
        ),
        [pltpu.VMEM((channels // LANES, double_cols + 8, LANES), f32)],
        3 * square,
        2 << 20,
        "ssvvv",
    )(core_at, space_at, early, w_here, above)
    pre_grad, moment_grad = full_call(
        grad_kernel,
        (array((cols, channels), bf16), array((2 * latent_dim, cols), bf16)),
        [pltpu.VMEM((spaces, tile[0], 2 * tile[1]), bf16)],
        square,
        1 << 20,
        "ssvvvvv",
    )(core_at, space_at, early, pre_act, hidden, came, other_came)
    beside_grad = lax.ppermute(pre_grad, "col", swap)
    keep_b, send_b = full_call(
        frame_terms_kernel,
        (
            array((spaces, rows_b, channels), f32),
            array((spaces, rows_b, channels), bf16),
        ),
        [],
        cols,
        cols,
        "svvvv",
    )(core_at, last_windows, pre_grad, hidden, moment_grad)
    got_b = lax.ppermute(send_b, "col", swap)
    own_a, cross_a = full_call(
        chip_terms_kernel,
        (array((spaces, rows_a, half), f32), array((spaces, rows_a, half), bf16)),
        [],
        6 * square,
        2 << 20,
        "svvv",
    )(time_at, chip_windows, pre_grad, beside_grad)
    crossed_a = lax.ppermute(cross_a, "tm", swap)
    half_grad = cols // 2
    pieces_b = full_call(
        pair_rim_kernel,
        tuple(
            array((rows_b + (half_grad if k == 1 else 0), channels), f32 if k == 0 else bf16)
            for k in range(spaces)
        ),
        [],
        spaces * rows_b * channels,
        1 << 20,
        "ssvvvv",
    )(core_at, space_at, keep_b, got_b, pre_grad, beside_grad)
    far_b = over_space(pieces_b)
    pieces_a = full_call(
        pair_kernel,
        tuple(array((rows_a, half), f32 if k == 0 else bf16) for k in range(spaces)),
        [],
        spaces * rows_a * half,
        1 << 20,
        "svv",
    )(space_at, own_a, crossed_a)
    far_a = over_space(pieces_a)
    sum_b, high = full_call(
        line_rim_kernel,
        (array((rows_b, channels), bf16), array((half_grad, channels), bf16)),
        [],
        4 * rows_b * channels,
        1 << 19,
        "v" * spaces,
    )(pieces_b[0], *far_b)
    other_b = lax.ppermute(sum_b, "tm", swap)
    low = lax.ppermute(high, "col", swap)
    sum_a = full_call(
        line_kernel, array((rows_a, half), bf16), [], 4 * rows_a * half, 1 << 19, "v" * spaces
    )(pieces_a[0], *far_a)
    other_a = lax.ppermute(sum_a, "tm", swap)
    x_grad = full_call(
        input_chip_kernel,
        array((2, double_cols, channels), bf16),
        [pltpu.VMEM((2 * (channels // LANES), double_cols, LANES), f32)],
        9 * square,
        4 << 20,
        "ssvvvvv",
    )(core_at, space_at, pre_grad, beside_grad, low, high, taps)
    other_a, x_grad = lax.optimization_barrier((other_a, x_grad))
    positions = frames * times * peers * cols
    kernel_grad, head_grad, bias_grad = full_call(
        functools.partial(final_kernel, 1.0 / math.sqrt(positions)),
        (
            array((9, share, channels), f32),
            array((share, 2 * latent_dim), f32),
            array((1, share), f32),
        ),
        [],
        rows_a * half + rows_b * channels,
        1 << 20,
        "svvvv",
    )(time_at, sum_a, other_a, sum_b, other_b)
    return (
        x_grad[None],
        kernel_grad.reshape(3, 3, share, channels),
        head_grad,
        bias_grad.reshape(share),
    )


def input_gradient(pre_grad, prev, taps):
    cols, channels = pre_grad.shape
    return full_call(
        input_kernel,
        jax.ShapeDtypeStruct((2, 2 * cols, channels), bf16),
        [pltpu.VMEM((2 * (channels // LANES), 2 * cols, LANES), f32)],
        18 * cols * channels * channels,
        4 << 20,
        "vvv",
    )(pre_grad, prev, taps)


def wide_body(activations, taps, conv_bias, head_weight, tiles, noise_sample):
    _, _, double_cols, channels = activations.shape
    cols = double_cols // 2
    latent_dim = noise_sample.shape[-1]
    line = ("space", "col")
    peers = lax.axis_size(line)
    next_row = lax.ppermute(activations[0, 0], line, [(i, i - 1) for i in range(1, peers)])
    upstream = lax.all_to_all(tiles, line, split_axis=0, concat_axis=0, tiled=True)
    padded = jnp.pad(jnp.concatenate([activations[0], next_row[None]], 0), ((0, 0), (0, 1), (0, 0)))
    windows = [
        padded[index // 3, index % 3 : index % 3 + 2 * cols : 2] for index in range(9)
    ]
    pre_act = jnp.zeros((cols, channels), f32) + conv_bias
    for index in range(9):
        pre_act = pre_act + dot(windows[index], taps[index], 1, 0)
    gating = jax.nn.sigmoid(pre_act)
    hidden = (pre_act * gating).astype(bf16)
    moments = dot(hidden, head_weight, 1, 0)
    upstream = jnp.transpose(upstream, (0, 2, 1)).reshape(cols, latent_dim).astype(f32)
    spread = jnp.exp(0.5 * moments[:, latent_dim:])
    mean_grad = upstream + kl_weight * moments[:, :latent_dim]
    logvar_grad = 0.5 * upstream * noise_sample[0, 0].astype(f32) * spread
    logvar_grad = logvar_grad + 0.5 * kl_weight * (spread * spread - 1.0)
    moment_grad = jnp.concatenate([mean_grad, logvar_grad], 1).astype(bf16)
    hidden_grad = dot(moment_grad, head_weight, 1, 1)
    pre_grad = (hidden_grad * gating * (1.0 + pre_act * (1.0 - gating))).astype(bf16)
    prev = lax.ppermute(pre_grad, line, [(i, i + 1) for i in range(peers - 1)])
    x_grad = input_gradient(pre_grad, prev, taps)
    kernel_term = jnp.stack([dot(window, pre_grad, 0, 0) for window in windows], 1)
    terms = (
        kernel_term.reshape(channels, 9 * channels),
        dot(hidden, moment_grad, 0, 0),
        jnp.sum(pre_grad, axis=0, dtype=f32),
    )
    grad_scale = 1.0 / math.sqrt(lax.axis_size("tm") * peers * cols)
    shares = [
        lax.psum_scatter(lax.psum(term, "tm"), line, scatter_dimension=0, tiled=True) * grad_scale
        for term in terms
    ]
    kernel_grad = jnp.transpose(shares[0].reshape(-1, 3, 3, channels), (1, 2, 0, 3))
    return x_grad[None], kernel_grad, shares[1], shares[2]


def solution(mesh):
    in_specs = (
        P(("groups", "tm"), ("space", "col"), None, None),
        P(),
        P(),
        P(),
        P(("groups", "tm"), None, ("space", "col"), None),
        P(("groups", "tm"), ("space", "col"), None, None),
    )
    out_specs = (
        P(("groups", "tm"), ("space", "col"), None, None),
        P(None, None, ("groups", "space", "col"), None),
        P(("groups", "space", "col"), None),
        P(("groups", "space", "col")),
    )
    return jax.shard_map(body, mesh=mesh, in_specs=in_specs, out_specs=out_specs, check_vma=False)
```

```python
import functools
import math

import jax
import jax.numpy as jnp
from jax import lax
from jax.experimental import pallas as pl
from jax.experimental.pallas import tpu as pltpu
from jax.sharding import PartitionSpec as P

f32 = jnp.float32
bf16 = jnp.bfloat16
kl_weight = 1.0
LANES = 128
HALVED = 6
TAIL = 8


def dot(a, b, ca, cb):
    return lax.dot_general(a, b, (((ca,), (cb,)), ((), ())), preferred_element_type=f32)


def params():
    return pltpu.CompilerParams(vmem_limit_bytes=12 << 20)


SPACES = {"s": pltpu.SMEM, "v": pltpu.VMEM, "h": pltpu.HBM}


def full_call(kernel, out_shape, scratch, flops, moved, places):
    call = pl.pallas_call(
        kernel,
        out_shape=out_shape,
        in_specs=[pl.BlockSpec(memory_space=SPACES[place]) for place in places],
        out_specs=jax.tree.map(lambda _: pl.BlockSpec(memory_space=pltpu.VMEM), out_shape),
        scratch_shapes=scratch,
        compiler_params=params(),
        cost_estimate=pl.CostEstimate(flops=flops, bytes_accessed=moved, transcendentals=0),
    )

    def placed(*args):
        pinned = [
            pltpu.with_memory_space_constraint(arg, pltpu.HBM) if place == "h" else arg
            for arg, place in zip(args, places)
        ]
        return call(*pinned)

    return placed


def start_kernel(act_ref, tiles_in, row_ref, second_ref, tiles_ref, sems):
    copies = [
        pltpu.make_async_copy(tiles_in, tiles_ref, sems.at[0]),
        pltpu.make_async_copy(act_ref.at[0], row_ref, sems.at[1]),
        pltpu.make_async_copy(act_ref.at[1], second_ref, sems.at[2]),
    ]
    for copy in copies:
        copy.start()
    for copy in copies:
        copy.wait()


def tiles_kernel(core_ref, space_ref, own_ref, got_ref, here_ref, far_ref, before_ref):
    spaces = own_ref.shape[0] // 2
    height, width = own_ref.shape[1:]
    core, chip = core_ref[0], space_ref[0]
    first = core == 0

    def side_by_side(at):
        mine, other = own_ref[at], got_ref[at]
        return [jnp.where(first, mine, other), jnp.where(first, other, mine)]

    rest = [jnp.zeros((height, here_ref.shape[1] - 2 * width), bf16)]
    here_ref[...] = jnp.concatenate(side_by_side(2 * chip + core) + rest, 1)
    there = 2 * lax.rem(chip + 1 + core, spaces)
    far_ref[...] = jnp.concatenate(side_by_side(there) + side_by_side(there + 1), 1)
    there = 2 * lax.rem(chip + spaces - 1, spaces)
    before_ref[...] = jnp.concatenate(side_by_side(there) + side_by_side(there + 1), 1)


def join_kernel(far_ref, next_ref, out_ref):
    height = far_ref.shape[0]
    out_ref[:height, :] = far_ref[...]
    out_ref[height:, :] = next_ref[...]


def split_columns(row, source, stage):
    length, width = source.shape
    lanes = width // LANES
    source = source.astype(f32)
    for lane in range(lanes):
        stage[row * lanes + lane, :length, :] = source[:, lane * LANES : (lane + 1) * LANES]
        stage[row * lanes + lane, length:, :] = jnp.zeros((8, LANES), f32)
    windows = []
    for tap in range(3):
        halves = [
            stage[row * lanes + lane, pl.ds(tap, length // 2, stride=2), :]
            for lane in range(lanes)
        ]
        windows.append(jnp.concatenate(halves, 1).astype(bf16))
    return windows


def load_kernel(row_ref, second_ref, before_ref, act_ref, later_ref):
    act_ref[0] = row_ref[...]
    act_ref[1] = second_ref[...]
    later_ref[...] = before_ref[...]


def early_kernel(
    bias_in, head_in, noise_in, w_in, act_ref, here_ref,
    pre_act_ref, w_ref, bias, head, noise, stage, sems,
):
    pairs = [(w_in.at[i : i + 3], w_ref.at[i : i + 3]) for i in (0, 3, 6)]
    pairs += [(bias_in, bias), (head_in, head), (noise_in, noise)]
    copies = [pltpu.make_async_copy(a, b, sems.at[i]) for i, (a, b) in enumerate(pairs)]
    for copy in copies:
        copy.start()
    cols = noise.shape[1]
    pre_act = None
    for row in range(2):
        windows = split_columns(row, act_ref[row], stage)
        copies[row].wait()
        for tap in range(3):
            term = dot(windows[tap], w_ref[3 * row + tap], 1, 0)
            pre_act = term if pre_act is None else pre_act + term
    for copy in copies[2:]:
        copy.wait()
    pre_act_ref[:cols, :] = pre_act + bias[...]
    at = cols
    for ref in (head, noise, here_ref):
        pre_act_ref[at : at + ref.shape[0], : ref.shape[1]] = ref[...].astype(f32)
        at += ref.shape[0]


def select_kernel(chips, core_ref, act_ref, beside_ref, windows_ref, stage):
    rows, length, width = beside_ref.shape
    kept = windows_ref.shape[2]
    share = kept // chips
    source = lax.broadcasted_iota(jnp.int32, (width, kept), 0)
    target = lax.broadcasted_iota(jnp.int32, (width, kept), 1)
    wanted = 2 * share * (target // share) + share * core_ref[0] + target % share
    select = jnp.where(source == wanted, 1.0, 0.0).astype(bf16)
    cols = length // 2
    for row in range(rows):
        for at, ref in enumerate((act_ref, beside_ref)):
            picked = dot(ref[row], select, 1, 0)
            windows = split_columns(rows * at + row, picked, stage)
            for tap in range(3):
                windows_ref[3 * row + tap, cols * at : cols * (at + 1), :] = windows[tap]


def conv_kernel(
    chips, core_ref, space_ref, early_ref, w_ref, above_ref,
    pre_act_ref, windows_ref, hidden_ref, stage,
):
    cols = hidden_ref.shape[0]
    last = (core_ref[0] == 1) & (space_ref[0] == chips - 1)
    row = above_ref[...]
    windows = split_columns(0, jnp.where(last, jnp.zeros_like(row), row), stage)
    pre_act = early_ref[:cols, :]
    for tap in range(3):
        windows_ref[tap] = windows[tap]
        pre_act = pre_act + dot(windows[tap], w_ref[6 + tap], 1, 0)
    pre_act_ref[...] = pre_act
    hidden_ref[...] = jax.nn.silu(pre_act).astype(bf16)


def grad_kernel(
    core_ref, space_ref, early_ref, pre_act_ref, hidden_ref, tiles_ref, other_tiles_ref,
    pre_grad_ref, moment_grad_ref, tiles_at,
):
    cols, width = pre_grad_ref.shape
    spaces, latent, lanes = tiles_at.shape
    head = early_ref[cols : cols + 2 * latent, :].astype(bf16)
    at = cols + 2 * latent
    sample = early_ref[at : at + latent, :cols]
    chip = space_ref[0]
    first = core_ref[0] == 0
    tiles_at[chip] = early_ref[at + latent : at + 2 * latent, :lanes].astype(bf16)
    mine, other = tiles_ref[...], other_tiles_ref[...]
    for there, both in (
        (spaces - 1, jnp.where(first, mine[:latent], other[:latent])),
        (spaces - 2, jnp.where(first, other[:latent], mine[:latent])),
        (1, jnp.where(first, mine[latent:], other[latent:])),
    ):
        band = jnp.where(first, both[:, :lanes], both[:, lanes:])
        tiles_at[lax.rem(chip + there, spaces)] = band
    pre_act = pre_act_ref[...]
    gating = jax.nn.sigmoid(pre_act)
    moments = dot(head, hidden_ref[...], 1, 1)
    mean_part = moments[:latent]
    logvar = moments[latent:]
    upstream = jnp.concatenate([tiles_at[i].astype(f32) for i in range(spaces)], 1)
    spread = jnp.exp(0.5 * logvar)
    mean_grad = upstream + kl_weight * mean_part
    logvar_grad = 0.5 * upstream * sample * spread + 0.5 * kl_weight * (spread * spread - 1.0)
    moment_grad = jnp.concatenate([mean_grad, logvar_grad], 0).astype(bf16)
    hidden_grad = dot(moment_grad, head, 0, 0)
    pre_grad = (hidden_grad * gating * (1.0 + pre_act * (1.0 - gating))).astype(bf16)
    pre_grad_ref[...] = pre_grad
    moment_grad_ref[...] = moment_grad


def put_shares(first, keep_ref, send_ref, at, term):
    spaces = keep_ref.shape[0]
    share = term.shape[0] // (2 * spaces)
    for s in range(spaces):
        row = 2 * share * s
        even, odd = term[row : row + share], term[row + share : row + 2 * share]
        keep_ref[s, at : at + share, :] = jnp.where(first, even, odd)
        send_ref[s, at : at + share, :] = jnp.where(first, odd, even).astype(bf16)


def frame_terms_kernel(
    core_ref, windows_ref, pre_grad_ref, hidden_ref, moment_grad_ref, keep_ref, send_ref
):
    cols, width = pre_grad_ref.shape
    spaces = keep_ref.shape[0]
    share = width // (2 * spaces)
    first = core_ref[0] == 0
    pre_grad = pre_grad_ref[...]
    taps = windows_ref.shape[0]
    for tap in range(taps):
        put_shares(first, keep_ref, send_ref, tap * share, dot(windows_ref[tap], pre_grad, 0, 0))
    head_term = dot(hidden_ref[...], moment_grad_ref[...], 0, 1)
    bias_term = dot(jnp.ones((TAIL, cols), bf16), pre_grad, 1, 0)

    def tail(row):
        pieces = [head_term[row + i : row + i + TAIL] for i in range(0, share, TAIL)]
        pieces.append(bias_term[:, row : row + share])
        used = sum(piece.shape[1] for piece in pieces)
        pieces.append(jnp.zeros((TAIL, width - used), f32))
        return jnp.concatenate(pieces, 1)

    tails = []
    for s in range(2 * spaces):
        tails.append(tail(share * s))
    put_shares(first, keep_ref, send_ref, taps * share, jnp.concatenate(tails, 0))


def chip_terms_kernel(
    time_ref, windows_ref, pre_grad_ref, beside_ref, own_ref, send_ref
):
    first = time_ref[0] == 0
    pre_grad = jnp.concatenate([pre_grad_ref[...], beside_ref[...]], 0)
    spaces, _, half = own_ref.shape
    share = windows_ref.shape[2] // spaces
    for index in range(HALVED):
        term = dot(windows_ref[index], pre_grad, 0, 0)
        low, high = term[:, :half], term[:, half:]
        mine = jnp.where(first, low, high)
        other = jnp.where(first, high, low).astype(bf16)
        here = slice(index * share, (index + 1) * share)
        for s in range(spaces):
            own_ref[s, here, :] = mine[s * share : (s + 1) * share]
            send_ref[s, here, :] = other[s * share : (s + 1) * share]


def pair_kernel(space_ref, keep_ref, got_ref, *outs):
    spaces = len(outs)
    for k, out in enumerate(outs):
        at = lax.rem(space_ref[0] + k, spaces)
        out[...] = (keep_ref[at] + got_ref[at].astype(f32)).astype(out.dtype)


def pair_rim_kernel(core_ref, space_ref, keep_ref, got_ref, mine_ref, beside_ref, *outs):
    spaces = len(outs)
    rows = keep_ref.shape[1]
    for k, out in enumerate(outs):
        at = lax.rem(space_ref[0] + k, spaces)
        out[:rows, :] = (keep_ref[at] + got_ref[at].astype(f32)).astype(out.dtype)
    half = mine_ref.shape[0] // 2
    first = core_ref[0] == 0
    outs[1][rows:, :] = jnp.where(first, beside_ref[half:, :], mine_ref[:half, :])


def line_kernel(own_ref, *refs):
    total = own_ref[...]
    for ref in refs[:-1]:
        total = total + ref[...].astype(f32)
    refs[-1][...] = total.astype(bf16)


def line_rim_kernel(own_ref, *refs):
    rows = own_ref.shape[0]
    total = own_ref[...]
    for ref in refs[:-2]:
        total = total + ref[:rows, :].astype(f32)
    refs[-2][...] = total.astype(bf16)
    refs[-1][...] = refs[0][rows:, :]


def final_kernel(
    scale, time_ref, a_ref, a_far_ref, b_ref, b_far_ref, kernel_ref, head_ref, bias_ref
):
    share, latents = head_ref.shape
    first = time_ref[0] == 0
    mine, far = a_ref[...].astype(f32) * scale, a_far_ref[...].astype(f32) * scale
    low, high = jnp.where(first, mine, far), jnp.where(first, far, mine)
    total = (b_ref[...].astype(f32) + b_far_ref[...].astype(f32)) * scale
    half = mine.shape[1]
    for index in range(HALVED):
        kernel_ref[index, :, :half] = low[index * share : (index + 1) * share]
        kernel_ref[index, :, half:] = high[index * share : (index + 1) * share]
    for index in range(HALVED, 9):
        at = (index - HALVED) * share
        kernel_ref[index] = total[at : at + share]
    tail = total[(9 - HALVED) * share :]
    for i in range(share // TAIL):
        head_ref[TAIL * i : TAIL * (i + 1), :] = tail[:, latents * i : latents * (i + 1)]
    at = latents * (share // TAIL)
    bias_ref[...] = tail[:1, at : at + share]


def input_kernel(pre_grad_ref, prev_ref, w_ref, out_ref, stage):
    input_rows(pre_grad_ref, prev_ref[...], w_ref, out_ref, stage)


def input_chip_kernel(
    core_ref, space_ref, pre_grad_ref, beside_ref, low_ref, high_ref, w_ref, out_ref, stage
):
    below = jnp.concatenate([low_ref[...], high_ref[...]], 0)
    below = jnp.where(space_ref[0] == 0, jnp.zeros_like(below), below)
    prev = jnp.where(core_ref[0] == 0, below, beside_ref[...])
    input_rows(pre_grad_ref, prev, w_ref, out_ref, stage)


def input_rows(pre_grad_ref, prev, w_ref, out_ref, stage):
    cols, width = pre_grad_ref.shape
    pre_grad = pre_grad_ref[...]
    row_at = lax.broadcasted_iota(jnp.int32, (cols, width), 0)

    def planes(source, row_tap):
        even = dot(source, w_ref[3 * row_tap], 1, 1)
        odd = dot(source, w_ref[3 * row_tap + 1], 1, 1)
        late = pltpu.roll(dot(source, w_ref[3 * row_tap + 2], 1, 1), 1, 0)
        return even + jnp.where(row_at == 0, 0.0, late), odd

    def weave(row, even, odd):
        for lane in range(width // LANES):
            at = row * (width // LANES) + lane
            here = slice(lane * LANES, (lane + 1) * LANES)
            stage[at, pl.ds(0, cols, stride=2), :] = even[:, here]
            stage[at, pl.ds(1, cols, stride=2), :] = odd[:, here]
            out_ref[row, :, here] = stage[at].astype(bf16)

    even, odd = planes(pre_grad, 1)
    weave(1, even, odd)
    even, odd = planes(pre_grad, 0)
    even_rim, odd_rim = planes(prev, 2)
    weave(0, even + even_rim, odd + odd_rim)


def body(activations, conv_weight, conv_bias, head_weight, latent_grad, noise_sample):
    frames, double_rows, double_cols, channels = activations.shape
    cols = double_cols // 2
    latent_dim = latent_grad.shape[-1]
    spaces = lax.axis_size("space")
    times = lax.axis_size("tm")
    line = ("space", "col")
    peers = lax.axis_size(line)
    assert frames == 1 and double_rows == 2 and lax.axis_size("col") == 2
    share = channels // peers
    taps = conv_weight.reshape(9, channels, channels)
    tiles = jnp.transpose(latent_grad[0], (0, 2, 1))
    if share % TAIL or spaces != 4 or times != 2:
        return wide_body(activations, taps, conv_bias, head_weight, tiles, noise_sample)
    core_at = lax.axis_index("col").astype(jnp.int32).reshape(1)
    space_at = lax.axis_index("space").astype(jnp.int32).reshape(1)
    time_at = lax.axis_index("tm").astype(jnp.int32).reshape(1)
    swap = [(0, 1), (1, 0)]
    array = jax.ShapeDtypeStruct

    def over_space(pieces):
        return [
            lax.ppermute(pieces[k], "space", [(i, (i + k) % spaces) for i in range(spaces)])
            for k in range(1, spaces)
        ]

    tile = tiles.shape[1:]
    got_tiles = lax.ppermute(tiles, "col", swap)
    row, second, own_tiles = full_call(
        start_kernel,
        (array((double_cols, channels), bf16),) * 2 + (array(tiles.shape, bf16),),
        [pltpu.SemaphoreType.DMA((3,))],
        0,
        1 << 19,
        "hh",
    )(activations[0], tiles)
    here, far, before = full_call(
        tiles_kernel, (array((tile[0], LANES), bf16),) * 3, [], 0, 1 << 16, "ssvv"
    )(core_at, space_at, own_tiles, got_tiles)
    row, far = lax.optimization_barrier((row, far))
    above = lax.ppermute(row, line, [(i, (i - 1) % peers) for i in range(peers)])
    hops = [(2 * i + c, 2 * ((i + 1 + c) % spaces) + c) for i in range(spaces) for c in range(2)]
    far = lax.ppermute(far, line, hops)
    square = 2 * cols * channels * channels
    act_here, before = full_call(
        load_kernel,
        (
            array((double_rows, double_cols, channels), bf16),
            array((tile[0], LANES), bf16),
        ),
        [],
        60 * square,
        2 << 20,
        "vvv",
    )(row, second, before)
    early, w_here = full_call(
        early_kernel,
        (array((cols + 4 * latent_dim, channels), f32), array(taps.shape, bf16)),
        [
            pltpu.VMEM((1, channels), f32),
            pltpu.VMEM((2 * latent_dim, channels), bf16),
            pltpu.VMEM((latent_dim, cols), bf16),
            pltpu.VMEM((2 * (channels // LANES), double_cols + 8, LANES), f32),
            pltpu.SemaphoreType.DMA((6,)),
        ],
        300 * square,
        3 << 20,
        "hhhhvv",
    )(
        conv_bias.reshape(1, channels),
        head_weight.T,
        jnp.transpose(noise_sample[0, 0]),
        taps,
        act_here,
        here,
    )
    back = [(2 * i + 1, 2 * ((i - 1) % spaces)) for i in range(spaces)]
    after = lax.ppermute(before, line, back + [(2 * i, 2 * i + 1) for i in range(spaces)])
    beside = lax.ppermute(act_here, "col", swap)
    chip_windows = full_call(
        functools.partial(select_kernel, spaces),
        array((6, 2 * cols, channels // 2), bf16),
        [pltpu.VMEM((4 * (channels // 2 // LANES), double_cols + 8, LANES), f32)],
        4 * square,
        2 << 20,
        "svv",
    )(core_at, act_here, beside)
    early, chip_windows, far, after = lax.optimization_barrier((early, chip_windows, far, after))
    came = full_call(
        join_kernel, array((2 * tile[0], LANES), bf16), [], 0, 1 << 14, "vv"
    )(far, after)
    other_came = lax.ppermute(came, "col", swap)
    above, came = lax.optimization_barrier((above, came))
    rows_a = HALVED * share
    rows_b = (9 - HALVED) * share + TAIL
    half = channels // 2
    pre_act, last_windows, hidden = full_call(
        functools.partial(conv_kernel, spaces),
        (
            array((cols, channels), f32),
            array((3, cols, channels), bf16),
            array((cols, channels), bf16),
        ),
        [pltpu.VMEM((channels // LANES, double_cols + 8, LANES), f32)],
        3 * square,
        2 << 20,
        "ssvvv",
    )(core_at, space_at, early, w_here, above)
    pre_grad, moment_grad = full_call(
        grad_kernel,
        (array((cols, channels), bf16), array((2 * latent_dim, cols), bf16)),
        [pltpu.VMEM((spaces, tile[0], 2 * tile[1]), bf16)],
        square,
        1 << 20,
        "ssvvvvv",
    )(core_at, space_at, early, pre_act, hidden, came, other_came)
    beside_grad = lax.ppermute(pre_grad, "col", swap)
    keep_b, send_b = full_call(
        frame_terms_kernel,
        (
            array((spaces, rows_b, channels), f32),
            array((spaces, rows_b, channels), bf16),
        ),
        [],
        cols,
        cols,
        "svvvv",
    )(core_at, last_windows, pre_grad, hidden, moment_grad)
    got_b = lax.ppermute(send_b, "col", swap)
    own_a, cross_a = full_call(
        chip_terms_kernel,
        (array((spaces, rows_a, half), f32), array((spaces, rows_a, half), bf16)),
        [],
        6 * square,
        2 << 20,
        "svvv",
    )(time_at, chip_windows, pre_grad, beside_grad)
    crossed_a = lax.ppermute(cross_a, "tm", swap)
    half_grad = cols // 2
    pieces_b = full_call(
        pair_rim_kernel,
        tuple(
            array((rows_b + (half_grad if k == 1 else 0), channels), f32 if k == 0 else bf16)
            for k in range(spaces)
        ),
        [],
        spaces * rows_b * channels,
        1 << 20,
        "ssvvvv",
    )(core_at, space_at, keep_b, got_b, pre_grad, beside_grad)
    far_b = over_space(pieces_b)
    pieces_a = full_call(
        pair_kernel,
        tuple(array((rows_a, half), f32 if k == 0 else bf16) for k in range(spaces)),
        [],
        spaces * rows_a * half,
        1 << 20,
        "svv",
    )(space_at, own_a, crossed_a)
    far_a = over_space(pieces_a)
    sum_b, high = full_call(
        line_rim_kernel,
        (array((rows_b, channels), bf16), array((half_grad, channels), bf16)),
        [],
        4 * rows_b * channels,
        1 << 19,
        "v" * spaces,
    )(pieces_b[0], *far_b)
    other_b = lax.ppermute(sum_b, "tm", swap)
    low = lax.ppermute(high, "col", swap)
    sum_a = full_call(
        line_kernel, array((rows_a, half), bf16), [], 4 * rows_a * half, 1 << 19, "v" * spaces
    )(pieces_a[0], *far_a)
    other_a = lax.ppermute(sum_a, "tm", swap)
    x_grad = full_call(
        input_chip_kernel,
        array((2, double_cols, channels), bf16),
        [pltpu.VMEM((2 * (channels // LANES), double_cols, LANES), f32)],
        9 * square,
        4 << 20,
        "ssvvvvv",
    )(core_at, space_at, pre_grad, beside_grad, low, high, taps)
    other_a, x_grad = lax.optimization_barrier((other_a, x_grad))
    positions = frames * times * peers * cols
    kernel_grad, head_grad, bias_grad = full_call(
        functools.partial(final_kernel, 1.0 / math.sqrt(positions)),
        (
            array((9, share, channels), f32),
            array((share, 2 * latent_dim), f32),
            array((1, share), f32),
        ),
        [],
        rows_a * half + rows_b * channels,
        1 << 20,
        "svvvv",
    )(time_at, sum_a, other_a, sum_b, other_b)
    return (
        x_grad[None],
        kernel_grad.reshape(3, 3, share, channels),
        head_grad,
        bias_grad.reshape(share),
    )


def input_gradient(pre_grad, prev, taps):
    cols, channels = pre_grad.shape
    return full_call(
        input_kernel,
        jax.ShapeDtypeStruct((2, 2 * cols, channels), bf16),
        [pltpu.VMEM((2 * (channels // LANES), 2 * cols, LANES), f32)],
        18 * cols * channels * channels,
        4 << 20,
        "vvv",
    )(pre_grad, prev, taps)


def wide_body(activations, taps, conv_bias, head_weight, tiles, noise_sample):
    _, _, double_cols, channels = activations.shape
    cols = double_cols // 2
    latent_dim = noise_sample.shape[-1]
    line = ("space", "col")
    peers = lax.axis_size(line)
    next_row = lax.ppermute(activations[0, 0], line, [(i, i - 1) for i in range(1, peers)])
    upstream = lax.all_to_all(tiles, line, split_axis=0, concat_axis=0, tiled=True)
    padded = jnp.pad(jnp.concatenate([activations[0], next_row[None]], 0), ((0, 0), (0, 1), (0, 0)))
    windows = [
        padded[index // 3, index % 3 : index % 3 + 2 * cols : 2] for index in range(9)
    ]
    pre_act = jnp.zeros((cols, channels), f32) + conv_bias
    for index in range(9):
        pre_act = pre_act + dot(windows[index], taps[index], 1, 0)
    gating = jax.nn.sigmoid(pre_act)
    hidden = (pre_act * gating).astype(bf16)
    moments = dot(hidden, head_weight, 1, 0)
    upstream = jnp.transpose(upstream, (0, 2, 1)).reshape(cols, latent_dim).astype(f32)
    spread = jnp.exp(0.5 * moments[:, latent_dim:])
    mean_grad = upstream + kl_weight * moments[:, :latent_dim]
    logvar_grad = 0.5 * upstream * noise_sample[0, 0].astype(f32) * spread
    logvar_grad = logvar_grad + 0.5 * kl_weight * (spread * spread - 1.0)
    moment_grad = jnp.concatenate([mean_grad, logvar_grad], 1).astype(bf16)
    hidden_grad = dot(moment_grad, head_weight, 1, 1)
    pre_grad = (hidden_grad * gating * (1.0 + pre_act * (1.0 - gating))).astype(bf16)
    prev = lax.ppermute(pre_grad, line, [(i, i + 1) for i in range(peers - 1)])
    x_grad = input_gradient(pre_grad, prev, taps)
    kernel_term = jnp.stack([dot(window, pre_grad, 0, 0) for window in windows], 1)
    terms = (
        kernel_term.reshape(channels, 9 * channels),
        dot(hidden, moment_grad, 0, 0),
        jnp.sum(pre_grad, axis=0, dtype=f32),
    )
    grad_scale = 1.0 / math.sqrt(lax.axis_size("tm") * peers * cols)
    shares = [
        lax.psum_scatter(lax.psum(term, "tm"), line, scatter_dimension=0, tiled=True) * grad_scale
        for term in terms
    ]
    kernel_grad = jnp.transpose(shares[0].reshape(-1, 3, 3, channels), (1, 2, 0, 3))
    return x_grad[None], kernel_grad, shares[1], shares[2]


def solution(mesh):
    in_specs = (
        P(("groups", "tm"), ("space", "col"), None, None),
        P(),
        P(),
        P(),
        P(("groups", "tm"), None, ("space", "col"), None),
        P(("groups", "tm"), ("space", "col"), None, None),
    )
    out_specs = (
        P(("groups", "tm"), ("space", "col"), None, None),
        P(None, None, ("groups", "space", "col"), None),
        P(("groups", "space", "col"), None),
        P(("groups", "space", "col")),
    )
    return jax.shard_map(body, mesh=mesh, in_specs=in_specs, out_specs=out_specs, check_vma=False)
```

```python
import functools
import math

import jax
import jax.numpy as jnp
from jax import lax
from jax.experimental import pallas as pl
from jax.experimental.pallas import tpu as pltpu
from jax.sharding import PartitionSpec as P

f32 = jnp.float32
bf16 = jnp.bfloat16
kl_weight = 1.0
LANES = 128
A_ORDER = (1, 2, 3)
B_ORDER = (1, 3, 2)
HALVED = 6
TAIL = 8


def dot(a, b, ca, cb):
    return lax.dot_general(a, b, (((ca,), (cb,)), ((), ())), preferred_element_type=f32)


def params():
    return pltpu.CompilerParams(vmem_limit_bytes=12 << 20)


SPACES = {"s": pltpu.SMEM, "v": pltpu.VMEM, "h": pltpu.HBM}


def full_call(kernel, out_shape, scratch, flops, moved, places):
    call = pl.pallas_call(
        kernel,
        out_shape=out_shape,
        in_specs=[pl.BlockSpec(memory_space=SPACES[place]) for place in places],
        out_specs=jax.tree.map(lambda _: pl.BlockSpec(memory_space=pltpu.VMEM), out_shape),
        scratch_shapes=scratch,
        compiler_params=params(),
        cost_estimate=pl.CostEstimate(flops=flops, bytes_accessed=moved, transcendentals=0),
    )

    def placed(*args):
        pinned = [
            pltpu.with_memory_space_constraint(arg, pltpu.HBM) if place == "h" else arg
            for arg, place in zip(args, places)
        ]
        return call(*pinned)

    return placed


def start_kernel(act_ref, tiles_in, row_ref, second_ref, tiles_ref, sems):
    copies = [
        pltpu.make_async_copy(tiles_in, tiles_ref, sems.at[0]),
        pltpu.make_async_copy(act_ref.at[0], row_ref, sems.at[1]),
        pltpu.make_async_copy(act_ref.at[1], second_ref, sems.at[2]),
    ]
    for copy in copies:
        copy.start()
    for copy in copies:
        copy.wait()


def tiles_kernel(core_ref, space_ref, own_ref, got_ref, here_ref, far_ref, before_ref):
    spaces = own_ref.shape[0] // 2
    height, width = own_ref.shape[1:]
    core, chip = core_ref[0], space_ref[0]
    first = core == 0

    def side_by_side(at):
        mine, other = own_ref[at], got_ref[at]
        return [jnp.where(first, mine, other), jnp.where(first, other, mine)]

    rest = [jnp.zeros((height, here_ref.shape[1] - 2 * width), bf16)]
    here_ref[...] = jnp.concatenate(side_by_side(2 * chip + core) + rest, 1)
    there = 2 * lax.rem(chip + 1 + core, spaces)
    far_ref[...] = jnp.concatenate(side_by_side(there) + side_by_side(there + 1), 1)
    there = 2 * lax.rem(chip + spaces - 1, spaces)
    before_ref[...] = jnp.concatenate(side_by_side(there) + side_by_side(there + 1), 1)


def join_kernel(far_ref, next_ref, out_ref):
    height = far_ref.shape[0]
    out_ref[:height, :] = far_ref[...]
    out_ref[height:, :] = next_ref[...]


def split_columns(row, source, stage):
    length, width = source.shape
    lanes = width // LANES
    source = source.astype(f32)
    for lane in range(lanes):
        stage[row * lanes + lane, :length, :] = source[:, lane * LANES : (lane + 1) * LANES]
        stage[row * lanes + lane, length:, :] = jnp.zeros((8, LANES), f32)
    windows = []
    for tap in range(3):
        halves = [
            stage[row * lanes + lane, pl.ds(tap, length // 2, stride=2), :]
            for lane in range(lanes)
        ]
        windows.append(jnp.concatenate(halves, 1).astype(bf16))
    return windows


def load_kernel(row_ref, second_ref, before_ref, act_ref, later_ref):
    act_ref[0] = row_ref[...]
    act_ref[1] = second_ref[...]
    later_ref[...] = before_ref[...]


def early_kernel(
    bias_in, head_in, noise_in, w_in, act_ref, here_ref,
    pre_act_ref, w_ref, bias, head, noise, stage, sems,
):
    pairs = [(w_in.at[i : i + 3], w_ref.at[i : i + 3]) for i in (0, 3, 6)]
    pairs += [(bias_in, bias), (head_in, head), (noise_in, noise)]
    copies = [pltpu.make_async_copy(a, b, sems.at[i]) for i, (a, b) in enumerate(pairs)]
    for copy in copies:
        copy.start()
    cols = noise.shape[1]
    pre_act = None
    for row in range(2):
        windows = split_columns(row, act_ref[row], stage)
        copies[row].wait()
        for tap in range(3):
            term = dot(windows[tap], w_ref[3 * row + tap], 1, 0)
            pre_act = term if pre_act is None else pre_act + term
    for copy in copies[2:]:
        copy.wait()
    pre_act_ref[:cols, :] = pre_act + bias[...]
    at = cols
    for ref in (head, noise, here_ref):
        pre_act_ref[at : at + ref.shape[0], : ref.shape[1]] = ref[...].astype(f32)
        at += ref.shape[0]


def select_kernel(chips, core_ref, act_ref, beside_ref, windows_ref, stage):
    rows, length, width = beside_ref.shape
    kept = windows_ref.shape[2]
    share = kept // chips
    source = lax.broadcasted_iota(jnp.int32, (width, kept), 0)
    target = lax.broadcasted_iota(jnp.int32, (width, kept), 1)
    wanted = 2 * share * (target // share) + share * core_ref[0] + target % share
    select = jnp.where(source == wanted, 1.0, 0.0).astype(bf16)
    cols = length // 2
    for row in range(rows):
        for at, ref in enumerate((act_ref, beside_ref)):
            picked = dot(ref[row], select, 1, 0)
            windows = split_columns(rows * at + row, picked, stage)
            for tap in range(3):
                windows_ref[3 * row + tap, cols * at : cols * (at + 1), :] = windows[tap]


def conv_kernel(
    chips, core_ref, space_ref, early_ref, w_ref, above_ref,
    pre_act_ref, windows_ref, hidden_ref, stage,
):
    cols = hidden_ref.shape[0]
    last = (core_ref[0] == 1) & (space_ref[0] == chips - 1)
    row = above_ref[...]
    windows = split_columns(0, jnp.where(last, jnp.zeros_like(row), row), stage)
    pre_act = early_ref[:cols, :]
    for tap in range(3):
        windows_ref[tap] = windows[tap]
        pre_act = pre_act + dot(windows[tap], w_ref[6 + tap], 1, 0)
    pre_act_ref[...] = pre_act
    hidden_ref[...] = jax.nn.silu(pre_act).astype(bf16)


def grad_kernel(
    core_ref, space_ref, early_ref, pre_act_ref, hidden_ref, tiles_ref, other_tiles_ref,
    pre_grad_ref, moment_grad_ref, tiles_at,
):
    cols, width = pre_grad_ref.shape
    spaces, latent, lanes = tiles_at.shape
    head = early_ref[cols : cols + 2 * latent, :].astype(bf16)
    at = cols + 2 * latent
    sample = early_ref[at : at + latent, :cols]
    chip = space_ref[0]
    first = core_ref[0] == 0
    tiles_at[chip] = early_ref[at + latent : at + 2 * latent, :lanes].astype(bf16)
    mine, other = tiles_ref[...], other_tiles_ref[...]
    for there, both in (
        (spaces - 1, jnp.where(first, mine[:latent], other[:latent])),
        (spaces - 2, jnp.where(first, other[:latent], mine[:latent])),
        (1, jnp.where(first, mine[latent:], other[latent:])),
    ):
        band = jnp.where(first, both[:, :lanes], both[:, lanes:])
        tiles_at[lax.rem(chip + there, spaces)] = band
    pre_act = pre_act_ref[...]
    gating = jax.nn.sigmoid(pre_act)
    moments = dot(head, hidden_ref[...], 1, 1)
    mean_part = moments[:latent]
    logvar = moments[latent:]
    upstream = jnp.concatenate([tiles_at[i].astype(f32) for i in range(spaces)], 1)
    spread = jnp.exp(0.5 * logvar)
    mean_grad = upstream + kl_weight * mean_part
    logvar_grad = 0.5 * upstream * sample * spread + 0.5 * kl_weight * (spread * spread - 1.0)
    moment_grad = jnp.concatenate([mean_grad, logvar_grad], 0).astype(bf16)
    hidden_grad = dot(moment_grad, head, 0, 0)
    pre_grad = (hidden_grad * gating * (1.0 + pre_act * (1.0 - gating))).astype(bf16)
    pre_grad_ref[...] = pre_grad
    moment_grad_ref[...] = moment_grad


def put_shares(first, keep_ref, send_ref, at, term):
    spaces = keep_ref.shape[0]
    share = term.shape[0] // (2 * spaces)
    for s in range(spaces):
        row = 2 * share * s
        even, odd = term[row : row + share], term[row + share : row + 2 * share]
        keep_ref[s, at : at + share, :] = jnp.where(first, even, odd)
        send_ref[s, at : at + share, :] = jnp.where(first, odd, even).astype(bf16)


def frame_terms_kernel(
    core_ref, windows_ref, pre_grad_ref, hidden_ref, moment_grad_ref, keep_ref, send_ref
):
    cols, width = pre_grad_ref.shape
    spaces = keep_ref.shape[0]
    share = width // (2 * spaces)
    first = core_ref[0] == 0
    pre_grad = pre_grad_ref[...]
    taps = windows_ref.shape[0]
    for tap in range(taps):
        put_shares(first, keep_ref, send_ref, tap * share, dot(windows_ref[tap], pre_grad, 0, 0))
    head_term = dot(hidden_ref[...], moment_grad_ref[...], 0, 1)
    bias_term = dot(jnp.ones((TAIL, cols), bf16), pre_grad, 1, 0)

    def tail(row):
        pieces = [head_term[row + i : row + i + TAIL] for i in range(0, share, TAIL)]
        pieces.append(bias_term[:, row : row + share])
        used = sum(piece.shape[1] for piece in pieces)
        pieces.append(jnp.zeros((TAIL, width - used), f32))
        return jnp.concatenate(pieces, 1)

    tails = []
    for s in range(2 * spaces):
        tails.append(tail(share * s))
    put_shares(first, keep_ref, send_ref, taps * share, jnp.concatenate(tails, 0))


def chip_terms_kernel(
    time_ref, windows_ref, pre_grad_ref, beside_ref, own_ref, send_ref
):
    first = time_ref[0] == 0
    pre_grad = jnp.concatenate([pre_grad_ref[...], beside_ref[...]], 0)
    spaces, _, half = own_ref.shape
    share = windows_ref.shape[2] // spaces
    for index in range(HALVED):
        term = dot(windows_ref[index], pre_grad, 0, 0)
        low, high = term[:, :half], term[:, half:]
        mine = jnp.where(first, low, high)
        other = jnp.where(first, high, low).astype(bf16)
        here = slice(index * share, (index + 1) * share)
        for s in range(spaces):
            own_ref[s, here, :] = mine[s * share : (s + 1) * share]
            send_ref[s, here, :] = other[s * share : (s + 1) * share]


def pair_kernel(space_ref, keep_ref, got_ref, *outs):
    spaces = len(outs)
    for k, out in enumerate(outs):
        at = lax.rem(space_ref[0] + k, spaces)
        out[...] = (keep_ref[at] + got_ref[at].astype(f32)).astype(out.dtype)


def pair_rim_kernel(core_ref, space_ref, keep_ref, got_ref, mine_ref, beside_ref, *outs):
    spaces = len(outs)
    rows = keep_ref.shape[1]
    for k, out in enumerate(outs):
        at = lax.rem(space_ref[0] + k, spaces)
        out[:rows, :] = (keep_ref[at] + got_ref[at].astype(f32)).astype(out.dtype)
    half = mine_ref.shape[0] // 2
    first = core_ref[0] == 0
    outs[1][rows:, :] = jnp.where(first, beside_ref[half:, :], mine_ref[:half, :])


def line_kernel(own_ref, *refs):
    total = own_ref[...]
    for ref in refs[:-1]:
        total = total + ref[...].astype(f32)
    refs[-1][...] = total.astype(bf16)


def line_rim_kernel(rim_at, own_ref, *refs):
    rows = own_ref.shape[0]
    total = own_ref[...]
    for ref in refs[:-2]:
        total = total + ref[:rows, :].astype(f32)
    refs[-2][...] = total.astype(bf16)
    refs[-1][...] = refs[rim_at][rows:, :]


def final_kernel(
    scale, time_ref, a_ref, a_far_ref, b_ref, b_far_ref, kernel_ref, head_ref, bias_ref
):
    share, latents = head_ref.shape
    first = time_ref[0] == 0
    mine, far = a_ref[...].astype(f32) * scale, a_far_ref[...].astype(f32) * scale
    low, high = jnp.where(first, mine, far), jnp.where(first, far, mine)
    total = (b_ref[...].astype(f32) + b_far_ref[...].astype(f32)) * scale
    half = mine.shape[1]
    for index in range(HALVED):
        kernel_ref[index, :, :half] = low[index * share : (index + 1) * share]
        kernel_ref[index, :, half:] = high[index * share : (index + 1) * share]
    for index in range(HALVED, 9):
        at = (index - HALVED) * share
        kernel_ref[index] = total[at : at + share]
    tail = total[(9 - HALVED) * share :]
    for i in range(share // TAIL):
        head_ref[TAIL * i : TAIL * (i + 1), :] = tail[:, latents * i : latents * (i + 1)]
    at = latents * (share // TAIL)
    bias_ref[...] = tail[:1, at : at + share]


def input_kernel(pre_grad_ref, prev_ref, w_ref, out_ref, stage):
    input_rows(pre_grad_ref, prev_ref[...], w_ref, out_ref, stage)


def input_chip_kernel(
    core_ref, space_ref, pre_grad_ref, beside_ref, low_ref, high_ref, w_ref, out_ref, stage
):
    below = jnp.concatenate([low_ref[...], high_ref[...]], 0)
    below = jnp.where(space_ref[0] == 0, jnp.zeros_like(below), below)
    prev = jnp.where(core_ref[0] == 0, below, beside_ref[...])
    input_rows(pre_grad_ref, prev, w_ref, out_ref, stage)


def input_rows(pre_grad_ref, prev, w_ref, out_ref, stage):
    cols, width = pre_grad_ref.shape
    pre_grad = pre_grad_ref[...]
    row_at = lax.broadcasted_iota(jnp.int32, (cols, width), 0)

    def planes(source, row_tap):
        even = dot(source, w_ref[3 * row_tap], 1, 1)
        odd = dot(source, w_ref[3 * row_tap + 1], 1, 1)
        late = pltpu.roll(dot(source, w_ref[3 * row_tap + 2], 1, 1), 1, 0)
        return even + jnp.where(row_at == 0, 0.0, late), odd

    def weave(row, even, odd):
        for lane in range(width // LANES):
            at = row * (width // LANES) + lane
            here = slice(lane * LANES, (lane + 1) * LANES)
            stage[at, pl.ds(0, cols, stride=2), :] = even[:, here]
            stage[at, pl.ds(1, cols, stride=2), :] = odd[:, here]
            out_ref[row, :, here] = stage[at].astype(bf16)

    even, odd = planes(pre_grad, 1)
    weave(1, even, odd)
    even, odd = planes(pre_grad, 0)
    even_rim, odd_rim = planes(prev, 2)
    weave(0, even + even_rim, odd + odd_rim)


def body(activations, conv_weight, conv_bias, head_weight, latent_grad, noise_sample):
    frames, double_rows, double_cols, channels = activations.shape
    cols = double_cols // 2
    latent_dim = latent_grad.shape[-1]
    spaces = lax.axis_size("space")
    times = lax.axis_size("tm")
    line = ("space", "col")
    peers = lax.axis_size(line)
    assert frames == 1 and double_rows == 2 and lax.axis_size("col") == 2
    share = channels // peers
    taps = conv_weight.reshape(9, channels, channels)
    tiles = jnp.transpose(latent_grad[0], (0, 2, 1))
    if share % TAIL or spaces != 4 or times != 2:
        return wide_body(activations, taps, conv_bias, head_weight, tiles, noise_sample)
    core_at = lax.axis_index("col").astype(jnp.int32).reshape(1)
    space_at = lax.axis_index("space").astype(jnp.int32).reshape(1)
    time_at = lax.axis_index("tm").astype(jnp.int32).reshape(1)
    swap = [(0, 1), (1, 0)]
    array = jax.ShapeDtypeStruct

    def over_space(pieces):
        return [
            lax.ppermute(pieces[k], "space", [(i, (i + k) % spaces) for i in range(spaces)])
            for k in range(1, spaces)
        ]

    tile = tiles.shape[1:]
    got_tiles = lax.ppermute(tiles, "col", swap)
    row, second, own_tiles = full_call(
        start_kernel,
        (array((double_cols, channels), bf16),) * 2 + (array(tiles.shape, bf16),),
        [pltpu.SemaphoreType.DMA((3,))],
        0,
        1 << 19,
        "hh",
    )(activations[0], tiles)
    here, far, before = full_call(
        tiles_kernel, (array((tile[0], LANES), bf16),) * 3, [], 0, 1 << 16, "ssvv"
    )(core_at, space_at, own_tiles, got_tiles)
    row, far = lax.optimization_barrier((row, far))
    above = lax.ppermute(row, line, [(i, (i - 1) % peers) for i in range(peers)])
    hops = [(2 * i + c, 2 * ((i + 1 + c) % spaces) + c) for i in range(spaces) for c in range(2)]
    far = lax.ppermute(far, line, hops)
    square = 2 * cols * channels * channels
    act_here, before = full_call(
        load_kernel,
        (
            array((double_rows, double_cols, channels), bf16),
            array((tile[0], LANES), bf16),
        ),
        [],
        60 * square,
        2 << 20,
        "vvv",
    )(row, second, before)
    early, w_here = full_call(
        early_kernel,
        (array((cols + 4 * latent_dim, channels), f32), array(taps.shape, bf16)),
        [
            pltpu.VMEM((1, channels), f32),
            pltpu.VMEM((2 * latent_dim, channels), bf16),
            pltpu.VMEM((latent_dim, cols), bf16),
            pltpu.VMEM((2 * (channels // LANES), double_cols + 8, LANES), f32),
            pltpu.SemaphoreType.DMA((6,)),
        ],
        300 * square,
        3 << 20,
        "hhhhvv",
    )(
        conv_bias.reshape(1, channels),
        head_weight.T,
        jnp.transpose(noise_sample[0, 0]),
        taps,
        act_here,
        here,
    )
    back = [(2 * i + 1, 2 * ((i - 1) % spaces)) for i in range(spaces)]
    after = lax.ppermute(before, line, back + [(2 * i, 2 * i + 1) for i in range(spaces)])
    beside = lax.ppermute(act_here, "col", swap)
    chip_windows = full_call(
        functools.partial(select_kernel, spaces),
        array((6, 2 * cols, channels // 2), bf16),
        [pltpu.VMEM((4 * (channels // 2 // LANES), double_cols + 8, LANES), f32)],
        4 * square,
        2 << 20,
        "svv",
    )(core_at, act_here, beside)
    early, chip_windows, far, after = lax.optimization_barrier((early, chip_windows, far, after))
    came = full_call(
        join_kernel, array((2 * tile[0], LANES), bf16), [], 0, 1 << 14, "vv"
    )(far, after)
    other_came = lax.ppermute(came, "col", swap)
    above, came = lax.optimization_barrier((above, came))
    rows_a = HALVED * share
    rows_b = (9 - HALVED) * share + TAIL
    half = channels // 2
    pre_act, last_windows, hidden = full_call(
        functools.partial(conv_kernel, spaces),
        (
            array((cols, channels), f32),
            array((3, cols, channels), bf16),
            array((cols, channels), bf16),
        ),
        [pltpu.VMEM((channels // LANES, double_cols + 8, LANES), f32)],
        3 * square,
        2 << 20,
        "ssvvv",
    )(core_at, space_at, early, w_here, above)
    pre_grad, moment_grad = full_call(
        grad_kernel,
        (array((cols, channels), bf16), array((2 * latent_dim, cols), bf16)),
        [pltpu.VMEM((spaces, tile[0], 2 * tile[1]), bf16)],
        square,
        1 << 20,
        "ssvvvvv",
    )(core_at, space_at, early, pre_act, hidden, came, other_came)
    beside_grad = lax.ppermute(pre_grad, "col", swap)
    keep_b, send_b = full_call(
        frame_terms_kernel,
        (
            array((spaces, rows_b, channels), f32),
            array((spaces, rows_b, channels), bf16),
        ),
        [],
        cols,
        cols,
        "svvvv",
    )(core_at, last_windows, pre_grad, hidden, moment_grad)
    got_b = lax.ppermute(send_b, "col", swap)
    own_a, cross_a = full_call(
        chip_terms_kernel,
        (array((spaces, rows_a, half), f32), array((spaces, rows_a, half), bf16)),
        [],
        6 * square,
        2 << 20,
        "svvv",
    )(time_at, chip_windows, pre_grad, beside_grad)
    crossed_a = lax.ppermute(cross_a, "tm", swap)
    half_grad = cols // 2
    pieces_b = full_call(
        pair_rim_kernel,
        tuple(
            array((rows_b + (half_grad if k == 1 else 0), channels), f32 if k == 0 else bf16)
            for k in range(spaces)
        ),
        [],
        spaces * rows_b * channels,
        1 << 20,
        "ssvvvv",
    )(core_at, space_at, keep_b, got_b, pre_grad, beside_grad)
    far_b = over_space(pieces_b)
    pieces_a = full_call(
        pair_kernel,
        tuple(array((rows_a, half), f32 if k == 0 else bf16) for k in range(spaces)),
        [],
        spaces * rows_a * half,
        1 << 20,
        "svv",
    )(space_at, own_a, crossed_a)
    far_a = over_space(pieces_a)
    sum_b, high = full_call(
        functools.partial(line_rim_kernel, B_ORDER.index(1)),
        (array((rows_b, channels), bf16), array((half_grad, channels), bf16)),
        [],
        4 * rows_b * channels,
        1 << 19,
        "v" * spaces,
    )(pieces_b[0], *(far_b[k - 1] for k in B_ORDER))
    other_b = lax.ppermute(sum_b, "tm", swap)
    low = lax.ppermute(high, "col", swap)
    sum_a = full_call(
        line_kernel, array((rows_a, half), bf16), [], 4 * rows_a * half, 1 << 19, "v" * spaces
    )(pieces_a[0], *(far_a[k - 1] for k in A_ORDER))
    other_a = lax.ppermute(sum_a, "tm", swap)
    x_grad = full_call(
        input_chip_kernel,
        array((2, double_cols, channels), bf16),
        [pltpu.VMEM((2 * (channels // LANES), double_cols, LANES), f32)],
        9 * square,
        4 << 20,
        "ssvvvvv",
    )(core_at, space_at, pre_grad, beside_grad, low, high, taps)
    other_a, x_grad = lax.optimization_barrier((other_a, x_grad))
    positions = frames * times * peers * cols
    kernel_grad, head_grad, bias_grad = full_call(
        functools.partial(final_kernel, 1.0 / math.sqrt(positions)),
        (
            array((9, share, channels), f32),
            array((share, 2 * latent_dim), f32),
            array((1, share), f32),
        ),
        [],
        rows_a * half + rows_b * channels,
        1 << 20,
        "svvvv",
    )(time_at, sum_a, other_a, sum_b, other_b)
    return (
        x_grad[None],
        kernel_grad.reshape(3, 3, share, channels),
        head_grad,
        bias_grad.reshape(share),
    )


def input_gradient(pre_grad, prev, taps):
    cols, channels = pre_grad.shape
    return full_call(
        input_kernel,
        jax.ShapeDtypeStruct((2, 2 * cols, channels), bf16),
        [pltpu.VMEM((2 * (channels // LANES), 2 * cols, LANES), f32)],
        18 * cols * channels * channels,
        4 << 20,
        "vvv",
    )(pre_grad, prev, taps)


def wide_body(activations, taps, conv_bias, head_weight, tiles, noise_sample):
    _, _, double_cols, channels = activations.shape
    cols = double_cols // 2
    latent_dim = noise_sample.shape[-1]
    line = ("space", "col")
    peers = lax.axis_size(line)
    next_row = lax.ppermute(activations[0, 0], line, [(i, i - 1) for i in range(1, peers)])
    upstream = lax.all_to_all(tiles, line, split_axis=0, concat_axis=0, tiled=True)
    padded = jnp.pad(jnp.concatenate([activations[0], next_row[None]], 0), ((0, 0), (0, 1), (0, 0)))
    windows = [
        padded[index // 3, index % 3 : index % 3 + 2 * cols : 2] for index in range(9)
    ]
    pre_act = jnp.zeros((cols, channels), f32) + conv_bias
    for index in range(9):
        pre_act = pre_act + dot(windows[index], taps[index], 1, 0)
    gating = jax.nn.sigmoid(pre_act)
    hidden = (pre_act * gating).astype(bf16)
    moments = dot(hidden, head_weight, 1, 0)
    upstream = jnp.transpose(upstream, (0, 2, 1)).reshape(cols, latent_dim).astype(f32)
    spread = jnp.exp(0.5 * moments[:, latent_dim:])
    mean_grad = upstream + kl_weight * moments[:, :latent_dim]
    logvar_grad = 0.5 * upstream * noise_sample[0, 0].astype(f32) * spread
    logvar_grad = logvar_grad + 0.5 * kl_weight * (spread * spread - 1.0)
    moment_grad = jnp.concatenate([mean_grad, logvar_grad], 1).astype(bf16)
    hidden_grad = dot(moment_grad, head_weight, 1, 1)
    pre_grad = (hidden_grad * gating * (1.0 + pre_act * (1.0 - gating))).astype(bf16)
    prev = lax.ppermute(pre_grad, line, [(i, i + 1) for i in range(peers - 1)])
    x_grad = input_gradient(pre_grad, prev, taps)
    kernel_term = jnp.stack([dot(window, pre_grad, 0, 0) for window in windows], 1)
    terms = (
        kernel_term.reshape(channels, 9 * channels),
        dot(hidden, moment_grad, 0, 0),
        jnp.sum(pre_grad, axis=0, dtype=f32),
    )
    grad_scale = 1.0 / math.sqrt(lax.axis_size("tm") * peers * cols)
    shares = [
        lax.psum_scatter(lax.psum(term, "tm"), line, scatter_dimension=0, tiled=True) * grad_scale
        for term in terms
    ]
    kernel_grad = jnp.transpose(shares[0].reshape(-1, 3, 3, channels), (1, 2, 0, 3))
    return x_grad[None], kernel_grad, shares[1], shares[2]


def solution(mesh):
    in_specs = (
        P(("groups", "tm"), ("space", "col"), None, None),
        P(),
        P(),
        P(),
        P(("groups", "tm"), None, ("space", "col"), None),
        P(("groups", "tm"), ("space", "col"), None, None),
    )
    out_specs = (
        P(("groups", "tm"), ("space", "col"), None, None),
        P(None, None, ("groups", "space", "col"), None),
        P(("groups", "space", "col"), None),
        P(("groups", "space", "col")),
    )
    return jax.shard_map(body, mesh=mesh, in_specs=in_specs, out_specs=out_specs, check_vma=False)
```
